32 devices in a mesh: dp: 8 (over y, x, core), tensor: 4 (over z).
Axes of the slice: x: 2, y: 2, z: 4, core: 2. Of those that a mesh axis runs over, the one named last changes fastest.
Arguments:
- block_in: bfloat16 [16384, 1024], P(('dp', 'tensor')), may hold values from -48 to 48
- segments: int32 [8, 2048], P('dp'), may hold values from 0 to 5, never falling along the last dimension, each value on 1 to 800 neighbouring positions
- norm_gain: float32 [1024], replicated, may hold values from 0.1 to 1.9
- ema_rate: float32 [16, 1024], replicated, may hold values from 0.0005 to 0.033
- ema_angle: float32 [16, 1024], replicated, may hold values from -3.140625 to 3.140625
- ema_input: float32 [16, 1024], replicated, may hold values from -4 to 4
- ema_output: float32 [2, 16, 1024], replicated, may hold values from -1 to 1
- ema_skip: float32 [1024], replicated, may hold values from -2 to 2
- w_shared: float32 [1024, 256], P('dp'), may hold values from -0.1875 to 0.1875
- query_gain: float32 [256], replicated, may hold values from 0.1 to 1.9
- query_bias: float32 [256], replicated, may hold values from -2 to 2
- key_gain: float32 [256], replicated, may hold values from 0.1 to 1.9
- w_value: float32 [1024, 2048], P('dp', 'tensor'), may hold values from -0.1875 to 0.1875
- w_gate: float32 [1024, 2048], P('dp', 'tensor'), may hold values from -0.1875 to 0.1875
- w_out: float32 [2048, 1024], P('tensor', 'dp'), may hold values from -0.5 to 0.5
- ffn_gain: float32 [1024], replicated, may hold values from 0.1 to 1.9
- w_swish: float32 [1024, 2560], P('dp', 'tensor'), may hold values from -0.1875 to 0.1875
- w_up: float32 [1024, 2560], P('dp', 'tensor'), may hold values from -0.1875 to 0.1875
- w_down: float32 [2560, 1024], P('tensor', 'dp'), may hold values from -0.25 to 0.25
- out_grad: bfloat16 [16384, 1024], P(('dp', 'tensor')), may hold values from -7.2 to 7.2
Outputs:
- block_out: bfloat16 [16384, 1024], P(('dp', 'tensor'))
- in_grad: float32 [16384, 1024], P(('dp', 'tensor'))
- grad_norm_gain: float32 [1024], replicated
- grad_ema_rate: float32 [16, 1024], replicated
- grad_ema_angle: float32 [16, 1024], replicated
- grad_ema_input: float32 [16, 1024], replicated
- grad_ema_output: float32 [2, 16, 1024], replicated
- grad_ema_skip: float32 [1024], replicated
- grad_shared: float32 [1024, 256], P('dp')
- grad_query_gain: float32 [256], replicated
- grad_query_bias: float32 [256], replicated
- grad_key_gain: float32 [256], replicated
- grad_value: float32 [1024, 2048], P('dp', 'tensor')
- grad_gate: float32 [1024, 2048], P('dp', 'tensor')
- grad_out: float32 [2048, 1024], P('tensor', 'dp')
- grad_ffn_gain: float32 [1024], replicated
- grad_swish: float32 [1024, 2560], P('dp', 'tensor')
- grad_up: float32 [1024, 2560], P('dp', 'tensor')
- grad_down: float32 [2560, 1024], P('tensor', 'dp')
The draws below stay inside these ranges and needn't reach their ends.
Inputs may be any that keep to these rules, and one draw needn't show every extreme that they name: `segments`: in each row of 2048 positions the document numbers never fall, and each document spans 1 to 800 positions.
All inputs are finite; a program needn't handle non-finite values.
Results may differ from the reference program's by a relative error of at most 0.02.
Values may be sent and summed in bfloat16 or wider, within the bound.
A program may use at most 576 MiB of HBM per device.

```python
import math
import jax
import jax.numpy as jnp
import numpy as np
from jax import lax

D = 1024
Z = 256
V = 2048
FF = 2560
N = 16
L = 2048
EMA_BLOCK = 128
TN_GROUPS = 16
SEQS = 8
TOKENS = 16384


def draw_block_in(key, part):
    streams = jax.random.split(key, 3)
    row_scale = jnp.exp(jax.random.uniform(streams[0], (TOKENS, 1), jnp.float32, math.log(0.4), math.log(4.0)))
    column_scale = jnp.exp(jax.random.uniform(streams[1], (1, D), jnp.float32, math.log(0.3), math.log(3.0)))
    entries = jnp.clip(jax.random.normal(streams[2], (TOKENS, D), jnp.float32), -4.0, 4.0)
    return (entries * row_scale * column_scale).astype(jnp.bfloat16)


def draw_out_grad(key, part):
    streams = jax.random.split(key, 1)
    seq_index = (jnp.arange(TOKENS, dtype=jnp.int32) // L).astype(jnp.float32)
    rising = (0.6 * jnp.exp(math.log(3.0) * seq_index / max(SEQS - 1, 1)))[:, None]
    entries = jnp.clip(jax.random.normal(streams[0], (TOKENS, D), jnp.float32), -4.0, 4.0)
    return (entries * rising).astype(jnp.bfloat16)


def level_of(stream_key, dims, shards, least, largest):
    gain = 1.0
    for position, shards_of in shards:
        draws = jax.random.uniform(jax.random.fold_in(jax.random.fold_in(stream_key, 6), position), (shards_of,), jnp.float32, least / len(shards), largest / len(shards))
        gain = gain * jnp.repeat(jnp.exp(draws), dims[position] // shards_of).reshape((-1,) + (1,) * (len(dims) - 1 - position))
    return gain


def split_up(number_of, total, bound, lean):
    loads = [(1 << 20) // math.isqrt(standing ** lean) + 1 for standing in range(2, number_of + 1)]
    spare, given = total - bound - (number_of - 1), [1] * (number_of - 1)
    while spare > 0:
        free = [i for i in range(number_of - 1) if given[i] < bound]
        mass, left = sum([loads[i] for i in free]), spare
        for i in free:
            addition = min(bound - given[i], max(1, left * loads[i] // mass), spare)
            given[i] = given[i] + addition
            spare = spare - addition
    return np.array([bound] + given)


def ragged_sizes(own_key, amount, total, reach, lean):
    if amount == 2:
        one = jax.random.randint(own_key, (), max(1, total - reach), min(reach, total - 1) + 1)
        return jnp.stack([one, total - one])
    tallies = jnp.asarray(split_up(amount, total, reach, lean), jnp.int32)
    couples = (amount - 1) // 2
    donor, taker = tallies[1:1 + 2 * couples:2], tallies[2:2 + 2 * couples:2]
    slack = jnp.minimum(donor - 1, reach - taker)
    shifted = jax.random.randint(jax.random.fold_in(own_key, 1), (couples,), 0, 1 << 20) % (slack + 1)
    tallies = tallies.at[1:1 + 2 * couples:2].set(donor - shifted).at[2:2 + 2 * couples:2].set(taker + shifted)
    return tallies[jax.random.permutation(jax.random.fold_in(own_key, 2), amount)]


def gaussian(stream_key, shape, deviation, bound, shards=(), kind=jnp.bfloat16):
    result = jax.random.normal(stream_key, shape, jnp.float32) * deviation
    if len(shards) > 0:
        result = level_of(stream_key, shape, shards, -0.22, 0.18) * result
    return jnp.clip(result, min=-bound, max=bound).astype(kind)


def setup_inputs(seed: int = 0) -> dict:
    seeds = jax.random.split(jax.random.key(seed), 21)
    return {
        "block_in": draw_block_in(jax.random.fold_in(seeds[20], 71), 0),
        "segments": jax.vmap(lambda own: jnp.searchsorted(jnp.cumsum(ragged_sizes(own, 6, L, min(800, L // 2), 1)), jnp.arange(L), side="right"))(jax.random.split(seeds[1], SEQS)).reshape((SEQS, L)).astype(jnp.int32),
        "norm_gain": jnp.clip(1.0 + 0.18 * jax.random.normal(seeds[2], (D,), jnp.float32), 0.1, 1.9),
        "ema_rate": jnp.clip(jnp.exp(jax.random.uniform(seeds[3], (N, D), jnp.float32, math.log(0.0005), math.log(0.033))), 0.0005, 0.033),
        "ema_angle": jnp.clip(jax.random.uniform(seeds[4], (N, D), jnp.float32, -3.140625, 3.140625), -3.140625, 3.140625),
        "ema_input": gaussian(seeds[5], (N, D), 1.0, 4.0, (), jnp.float32),
        "ema_output": gaussian(seeds[6], (2, N, D), (2 * N) ** -0.5, 1.0, (), jnp.float32),
        "ema_skip": gaussian(seeds[7], (D,), 0.5, 2.0, (), jnp.float32),
        "w_shared": gaussian(seeds[8], (D, Z), D ** -0.5, 0.1875, ((0, 8),), jnp.float32),
        "query_gain": jnp.clip(1.0 + 0.18 * jax.random.normal(seeds[9], (Z,), jnp.float32), 0.1, 1.9),
        "query_bias": gaussian(seeds[10], (Z,), 0.5, 2.0, (), jnp.float32),
        "key_gain": jnp.clip(1.0 + 0.18 * jax.random.normal(seeds[11], (Z,), jnp.float32), 0.1, 1.9),
        "w_value": gaussian(seeds[12], (D, V), D ** -0.5, 0.1875, ((0, 8), (1, 4)), jnp.float32),
        "w_gate": gaussian(seeds[13], (D, V), D ** -0.5, 0.1875, ((0, 8), (1, 4)), jnp.float32),
        "w_out": gaussian(seeds[14], (V, D), (V // 16) ** -0.5, 0.5, ((0, 4), (1, 8)), jnp.float32),
        "ffn_gain": jnp.clip(1.0 + 0.18 * jax.random.normal(seeds[15], (D,), jnp.float32), 0.1, 1.9),
        "w_swish": gaussian(seeds[16], (D, FF), D ** -0.5, 0.1875, ((0, 8), (1, 4)), jnp.float32),
        "w_up": gaussian(seeds[17], (D, FF), D ** -0.5, 0.1875, ((0, 8), (1, 4)), jnp.float32),
        "w_down": gaussian(seeds[18], (FF, D), (FF // 4) ** -0.5, 0.25, ((0, 4), (1, 8)), jnp.float32),
        "out_grad": draw_out_grad(jax.random.fold_in(seeds[20], 71), 0),
    }


EPSILON = 1e-05
HIGHEST = lax.Precision.HIGHEST

@jax.custom_vjp
def low(v):
    return lax.optimization_barrier(v.astype(jnp.bfloat16)).astype(jnp.float32)

@jax.custom_vjp
def low_back(v):
    return v

def low_keep(v):
    return (low(v), None)

def low_pass(kept, grad):
    return (grad,)

def back_keep(v):
    return (v, None)

def back_low(kept, grad):
    return (low(grad),)
low.defvjp(low_keep, low_pass)
low_back.defvjp(back_keep, back_low)

def silu_of(values_in):
    return values_in * jax.nn.sigmoid(values_in)

def prefix_reset(flags, values_in):

    def combine(earlier, later):
        return (jnp.maximum(earlier[0], later[0]), later[1] + (1.0 - later[0]) * earlier[1])
    return lax.associative_scan(combine, (flags, values_in), axis=0)[1]

def step_norm(inputs, norm_scale, seg_ids, group_count):
    seq_length, features = inputs.shape
    group_width = features // group_count
    grouped = inputs.reshape(seq_length, group_count, group_width)
    sums_first = lax.optimization_barrier(jnp.sum(grouped, axis=2))
    sums_second = lax.optimization_barrier(jnp.sum(grouped * grouped, axis=2))
    starts = jnp.concatenate([jnp.ones((1,), jnp.float32), (seg_ids[1:] != seg_ids[:-1]).astype(jnp.float32)])[:, None]
    counter = jnp.ones((seq_length, 1), jnp.float32)
    running = prefix_reset(starts, jnp.concatenate([sums_first, sums_second, counter], axis=1))
    entries = running[:, 2 * group_count:] * group_width
    average = running[:, :group_count] / entries
    spread = running[:, group_count:2 * group_count] / entries - average * average
    centred = (grouped - average[:, :, None]) * lax.rsqrt(spread + EPSILON)[:, :, None]
    return centred.reshape(seq_length, features) * norm_scale

def ema_apply(hidden, decay_rate, turn_angle, feed_gain, read_gain, skip_gain, seg_ids):
    seq_length, channels = hidden.shape
    ema_dims = decay_rate.shape[0]
    block_len = EMA_BLOCK
    block_count = seq_length // block_len
    offsets = jnp.arange(block_len).astype(jnp.float32)[:, None, None]
    grow = jnp.exp(decay_rate * offsets)
    shrink = jnp.exp(-decay_rate * offsets)
    cosine = jnp.cos(turn_angle * offsets)
    sine_part = jnp.sin(turn_angle * offsets)
    feed = feed_gain * jnp.sqrt(1.0 - jnp.exp(-2.0 * decay_rate))
    tiled = hidden.reshape(block_count, block_len, 1, channels)
    drive_real = tiled * (feed * grow * cosine)
    drive_imag = tiled * (-feed * grow * sine_part)
    seg_blocks = seg_ids.reshape(block_count, block_len)
    lower = jnp.arange(block_len)[:, None] >= jnp.arange(block_len)[None, :]
    same_doc = seg_blocks[:, :, None] == seg_blocks[:, None, :]
    within = jnp.logical_and(same_doc, lower[None]).astype(jnp.float32)
    stacked = jnp.stack([drive_real, drive_imag], axis=2).reshape(block_count, block_len, 2 * ema_dims * channels)
    inner = jnp.einsum('nts,nsk->ntk', within, stacked, precision=HIGHEST)
    inner = inner.reshape(block_count, block_len, 2, ema_dims, channels)
    inner_real = inner[:, :, 0]
    inner_imag = inner[:, :, 1]
    prior = jnp.concatenate([jnp.full((1,), -1, jnp.int32), seg_blocks[:-1, -1].astype(jnp.int32)])
    linked = (seg_blocks.astype(jnp.int32) == prior[:, None]).astype(jnp.float32)
    power_real = shrink * cosine
    power_imag = shrink * sine_part
    end_real = power_real[-1] * inner_real[:, -1] - power_imag[-1] * inner_imag[:, -1]
    end_imag = power_real[-1] * inner_imag[:, -1] + power_imag[-1] * inner_real[:, -1]
    whole_mod = jnp.exp(-decay_rate * block_len)
    carry_real = (whole_mod * jnp.cos(turn_angle * block_len))[None] * linked[:, -1, None, None]
    carry_imag = (whole_mod * jnp.sin(turn_angle * block_len))[None] * linked[:, -1, None, None]

    def combine(earlier, later):
        return (later[0] * earlier[0] - later[1] * earlier[1], later[0] * earlier[1] + later[1] * earlier[0], later[0] * earlier[2] - later[1] * earlier[3] + later[2], later[0] * earlier[3] + later[1] * earlier[2] + later[3])
    states = lax.associative_scan(combine, (carry_real, carry_imag, end_real, end_imag), axis=0)
    zero_state = jnp.zeros((1, ema_dims, channels), jnp.float32)
    before_real = jnp.concatenate([zero_state, states[2][:-1]], axis=0)
    before_imag = jnp.concatenate([zero_state, states[3][:-1]], axis=0)
    step_real = jnp.exp(-decay_rate) * jnp.cos(turn_angle)
    step_imag = jnp.exp(-decay_rate) * jnp.sin(turn_angle)
    push_real = step_real * before_real - step_imag * before_imag
    push_imag = step_real * before_imag + step_imag * before_real
    link_full = linked[:, :, None, None]
    total_real = inner_real + link_full * push_real[:, None]
    total_imag = inner_imag + link_full * push_imag[:, None]
    state_real = power_real * total_real - power_imag * total_imag
    state_imag = power_real * total_imag + power_imag * total_real
    mixed = lax.optimization_barrier(jnp.sum(read_gain[0] * state_real - read_gain[1] * state_imag, axis=2))
    return mixed.reshape(seq_length, channels) + skip_gain * hidden

def ema_all(normed, decay_rate, turn_angle, feed_gain, read_gain, skip_gain, seg_ids):
    seq_length, features = normed.shape
    ema_dims = decay_rate.shape[0]
    group_span = math.gcd(features, 256)
    group_total = features // group_span

    def one_group(pieces):
        return ema_apply(pieces[0], pieces[1], pieces[2], pieces[3], pieces[4], pieces[5], seg_ids)
    pieces = (normed.reshape(seq_length, group_total, group_span).transpose(1, 0, 2), decay_rate.reshape(ema_dims, group_total, group_span).transpose(1, 0, 2), turn_angle.reshape(ema_dims, group_total, group_span).transpose(1, 0, 2), feed_gain.reshape(ema_dims, group_total, group_span).transpose(1, 0, 2), read_gain.reshape(2, ema_dims, group_total, group_span).transpose(2, 0, 1, 3), skip_gain.reshape(group_total, group_span))
    results = lax.map(jax.checkpoint(one_group), pieces)
    return results.transpose(1, 0, 2).reshape(seq_length, features)

def attention(queries, keys_in, values_in, seg_ids):
    seq_length, head_dim = queries.shape
    block_len = min(512, seq_length)
    score_scale = 1.0 / math.sqrt(head_dim)
    positions = jnp.arange(seq_length, dtype=jnp.int32)

    def one_block(block_index):
        row_start = (block_index * block_len).astype(jnp.int32)
        query_rows = lax.dynamic_slice_in_dim(queries, row_start, block_len, 0)
        query_pos = row_start + jnp.arange(block_len, dtype=jnp.int32)
        query_seg = lax.dynamic_slice_in_dim(seg_ids, row_start, block_len, 0)
        allowed = jnp.logical_and(positions[None, :] <= query_pos[:, None], seg_ids[None, :] == query_seg[:, None])
        scores = low_back(score_scale * jnp.dot(query_rows, keys_in.T, precision=HIGHEST))
        masked = jnp.where(allowed, scores, -1e+30)
        row_peak = lax.optimization_barrier(jnp.max(masked, axis=1, keepdims=True))
        raw_weights = jnp.exp(masked - row_peak)
        attn_probs = raw_weights / lax.optimization_barrier(jnp.sum(raw_weights, axis=1, keepdims=True))
        return jnp.dot(low(attn_probs), values_in, precision=HIGHEST)
    blocks_out = lax.map(jax.checkpoint(one_block), jnp.arange(seq_length // block_len, dtype=jnp.int32))
    return blocks_out.reshape(seq_length, values_in.shape[1])

def sequence_forward(params, inputs, seg_ids):
    norm_gain, ema_rate, ema_angle, ema_input, ema_output, ema_skip, w_shared, query_gain, query_bias, key_gain, w_value, w_gate, w_out, ffn_gain, w_swish, w_up, w_down = params
    shared_w = low(w_shared)
    value_w = low(w_value)
    gate_w = low(w_gate)
    out_w = low(w_out)
    swish_w = low(w_swish)
    up_w = low(w_up)
    down_w = low(w_down)
    normed = step_norm(inputs, norm_gain, seg_ids, TN_GROUPS)
    ema_out = ema_all(normed, ema_rate, ema_angle, ema_input, ema_output, ema_skip, seg_ids)
    mixed_in = low(silu_of(ema_out))
    latent = low_back(jnp.dot(mixed_in, shared_w, precision=HIGHEST))
    queries = low(latent * query_gain + query_bias)
    keys_in = low(latent * key_gain)
    values_in = low(silu_of(low_back(jnp.dot(low(normed), value_w, precision=HIGHEST))))
    gate_act = silu_of(low_back(jnp.dot(mixed_in, gate_w, precision=HIGHEST)))
    attended = low_back(attention(queries, keys_in, values_in, seg_ids))
    branch = low_back(jnp.dot(low(gate_act * attended), out_w, precision=HIGHEST))
    residual = inputs + branch
    norm_in = low(residual * lax.rsqrt(lax.optimization_barrier(jnp.mean(residual * residual, axis=1, keepdims=True)) + EPSILON) * ffn_gain)
    swish_in = low_back(jnp.dot(norm_in, swish_w, precision=HIGHEST))
    up_in = low_back(jnp.dot(norm_in, up_w, precision=HIGHEST))
    hidden = low(silu_of(swish_in) * up_in)
    return residual + low_back(jnp.dot(hidden, down_w, precision=HIGHEST))

def reference(block_in, segments, norm_gain, ema_rate, ema_angle, ema_input, ema_output, ema_skip, w_shared, query_gain, query_bias, key_gain, w_value, w_gate, w_out, ffn_gain, w_swish, w_up, w_down, out_grad):
    weights = (norm_gain, ema_rate, ema_angle, ema_input, ema_output, ema_skip, w_shared, query_gain, query_bias, key_gain, w_value, w_gate, w_out, ffn_gain, w_swish, w_up, w_down)
    seq_total, seq_length = segments.shape
    features = block_in.shape[1]
    inputs = block_in.astype(jnp.float32).reshape(seq_total, seq_length, features)
    cotangent = out_grad.astype(jnp.float32).reshape(seq_total, seq_length, features)

    def one_sequence(totals, seq_items):
        rows_in, seg_ids, rows_grad = seq_items

        def forward(params, layer_in):
            return sequence_forward(params, layer_in, seg_ids)
        outputs, pullback = jax.vjp(forward, weights, rows_in)
        grad_params, grad_rows = pullback(rows_grad)
        return (jax.tree.map(jnp.add, totals, grad_params), (outputs, grad_rows))
    zero_grads = jax.tree.map(jnp.zeros_like, weights)
    totals, (outputs, grad_inputs) = lax.scan(one_sequence, zero_grads, (inputs, segments, cotangent))
    block_out = outputs.reshape(seq_total * seq_length, features).astype(jnp.bfloat16)
    in_grad = grad_inputs.reshape(seq_total * seq_length, features)
    return (block_out, in_grad, totals[0], totals[1], totals[2], totals[3], totals[4], totals[5], totals[6], totals[7], totals[8], totals[9], totals[10], totals[11], totals[12], totals[13], totals[14], totals[15], totals[16])
```

```python
import functools
import math

import jax
import jax.numpy as jnp
from jax import lax
from jax.experimental import pallas as pl
from jax.experimental.pallas import tpu as pltpu
from jax.sharding import PartitionSpec as P

TN_GROUPS = 16
EPSILON = 1e-05
REACH = 800
STEP = 16
LANES = 128
F32 = jnp.float32
BF16 = jnp.bfloat16
HIGHEST = lax.Precision.HIGHEST
BOTH = ("dp", "tensor")


def dot32(a, b, dims=((1,), (0,)), precision=None):
    return lax.dot_general(a, b, (dims, ((), ())), precision=precision, preferred_element_type=F32)


NT = ((1,), (1,))
TN = ((0,), (0,))


def silu_of(v):
    return v * jax.nn.sigmoid(v)


def silu_slope(v):
    sg = jax.nn.sigmoid(v)
    return sg * (1.0 + v * (1.0 - sg))


def broadcast_row(ref, row):
    return ref[pl.ds(row, 8, stride=0), :]


def rotate(x, shift):
    return pltpu.roll(x, shift % 8, axis=0)


def ema_enter(rows, dims, h_ref, kend_ref, br_ref, bi_ref, qs_ref, cont_ref, mk_ref, l_ref, end_ref, hm):
    groups = rows // (8 * STEP)
    for g in range(groups):
        for i in range(STEP):
            at = g * STEP + i
            h = h_ref[pl.ds(at, 8, stride=groups * STEP), :]
            hm[at] = h * kend_ref[at]

    def quad(jq, carry):
        for half in range(2):
            acc = [[None] * 4 for _ in range(groups)]
            for i in range(STEP):
                cr = [broadcast_row(br_ref, i * dims + jq * 4 + half * 2 + k) for k in range(2)]
                ci = [broadcast_row(bi_ref, i * dims + jq * 4 + half * 2 + k) for k in range(2)]
                for g in range(groups):
                    h = hm[g * STEP + i]
                    terms = [cr[0] * h, ci[0] * h, cr[1] * h, ci[1] * h]
                    acc[g] = terms if i == 0 else [a + t for a, t in zip(acc[g], terms)]
            for g in range(groups):
                for k in range(2):
                    j = jq * 4 + half * 2 + k
                    l_ref[(g * dims + j) * 2] = acc[g][2 * k]
                    l_ref[(g * dims + j) * 2 + 1] = acc[g][2 * k + 1]
        return carry

    lax.fori_loop(0, dims // 4, quad, 0)

    def one(j, carry):
        zero = jnp.zeros((8, LANES), F32)
        states = scan_states(groups, dims, j, l_ref, qs_ref, cont_ref, mk_ref, zero, zero)
        end_ref[pl.ds(2 * j, 1), :] = states[1][0][7:8]
        end_ref[pl.ds(2 * j + 1, 1), :] = states[1][1][7:8]
        return carry

    lax.fori_loop(0, dims, one, 0)


def scan_states(groups, dims, j, l_ref, qs_ref, cont_ref, mk_ref, inr, ini):
    qr, qi = broadcast_row(qs_ref, 2 * j), broadcast_row(qs_ref, 2 * j + 1)
    part = [(l_ref[(g * dims + j) * 2], l_ref[(g * dims + j) * 2 + 1]) for g in range(groups)]

    def through(sr, si):
        starts = []
        for g in range(groups):
            starts.append((sr, si))
            keep = cont_ref[g]
            sr, si = (
                keep * (qr * sr - qi * si) + part[g][0],
                keep * (qr * si + qi * sr) + part[g][1],
            )
        return starts, sr, si

    _, er, ei = through(inr, ini)
    for k in range(3):
        wr = broadcast_row(qs_ref, 2 * dims * (k + 1) + 2 * j)
        wi = broadcast_row(qs_ref, 2 * dims * (k + 1) + 2 * j + 1)
        pr, pi = rotate(er, 1 << k), rotate(ei, 1 << k)
        keep = mk_ref[k]
        er, ei = er + keep * (wr * pr - wi * pi), ei + keep * (wr * pi + wi * pr)
    first = lax.broadcasted_iota(jnp.int32, (8, LANES), 0) == 0
    sr = jnp.where(first, inr, rotate(er, 1))
    si = jnp.where(first, ini, rotate(ei, 1))
    starts, _, _ = through(sr, si)
    return starts, (er, ei)


def ema_read(
    rows, dims, h_ref, seg_ref, k0_ref, ar_ref, ai_ref, kd_ref, qs_ref, cont_ref, mk_ref, l_ref, in_ref, skip_ref,
    e_ref, m_ref, s_ref, hs
):
    groups = rows // (8 * STEP)
    first = lax.broadcasted_iota(jnp.int32, (8, LANES), 0) == 0

    def one(j, carry):
        inr = jnp.where(first, broadcast_row(in_ref, 2 * j), 0.0)
        ini = jnp.where(first, broadcast_row(in_ref, 2 * j + 1), 0.0)
        starts, _ = scan_states(groups, dims, j, l_ref, qs_ref, cont_ref, mk_ref, inr, ini)
        for g in range(groups):
            s_ref[(g * dims + j) * 2] = starts[g][0]
            s_ref[(g * dims + j) * 2 + 1] = starts[g][1]
        return carry

    lax.fori_loop(0, dims, one, 0)
    for g in range(groups):
        for i in range(STEP):
            at = g * STEP + i
            hs[at] = h_ref[pl.ds(at, 8, stride=groups * STEP), :]

    block = 4

    def some(iq, carry):
        acc = [[None] * block for _ in range(groups)]
        for j in range(dims):
            states = [(s_ref[(g * dims + j) * 2], s_ref[(g * dims + j) * 2 + 1]) for g in range(groups)]
            for i in range(block):
                cr = broadcast_row(ar_ref, (iq * block + i) * dims + j)
                ci = broadcast_row(ai_ref, (iq * block + i) * dims + j)
                for g in range(groups):
                    term = cr * states[g][0] - ci * states[g][1]
                    acc[g][i] = term if j == 0 else acc[g][i] + term
        for g in range(groups):
            for i in range(block):
                at = g * STEP + iq * block + i
                hs[groups * STEP + at] = acc[g][i] * k0_ref[at]
        return carry

    lax.fori_loop(0, STEP // block, some, 0)
    taps = [jnp.broadcast_to(kd_ref[d : d + 1, :], (8, LANES)) for d in range(STEP)]
    skip = jnp.broadcast_to(skip_ref[...], (8, LANES))
    tap0 = taps[0] + skip
    for g in range(groups):
        for i in range(STEP):
            at = g * STEP + i
            seg = seg_ref[at]
            out = hs[groups * STEP + at] + tap0 * hs[at]
            for s in range(i):
                src = g * STEP + s
                out = out + taps[i - s] * jnp.where(seg_ref[src] == seg, hs[src], 0.0)
            e_ref[pl.ds(at, 8, stride=groups * STEP), :] = out
    e = e_ref[...]
    m_ref[...] = silu_of(e).astype(m_ref.dtype)


def reverse_states(groups, dims, j, g_ref, qs_ref, cont_ref, mkr_ref, inr, ini):
    qr, qi = broadcast_row(qs_ref, 2 * j), broadcast_row(qs_ref, 2 * j + 1)
    part = [(g_ref[(g * dims + j) * 2], g_ref[(g * dims + j) * 2 + 1]) for g in range(groups)]

    def through(yr, yi):
        ends = [None] * groups
        for g in reversed(range(groups)):
            ends[g] = (yr, yi)
            keep = cont_ref[g]
            yr, yi = (
                keep * (qr * yr + qi * yi) + part[g][0],
                keep * (qr * yi - qi * yr) + part[g][1],
            )
        return ends, yr, yi

    _, fr, fi = through(inr, ini)
    for k in range(3):
        wr = broadcast_row(qs_ref, 2 * dims * (k + 1) + 2 * j)
        wi = broadcast_row(qs_ref, 2 * dims * (k + 1) + 2 * j + 1)
        pr, pi = rotate(fr, -(1 << k)), rotate(fi, -(1 << k))
        keep = mkr_ref[k]
        fr, fi = fr + keep * (wr * pr + wi * pi), fi + keep * (wr * pi - wi * pr)
    last = lax.broadcasted_iota(jnp.int32, (8, LANES), 0) == 7
    yr = jnp.where(last, inr, rotate(fr, -1))
    yi = jnp.where(last, ini, rotate(fi, -1))
    ends, _, _ = through(yr, yi)
    return ends, (fr, fi)


def ema_leave(rows, dims, de_ref, k0_ref, ar_ref, ai_ref, qs_ref, cont_ref, mkr_ref, g_ref, head_ref, dm):
    groups = rows // (8 * STEP)
    for g in range(groups):
        for i in range(STEP):
            at = g * STEP + i
            dm[at] = de_ref[pl.ds(at, 8, stride=groups * STEP), :] * k0_ref[at]

    def quad(jq, carry):
        for half in range(2):
            acc = [[None] * 4 for _ in range(groups)]
            for i in range(STEP):
                cr = [broadcast_row(ar_ref, i * dims + jq * 4 + half * 2 + k) for k in range(2)]
                ci = [broadcast_row(ai_ref, i * dims + jq * 4 + half * 2 + k) for k in range(2)]
                for g in range(groups):
                    d = dm[g * STEP + i]
                    terms = [cr[0] * d, ci[0] * d, cr[1] * d, ci[1] * d]
                    acc[g] = terms if i == 0 else [a + t for a, t in zip(acc[g], terms)]
            for g in range(groups):
                for k in range(2):
                    j = jq * 4 + half * 2 + k
                    g_ref[(g * dims + j) * 2] = acc[g][2 * k]
                    g_ref[(g * dims + j) * 2 + 1] = -acc[g][2 * k + 1]
        return carry

    lax.fori_loop(0, dims // 4, quad, 0)

    def one(j, carry):
        zero = jnp.zeros((8, LANES), F32)
        _, heads = reverse_states(groups, dims, j, g_ref, qs_ref, cont_ref, mkr_ref, zero, zero)
        head_ref[pl.ds(2 * j, 1), :] = heads[0][0:1]
        head_ref[pl.ds(2 * j + 1, 1), :] = heads[1][0:1]
        return carry

    lax.fori_loop(0, dims, one, 0)


def ema_grads(
    rows, dims, h_ref, de_ref, seg_ref, kend_ref, rk0_ref, rkend_ref, br_ref, bi_ref, kd_ref, qs_ref, cont_ref,
    mkr_ref, g_ref, in_ref, s_ref, skip_ref, dh_ref, ga_ref, gb_ref, gk_ref, gq_ref, gs_ref, hs, ds, la
):
    groups = rows // (8 * STEP)
    last = lax.broadcasted_iota(jnp.int32, (8, LANES), 0) == 7

    def one(j, carry):
        inr = jnp.where(last, broadcast_row(in_ref, 2 * j), 0.0)
        ini = jnp.where(last, broadcast_row(in_ref, 2 * j + 1), 0.0)
        ends, _ = reverse_states(groups, dims, j, g_ref, qs_ref, cont_ref, mkr_ref, inr, ini)
        qr = jnp.zeros((8, LANES), F32)
        qi = jnp.zeros((8, LANES), F32)
        for g in range(groups):
            yr, yi = ends[g]
            la[(g * dims + j) * 2] = yr
            la[(g * dims + j) * 2 + 1] = yi
            keep = cont_ref[g]
            sr, si = s_ref[(g * dims + j) * 2], s_ref[(g * dims + j) * 2 + 1]
            qr = qr + keep * (yr * sr + yi * si)
            qi = qi + keep * (yi * sr - yr * si)
        gq_ref[pl.ds(2 * j, 1), :] = jnp.sum(qr, axis=0, keepdims=True)
        gq_ref[pl.ds(2 * j + 1, 1), :] = jnp.sum(qi, axis=0, keepdims=True)
        return carry

    lax.fori_loop(0, dims, one, 0)
    total = jnp.zeros((8, LANES), F32)
    for g in range(groups):
        for i in range(STEP):
            at = g * STEP + i
            h = h_ref[pl.ds(at, 8, stride=groups * STEP), :]
            d = de_ref[pl.ds(at, 8, stride=groups * STEP), :]
            hs[at] = h
            ds[at] = d
            total = total + h * d
    gs_ref[...] = jnp.sum(total, axis=0, keepdims=True)
    block = 4

    def some(iq, carry):
        acc = [[None] * block for _ in range(groups)]
        for j in range(dims):
            ends = [(la[(g * dims + j) * 2], la[(g * dims + j) * 2 + 1]) for g in range(groups)]
            for i in range(block):
                cr = broadcast_row(br_ref, (iq * block + i) * dims + j)
                ci = broadcast_row(bi_ref, (iq * block + i) * dims + j)
                for g in range(groups):
                    term = cr * ends[g][0] + ci * ends[g][1]
                    acc[g][i] = term if j == 0 else acc[g][i] + term
        for g in range(groups):
            for i in range(block):
                at = g * STEP + iq * block + i
                hs[groups * STEP + at] = acc[g][i] * kend_ref[at]
        return carry

    lax.fori_loop(0, STEP // block, some, 0)
    taps = [jnp.broadcast_to(kd_ref[d : d + 1, :], (8, LANES)) for d in range(STEP)]
    skip = jnp.broadcast_to(skip_ref[...], (8, LANES))
    tap0 = taps[0] + skip
    kacc = [jnp.zeros((8, LANES), F32) for _ in range(STEP)]
    kacc[0] = total
    for g in range(groups):
        for s in range(STEP):
            at = g * STEP + s
            seg = seg_ref[at]
            h = hs[at]
            out = hs[groups * STEP + at] + tap0 * ds[at]
            for t in range(s + 1, STEP):
                d = jnp.where(seg_ref[g * STEP + t] == seg, ds[g * STEP + t], 0.0)
                out = out + taps[t - s] * d
                kacc[t - s] = kacc[t - s] + h * d
            dh_ref[pl.ds(at, 8, stride=groups * STEP), :] = out
    for d in range(STEP):
        gk_ref[d : d + 1, :] = jnp.sum(kacc[d], axis=0, keepdims=True)

    def tables(jq, carry):
        width = 4

        def chunk(n, acc):
            sub, g = n // groups, n % groups
            base = pl.multiple_of(n * STEP, STEP)
            d = de_ref[pl.ds(base, STEP), :] * rk0_ref[pl.ds(base, STEP), :]
            h = h_ref[pl.ds(base, STEP), :] * rkend_ref[pl.ds(base, STEP), :]
            out = []
            for k in range(width):
                at = (g * dims + jq * width + k) * 2
                sr = s_ref[at, pl.ds(sub, STEP, stride=0), :]
                si = s_ref[at + 1, pl.ds(sub, STEP, stride=0), :]
                yr = la[at, pl.ds(sub, STEP, stride=0), :]
                yi = la[at + 1, pl.ds(sub, STEP, stride=0), :]
                a0, a1, b0, b1 = acc[4 * k : 4 * k + 4]
                out += [a0 + d * sr, a1 - d * si, b0 + h * yr, b1 + h * yi]
            return tuple(out)

        zero = jnp.zeros((STEP, LANES), F32)
        acc = lax.fori_loop(0, 8 * groups, chunk, (zero,) * (4 * width))
        for k in range(width):
            j = jq * width + k
            ga_ref[2 * j] = acc[4 * k]
            ga_ref[2 * j + 1] = acc[4 * k + 1]
            gb_ref[2 * j] = acc[4 * k + 2]
            gb_ref[2 * j + 1] = acc[4 * k + 3]
        return carry

    lax.fori_loop(0, dims // 4, tables, 0)


def col(rows):
    return pl.BlockSpec((rows, LANES), lambda i: (0, i))


def col3(a, b):
    return pl.BlockSpec((a, b, LANES), lambda i: (0, 0, i))


def whole(*shape):
    return pl.BlockSpec(shape, lambda i: (0,) * len(shape))


def ema_call(body, rows, dims, width, ins, outs, scratch, name, flops):
    specs = [s for _, s in ins]
    return pl.pallas_call(
        functools.partial(body, rows, dims),
        grid=(width // LANES,),
        in_specs=specs,
        out_specs=[s for _, s in outs],
        out_shape=[o for o, _ in outs],
        scratch_shapes=scratch,
        compiler_params=pltpu.CompilerParams(vmem_limit_bytes=48 << 20),
        cost_estimate=pl.CostEstimate(flops=flops, bytes_accessed=16 << 20, transcendentals=0),
        name=name,
    )(*[a for a, _ in ins])


def powers(rate, angle, first, count, axis):
    n = (first + jnp.arange(count)).astype(F32)
    n = n[:, None, None] if axis == 0 else n[None, :, None]
    rate, angle = jnp.expand_dims(rate, axis), jnp.expand_dims(angle, axis)
    size = jnp.exp(-rate * n)
    return size * jnp.cos(angle * n), size * jnp.sin(angle * n)


def ema_tables(rate, angle, feed_gain, read_gain, axis):
    feed = feed_gain * jnp.sqrt(1.0 - jnp.exp(-2.0 * rate))
    pr, pi = powers(rate, angle, 0, STEP + 1, axis)
    low = functools.partial(lax.slice_in_dim, start_index=0, limit_index=STEP, axis=axis)
    high = functools.partial(lax.slice_in_dim, start_index=1, limit_index=STEP + 1, axis=axis)
    e0, e1, f = (jnp.expand_dims(v, axis) for v in (read_gain[0], read_gain[1], feed))
    hr, hi, lr, li = high(pr), high(pi), low(pr), low(pi)
    ar, ai = e0 * hr - e1 * hi, e0 * hi + e1 * hr
    br, bi = jnp.flip(f * lr, axis), jnp.flip(f * li, axis)
    taps = jnp.sum(f * (e0 * lr - e1 * li), axis=1 - axis)
    top = functools.partial(lax.index_in_dim, index=STEP, axis=axis, keepdims=False)
    return ar, ai, br, bi, taps, top(pr), top(pi)


def power_of(rate, angle, n):
    size = jnp.exp(-rate * n)
    return size * jnp.cos(angle * n), size * jnp.sin(angle * n)


def spread(v):
    return jnp.broadcast_to(v[..., None], v.shape + (LANES,))


def row_masks(seg, before):
    rows = seg.shape[0]
    groups = rows // (8 * STEP)
    cube = seg.reshape(8, groups, STEP)
    chunk_last = cube[:, :, -1]
    prior = jnp.concatenate([before[None], chunk_last.reshape(-1)[:-1]]).reshape(8, groups)
    keep0 = (cube == prior[:, :, None]).astype(F32)
    kend = (cube == chunk_last[:, :, None]).astype(F32)
    order = lambda v: spread(v.transpose(1, 2, 0).reshape(groups * STEP, 8))
    cont = spread((chunk_last == prior).astype(F32).transpose(1, 0))
    ends = jnp.concatenate([before[None], chunk_last[:, -1]])
    sub = jnp.arange(8)
    ahead, behind = [], []
    for k in range(3):
        w = 1 << k
        a = jnp.take(ends, jnp.maximum(sub + 1 - w, 0))
        ahead.append(((ends[1:] == a) & (sub >= w)).astype(F32))
        b = jnp.take(ends, jnp.minimum(sub + w, 8))
        behind.append(((ends[:8] == b) & (sub + w <= 7)).astype(F32))
    return dict(
        seg=order(cube.astype(F32)), keep0=order(keep0), kend=order(kend), cont=cont,
        mk=spread(jnp.stack(ahead)), mkr=spread(jnp.stack(behind)),
        rk0=spread(keep0.reshape(rows)), rkend=spread(kend.reshape(rows)),
    )


def on_device(
    block_in, segments, norm_gain, ema_rate, ema_angle, ema_input, ema_output, ema_skip, w_shared, query_gain,
    query_bias, key_gain, w_value, w_gate, w_out, ffn_gain, w_swish, w_up, w_down, out_grad,
):
    parts = lax.axis_size("tensor")
    replicas = lax.axis_size("dp")
    rank = lax.axis_index("tensor")
    rows, width = block_in.shape
    dims = ema_rate.shape[0]
    length = segments.shape[1]
    groups = TN_GROUPS
    span = width // groups
    latent_width = w_shared.shape[1]
    value_width = w_value.shape[1] * parts
    ffn_width = w_swish.shape[1] * parts
    depth = w_value.shape[0]
    hops = [min(rows, REACH - h * rows) for h in range(-(-REACH // rows))]
    halo = sum(hops)

    def from_earlier(x, hop):
        return lax.ppermute(x, "tensor", [(i, i + hop) for i in range(parts - hop)])

    def from_later(x, hop):
        return lax.ppermute(x, "tensor", [(i + hop, i) for i in range(parts - hop)])

    def halo_of(x):
        pieces = [from_earlier(x[rows - n :], h + 1) for h, n in enumerate(hops)]
        return jnp.concatenate(pieces[::-1] + [x], axis=0)

    def give_back(x):
        total = x[halo:].astype(F32)
        end = halo
        for h, n in enumerate(hops):
            got = from_later(x[end - n : end].astype(BF16), h + 1).astype(F32)
            total = total.at[rows - n :].add(got)
            end -= n
        return total

    piece = depth // parts
    shared_piece = lax.dynamic_slice_in_dim(w_shared, rank * piece, piece, 0)
    low = lambda w: w.astype(BF16)
    vw, fw = value_width // parts, ffn_width // parts
    pack_a = jnp.concatenate([low(w_value), low(w_gate), low(w_out.T)], axis=0)
    pack_f = jnp.concatenate([low(w_swish), low(w_up), low(w_down.T)], axis=0)
    all_s = lax.all_gather(low(shared_piece), BOTH, axis=0, tiled=True)
    all_a = lax.all_gather(pack_a, BOTH, axis=0).reshape(replicas, parts, 3, depth, vw)
    all_f = lax.all_gather(pack_f, BOTH, axis=0).reshape(replicas, parts, 3, depth, fw)
    flat = lambda w, k: w[:, :, k].transpose(0, 2, 1, 3).reshape(width, -1)
    value_b, gate_b, out_t = (flat(all_a, k) for k in range(3))
    swish_b, up_b, down_t = (flat(all_f, k) for k in range(3))
    shared_b = all_s

    seg_all = segments[0]
    padded = jnp.concatenate([jnp.full((halo,), -1, jnp.int32), seg_all, jnp.full((halo,), -2, jnp.int32)])
    near = lax.dynamic_slice_in_dim(padded, rank * rows, halo + rows + halo, 0)
    seg_keys = near[: halo + rows]
    seg = near[halo : halo + rows]
    before = near[halo - 1]
    masks = row_masks(seg, before)
    index = rank * rows + jnp.arange(rows, dtype=jnp.int32)
    start = jnp.sum((seg_all[None, :] < seg[:, None]).astype(jnp.int32), axis=1)
    count = (index - start + 1).astype(F32)[:, None] * span
    tri = jnp.arange(rows)
    same = seg[:, None] == seg[None, :]
    lower = (same & (tri[:, None] >= tri[None, :])).astype(F32)
    link1 = (seg[0] == before).astype(F32)
    link2 = (before == near[halo - rows - 1]).astype(F32)
    last = seg[-1]
    next1 = (near[halo + rows] == last).astype(F32)
    next2 = ((near[halo + 2 * rows - 1] == last) & (near[halo + 2 * rows] == last)).astype(F32) if halo > rows else 0.0
    heads = (seg == before).astype(F32)[:, None]
    tails = (seg == last).astype(F32)[:, None]

    x = block_in.astype(F32)
    gather = (jnp.arange(width)[:, None] // span == jnp.arange(groups)[None, :]).astype(F32)
    sums_of = lambda v: dot32(v, gather, precision=HIGHEST)
    spread_of = lambda v: dot32(v, gather, NT, precision=HIGHEST)
    sums = jnp.concatenate([dot32(block_in, gather.astype(BF16)), sums_of(x * x)], axis=1)
    running = dot32(lower, sums, precision=HIGHEST)
    tail = running[-1:]
    carry = from_earlier(tail, 1) + link2 * from_earlier(tail, 2)
    running = running + heads * carry
    mean = running[:, :groups] / count
    var = running[:, groups:] / count - mean * mean
    rho = lax.rsqrt(var + EPSILON)
    mean_full, rho_full = spread_of(mean), spread_of(rho)
    centred = (x - mean_full) * rho_full
    hidden = centred * norm_gain
    hidden_b = low(hidden)

    ar, ai, br, bi, taps, qr, qi = ema_tables(ema_rate, ema_angle, ema_input, ema_output, 0)
    stack2 = lambda r, i: jnp.stack([r, i], axis=1).reshape(2 * dims, width)
    sub_rows = rows // 8
    scales = jnp.concatenate(
        [stack2(qr, qi)] + [stack2(*power_of(ema_rate, ema_angle, float(sub_rows << k))) for k in range(3)]
    )
    flat2 = lambda v: v.reshape(STEP * dims, width)
    ar, ai, br, bi = flat2(ar), flat2(ai), flat2(br), flat2(bi)
    skip = ema_skip[None]
    gcount = rows // (8 * STEP)
    nstate = gcount * dims * 2
    at_rows = gcount * STEP
    state_shape = (jax.ShapeDtypeStruct((nstate, 8, width), F32), col3(nstate, 8))
    edge_shape = (jax.ShapeDtypeStruct((2 * dims, width), F32), col(2 * dims))
    table = col(STEP * dims)
    mask_spec = whole(at_rows, 8, LANES)
    cont_spec, mk_spec = whole(gcount, 8, LANES), whole(3, 8, LANES)
    qs_spec = col(8 * dims)
    vm = lambda n: pltpu.VMEM((n, 8, LANES), F32)
    mac = rows * width * dims * 4
    entering, end = ema_call(
        ema_enter, rows, dims, width,
        [(hidden, col(rows)), (masks["kend"], mask_spec), (br, table), (bi, table), (scales, qs_spec),
         (masks["cont"], cont_spec), (masks["mk"], mk_spec)],
        [state_shape, edge_shape], [vm(at_rows)], "ema_enter", mac,
    )
    whole_r, whole_i = power_of(ema_rate, ema_angle, float(rows))

    def turned(v, sign):
        v = v.reshape(dims, 2, width)
        r, i = v[:, 0], v[:, 1]
        wi = sign * whole_i
        return stack2(whole_r * r - wi * i, whole_r * i + wi * r)

    state_in = from_earlier(end, 1) + link2 * turned(from_earlier(end, 2), 1.0)
    ema_out, mixed, states = ema_call(
        ema_read, rows, dims, width,
        [(hidden, col(rows)), (masks["seg"], mask_spec), (masks["keep0"], mask_spec), (ar, table), (ai, table),
         (taps, col(STEP)), (scales, qs_spec), (masks["cont"], cont_spec), (masks["mk"], mk_spec),
         (entering, col3(nstate, 8)), (state_in, col(2 * dims)), (skip, col(1))],
        [(jax.ShapeDtypeStruct((rows, width), F32), col(rows)), (jax.ShapeDtypeStruct((rows, width), BF16), col(rows)),
         state_shape],
        [vm(2 * at_rows)], "ema_read", mac,
    )

    hidden_near = halo_of(hidden_b)
    latent = dot32(mixed, shared_b)
    queries = low(latent * query_gain + query_bias)
    keys_own = low(latent * key_gain)
    keys_near = halo_of(keys_own)
    value_pre = dot32(hidden_near, value_b)
    values = low(silu_of(value_pre))
    gate_pre = dot32(mixed, gate_b)
    gate_act = silu_of(gate_pre)
    scale = 1.0 / math.sqrt(latent_width)
    key_at = jnp.arange(halo + rows, dtype=jnp.int32)
    allowed = (key_at[None, :] <= halo + tri[:, None]) & (seg_keys[None, :] == seg[:, None])
    scores = jnp.where(allowed, dot32(queries, keys_near, NT) * scale, -1e30)
    peak = jnp.max(scores, axis=1, keepdims=True)
    raw = jnp.exp(scores - peak)
    probs = raw / jnp.sum(raw, axis=1, keepdims=True)
    probs_b = low(probs)
    attended = dot32(probs_b, values)
    gated = low(gate_act * attended)
    residual = x + dot32(gated, out_t, NT)

    rr = lax.rsqrt(jnp.mean(residual * residual, axis=1, keepdims=True) + EPSILON)
    nh = residual * rr
    norm_in = low(nh * ffn_gain)
    swish_pre = dot32(norm_in, swish_b)
    up_pre = dot32(norm_in, up_b)
    swish_act = silu_of(swish_pre)
    inner = low(swish_act * up_pre)
    block_out = low(residual + dot32(inner, down_t, NT))

    grad_inner = dot32(out_grad, down_t)
    grad_swish_pre = low(grad_inner * up_pre * silu_slope(swish_pre))
    grad_up_pre = low(grad_inner * swish_act)

    def shards(g):
        return low(g).reshape(replicas, depth, parts, -1).transpose(0, 2, 1, 3)

    def summed(pieces):
        g = jnp.concatenate(pieces, axis=2)
        g = lax.psum_scatter(g, "dp", scatter_dimension=0, tiled=False)
        return lax.psum_scatter(g, "tensor", scatter_dimension=0, tiled=False).astype(F32)

    ffn_sum = summed([
        shards(dot32(norm_in, grad_swish_pre, TN)),
        shards(dot32(norm_in, grad_up_pre, TN)),
        shards(dot32(out_grad, inner, TN)),
    ])
    grad_nn = dot32(grad_swish_pre, swish_b, NT) + dot32(grad_up_pre, up_b, NT)
    grad_ffn_gain = jnp.sum(nh * grad_nn, axis=0)
    scaled = grad_nn * ffn_gain
    grad_residual = out_grad.astype(F32) + rr * (scaled - nh * jnp.mean(nh * scaled, axis=1, keepdims=True))
    branch = low(grad_residual)

    grad_gated = dot32(branch, out_t)
    grad_attended = low(grad_gated * gate_act)
    grad_gate_pre = low(grad_gated * attended * silu_slope(gate_pre))
    grad_probs = dot32(grad_attended, values, NT)
    centre = jnp.sum(probs * grad_probs, axis=1, keepdims=True)
    grad_scores = low(probs * (grad_probs - centre))
    grad_queries = dot32(grad_scores, keys_near) * scale
    grad_keys = give_back(dot32(grad_scores, queries, TN) * scale)
    grad_value_pre = low(dot32(probs_b, grad_attended, TN) * silu_slope(value_pre))
    grad_hidden = give_back(dot32(grad_value_pre, value_b, NT))
    grad_query_gain = jnp.sum(latent * grad_queries, axis=0)
    grad_query_bias = jnp.sum(grad_queries, axis=0)
    grad_key_gain = jnp.sum(latent * grad_keys, axis=0)
    grad_latent = low(grad_queries * query_gain + grad_keys * key_gain)
    grad_shared = low(dot32(mixed, grad_latent, TN)).reshape(replicas, parts, -1, vw)
    attn_sum = summed([
        shards(dot32(hidden_near, grad_value_pre, TN)),
        shards(dot32(mixed, grad_gate_pre, TN)),
        shards(dot32(branch, gated, TN)),
        grad_shared,
    ])
    grad_ema = (dot32(grad_latent, shared_b, NT) + dot32(grad_gate_pre, gate_b, NT)) * silu_slope(ema_out)

    pulls, head = ema_call(
        ema_leave, rows, dims, width,
        [(grad_ema, col(rows)), (masks["keep0"], mask_spec), (ar, table), (ai, table), (scales, qs_spec),
         (masks["cont"], cont_spec), (masks["mkr"], mk_spec)],
        [state_shape, edge_shape], [vm(at_rows)], "ema_leave", mac,
    )
    cross = (near[halo + 2 * rows - 1] == last).astype(F32)
    pull_in = from_later(head, 1) + cross * turned(from_later(head, 2), -1.0)
    grad_hidden_ema, grad_a, grad_b, grad_taps, grad_q, grad_skip = ema_call(
        ema_grads, rows, dims, width,
        [(hidden, col(rows)), (grad_ema, col(rows)), (masks["seg"], mask_spec), (masks["kend"], mask_spec),
         (masks["rk0"], whole(rows, LANES)), (masks["rkend"], whole(rows, LANES)), (br, table), (bi, table),
         (taps, col(STEP)), (scales, qs_spec), (masks["cont"], cont_spec), (masks["mkr"], mk_spec),
         (pulls, col3(nstate, 8)), (pull_in, col(2 * dims)), (states, col3(nstate, 8)), (skip, col(1))],
        [(jax.ShapeDtypeStruct((rows, width), F32), col(rows)),
         (jax.ShapeDtypeStruct((2 * dims, STEP, width), F32), col3(2 * dims, STEP)),
         (jax.ShapeDtypeStruct((2 * dims, STEP, width), F32), col3(2 * dims, STEP)),
         (jax.ShapeDtypeStruct((STEP, width), F32), col(STEP)), edge_shape,
         (jax.ShapeDtypeStruct((1, width), F32), col(1))],
        [vm(2 * at_rows), vm(at_rows), vm(nstate)], "ema_grads", 3 * mac,
    )
    four = lambda v: v.reshape(dims, 2, STEP, width)
    ga, gb, gq = four(grad_a), four(grad_b), grad_q.reshape(dims, 2, width)
    _, table_pull = jax.vjp(functools.partial(ema_tables, axis=1), ema_rate, ema_angle, ema_input, ema_output)
    rate_grad, angle_grad, input_grad, output_grad = table_pull(
        (ga[:, 0], ga[:, 1], gb[:, 0], gb[:, 1], grad_taps, gq[:, 0], gq[:, 1])
    )

    grad_hidden = grad_hidden + grad_hidden_ema
    gain_grad = jnp.sum(centred * grad_hidden, axis=0)
    spread_grad = grad_hidden * norm_gain
    sum_a = rho * sums_of(spread_grad)
    sum_b = sums_of(spread_grad * (x - mean_full))
    cube = sum_b * rho * rho * rho
    push = jnp.concatenate([(cube * mean - sum_a) / count, -cube / (2.0 * count)], axis=1)
    backed = dot32(lower, push, TN, precision=HIGHEST)
    first = backed[:1]
    carry = next1 * from_later(first, 1) + next2 * from_later(first, 2)
    backed = backed + tails * carry
    grad_x = spread_grad * rho_full + spread_of(backed[:, :groups]) + 2.0 * x * spread_of(backed[:, groups:])
    in_grad = grad_residual + grad_x

    small = [gain_grad, rate_grad, angle_grad, input_grad, output_grad, grad_skip, grad_query_gain,
             grad_query_bias, grad_key_gain, grad_ffn_gain]
    sizes = [v.size for v in small]
    total = sum(sizes)
    members = parts * replicas
    unit = members * 8 * LANES
    packed = jnp.concatenate([v.reshape(-1) for v in small] + [jnp.zeros((-total % unit,), F32)])
    packed = packed.reshape(members * 8, -1)
    packed = lax.psum_scatter(packed, BOTH, scatter_dimension=0, tiled=True)
    packed = lax.all_gather(packed, BOTH, axis=0, tiled=True).reshape(-1)
    small_sums, at = [], 0
    for n in sizes:
        small_sums.append(packed[at : at + n])
        at += n
    shape = lambda k, like: small_sums[k].reshape(like.shape)

    shared_sum = lax.all_gather(attn_sum[3 * depth :].reshape(piece, latent_width), "tensor", axis=0, tiled=True)
    cut = lambda g, k: g[k * depth : (k + 1) * depth]
    return (
        block_out, in_grad, shape(0, norm_gain), shape(1, ema_rate), shape(2, ema_angle), shape(3, ema_input),
        shape(4, ema_output), shape(5, ema_skip), shared_sum, shape(6, query_gain), shape(7, query_bias),
        shape(8, key_gain), cut(attn_sum, 0), cut(attn_sum, 1), cut(attn_sum, 2).T, shape(9, ffn_gain),
        cut(ffn_sum, 0), cut(ffn_sum, 1), cut(ffn_sum, 2).T,
    )


def solution(mesh):
    rows, dp, copy = P(BOTH, None), P("dp", None), P()
    wide, tall = P("dp", "tensor"), P("tensor", "dp")
    return jax.shard_map(
        on_device,
        mesh=mesh,
        in_specs=(
            rows, dp, copy, copy, copy, copy, copy, copy, dp, copy, copy, copy, wide, wide, tall, copy, wide, wide,
            tall, rows,
        ),
        out_specs=(
            rows, rows, copy, copy, copy, copy, copy, copy, dp, copy, copy, copy, wide, wide, tall, copy, wide, wide,
            tall,
        ),
        check_vma=False,
    )
```

```python
import functools
import math

import jax
import jax.numpy as jnp
from jax import lax
from jax.experimental import pallas as pl
from jax.experimental.pallas import tpu as pltpu
from jax.experimental.layout import Layout, with_layout_constraint
from jax.sharding import PartitionSpec as P

TN_GROUPS = 16
EPSILON = 1e-05
REACH = 800
STEP = 16
LANES = 128
F32 = jnp.float32
BF16 = jnp.bfloat16
HIGHEST = lax.Precision.HIGHEST
BOTH = ("dp", "tensor")


def dot32(a, b, dims=((1,), (0,)), precision=None):
    return lax.dot_general(a, b, (dims, ((), ())), precision=precision, preferred_element_type=F32)


NT = ((1,), (1,))
TN = ((0,), (0,))


def silu_of(v):
    return v * jax.nn.sigmoid(v)


def silu_slope(v):
    sg = jax.nn.sigmoid(v)
    return sg * (1.0 + v * (1.0 - sg))


def broadcast_row(ref, row):
    return ref[pl.ds(row, 8, stride=0), :]


def rotate(x, shift):
    return pltpu.roll(x, shift % 8, axis=0)


def times(ar, ai, br, bi):
    return ar * br - ai * bi, ar * bi + ai * br


def power_list(dims, q_ref):
    qr, qi = q_ref[:dims], q_ref[dims:]
    out = [(jnp.ones_like(qr), jnp.zeros_like(qr))]
    for n in range(STEP):
        out.append(times(*out[-1], qr, qi))
    return out


def fill_scales(groups, dims, pw, qs):
    step = pw[STEP]
    qs[:dims], qs[dims : 2 * dims] = step
    turn = step
    for _ in range(groups - 1):
        turn = times(*turn, *step)
    for k in range(3):
        base = 2 * dims * (k + 1)
        qs[base : base + dims], qs[base + dims : base + 2 * dims] = turn
        turn = times(*turn, *turn)
    return turn


def fill_read(dims, pw, e_ref, ta):
    e0, e1 = e_ref[:dims], e_ref[dims:]
    for i in range(STEP):
        ta[0, i * dims : (i + 1) * dims], ta[1, i * dims : (i + 1) * dims] = times(e0, e1, *pw[i + 1])


def fill_feed(dims, pw, f_ref, tb):
    f = f_ref[...]
    for i in range(STEP):
        r, m = pw[STEP - 1 - i]
        tb[0, i * dims : (i + 1) * dims], tb[1, i * dims : (i + 1) * dims] = f * r, f * m


def tap_list(dims, pw, e_ref, f_ref):
    e0, e1, f = e_ref[:dims], e_ref[dims:], f_ref[...]
    out = []
    for d in range(STEP):
        row = jnp.sum(f * (e0 * pw[d][0] - e1 * pw[d][1]), axis=0, keepdims=True)
        out.append(jnp.broadcast_to(row, (8, LANES)))
    return out


def chunk_sums(groups, dims, table, source, out, sign):
    def pair(jp, carry):
        acc = [None] * groups
        for i in range(STEP):
            c = [broadcast_row(table.at[p], i * dims + jp * 2 + k) for k in range(2) for p in range(2)]
            for g in range(groups):
                h = source[g * STEP + i]
                terms = [v * h for v in c]
                acc[g] = terms if i == 0 else [u + v for u, v in zip(acc[g], terms)]
        for g in range(groups):
            for k in range(2):
                at = (g * dims + jp * 2 + k) * 2
                out[at] = acc[g][2 * k]
                out[at + 1] = acc[g][2 * k + 1] if sign > 0 else -acc[g][2 * k + 1]
        return carry

    lax.fori_loop(0, dims // 2, pair, 0)


def position_sums(groups, dims, table, states, mask, out, base, sign):
    block = 4

    def some(iq, carry):
        acc = [[None] * block for _ in range(groups)]
        for j in range(dims):
            here = [(states[(g * dims + j) * 2], states[(g * dims + j) * 2 + 1]) for g in range(groups)]
            for i in range(block):
                cr = broadcast_row(table.at[0], (iq * block + i) * dims + j)
                ci = broadcast_row(table.at[1], (iq * block + i) * dims + j)
                for g in range(groups):
                    u, v = cr * here[g][0], ci * here[g][1]
                    term = u - v if sign < 0 else u + v
                    acc[g][i] = term if j == 0 else acc[g][i] + term
        for g in range(groups):
            for i in range(block):
                at = g * STEP + iq * block + i
                out[base + at] = acc[g][i] * mask[at]
        return carry

    lax.fori_loop(0, STEP // block, some, 0)


def ema_enter(rows, dims, h_ref, kend_ref, q_ref, f_ref, cont_ref, mk_ref, l_ref, end_ref, turn_ref, hm, tb, qs):
    groups = rows // (8 * STEP)
    pw = power_list(dims, q_ref)
    turn_ref[:dims], turn_ref[dims:] = fill_scales(groups, dims, pw, qs)
    fill_feed(dims, pw, f_ref, tb)
    for at in range(groups * STEP):
        hm[at] = h_ref[pl.ds(at, 8, stride=groups * STEP), :] * kend_ref[at]
    chunk_sums(groups, dims, tb, hm, l_ref, 1)

    def one(j, carry):
        zero = jnp.zeros((8, LANES), F32)
        _, ends = scan_states(groups, dims, j, l_ref, qs, cont_ref, mk_ref, zero, zero)
        end_ref[pl.ds(j, 1), :] = ends[0][7:8]
        end_ref[pl.ds(dims + j, 1), :] = ends[1][7:8]
        return carry

    lax.fori_loop(0, dims, one, 0)


def scan_states(groups, dims, j, l_ref, qs, cont_ref, mk_ref, inr, ini):
    qr, qi = broadcast_row(qs, j), broadcast_row(qs, dims + j)
    part = [(l_ref[(g * dims + j) * 2], l_ref[(g * dims + j) * 2 + 1]) for g in range(groups)]

    def through(sr, si):
        starts = []
        for g in range(groups):
            starts.append((sr, si))
            keep = cont_ref[g]
            tr, ti = times(qr, qi, sr, si)
            sr, si = keep * tr + part[g][0], keep * ti + part[g][1]
        return starts, sr, si

    _, er, ei = through(inr, ini)
    for k in range(3):
        base = 2 * dims * (k + 1)
        wr, wi = broadcast_row(qs, base + j), broadcast_row(qs, base + dims + j)
        pr, pi = times(wr, wi, rotate(er, 1 << k), rotate(ei, 1 << k))
        keep = mk_ref[k]
        er, ei = er + keep * pr, ei + keep * pi
    first = lax.broadcasted_iota(jnp.int32, (8, LANES), 0) == 0
    starts, _, _ = through(jnp.where(first, inr, rotate(er, 1)), jnp.where(first, ini, rotate(ei, 1)))
    return starts, (er, ei)


def ema_read(
    rows, dims, h_ref, seg_ref, k0_ref, q_ref, f_ref, e_ref, cont_ref, mk_ref, l_ref, in_ref, skip_ref,
    out_ref, m_ref, s_ref, hs, ta, qs
):
    groups = rows // (8 * STEP)
    first = lax.broadcasted_iota(jnp.int32, (8, LANES), 0) == 0
    pw = power_list(dims, q_ref)
    fill_scales(groups, dims, pw, qs)
    fill_read(dims, pw, e_ref, ta)
    taps = tap_list(dims, pw, e_ref, f_ref)

    def one(j, carry):
        inr = jnp.where(first, broadcast_row(in_ref, j), 0.0)
        ini = jnp.where(first, broadcast_row(in_ref, dims + j), 0.0)
        starts, _ = scan_states(groups, dims, j, l_ref, qs, cont_ref, mk_ref, inr, ini)
        for g in range(groups):
            s_ref[(g * dims + j) * 2] = starts[g][0]
            s_ref[(g * dims + j) * 2 + 1] = starts[g][1]
        return carry

    lax.fori_loop(0, dims, one, 0)
    for at in range(groups * STEP):
        hs[at] = h_ref[pl.ds(at, 8, stride=groups * STEP), :]
    position_sums(groups, dims, ta, s_ref, k0_ref, hs, groups * STEP, -1)
    tap0 = taps[0] + jnp.broadcast_to(skip_ref[...], (8, LANES))
    for g in range(groups):
        for i in range(STEP):
            at = g * STEP + i
            seg = seg_ref[at]
            out = hs[groups * STEP + at] + tap0 * hs[at]
            for s in range(i):
                src = g * STEP + s
                out = out + taps[i - s] * jnp.where(seg_ref[src] == seg, hs[src], 0.0)
            out_ref[pl.ds(at, 8, stride=groups * STEP), :] = out
    m_ref[...] = silu_of(out_ref[...]).astype(m_ref.dtype)


def reverse_states(groups, dims, j, g_ref, qs, cont_ref, mkr_ref, inr, ini):
    qr, qi = broadcast_row(qs, j), broadcast_row(qs, dims + j)
    part = [(g_ref[(g * dims + j) * 2], g_ref[(g * dims + j) * 2 + 1]) for g in range(groups)]

    def through(yr, yi):
        ends = [None] * groups
        for g in reversed(range(groups)):
            ends[g] = (yr, yi)
            keep = cont_ref[g]
            tr, ti = qr * yr + qi * yi, qr * yi - qi * yr
            yr, yi = keep * tr + part[g][0], keep * ti + part[g][1]
        return ends, yr, yi

    _, fr, fi = through(inr, ini)
    for k in range(3):
        base = 2 * dims * (k + 1)
        wr, wi = broadcast_row(qs, base + j), broadcast_row(qs, base + dims + j)
        pr, pi = rotate(fr, -(1 << k)), rotate(fi, -(1 << k))
        keep = mkr_ref[k]
        fr, fi = fr + keep * (wr * pr + wi * pi), fi + keep * (wr * pi - wi * pr)
    last = lax.broadcasted_iota(jnp.int32, (8, LANES), 0) == 7
    ends, _, _ = through(jnp.where(last, inr, rotate(fr, -1)), jnp.where(last, ini, rotate(fi, -1)))
    return ends, (fr, fi)


def ema_leave(rows, dims, de_ref, k0_ref, q_ref, e_ref, cont_ref, mkr_ref, g_ref, head_ref, dm, ta, qs):
    groups = rows // (8 * STEP)
    pw = power_list(dims, q_ref)
    fill_scales(groups, dims, pw, qs)
    fill_read(dims, pw, e_ref, ta)
    for at in range(groups * STEP):
        dm[at] = de_ref[pl.ds(at, 8, stride=groups * STEP), :] * k0_ref[at]
    chunk_sums(groups, dims, ta, dm, g_ref, -1)

    def one(j, carry):
        zero = jnp.zeros((8, LANES), F32)
        _, heads = reverse_states(groups, dims, j, g_ref, qs, cont_ref, mkr_ref, zero, zero)
        head_ref[pl.ds(j, 1), :] = heads[0][0:1]
        head_ref[pl.ds(dims + j, 1), :] = heads[1][0:1]
        return carry

    lax.fori_loop(0, dims, one, 0)


def ema_grads(
    rows, dims, h_ref, de_ref, seg_ref, kend_ref, rk0_ref, rkend_ref, q_ref, f_ref, e_ref, root_ref, feed_ref, cont_ref,
    mkr_ref, g_ref, in_ref, s_ref, skip_ref, dh_ref, ge_ref, gf_ref, gr_ref, ga_ref, gs_ref, hs, ds, la, tb, qs, pf, red, hn, dn
):
    groups = rows // (8 * STEP)
    last = lax.broadcasted_iota(jnp.int32, (8, LANES), 0) == 7
    pw = power_list(dims, q_ref)
    fill_scales(groups, dims, pw, qs)
    fill_feed(dims, pw, f_ref, tb)
    taps = tap_list(dims, pw, e_ref, f_ref)
    for i in range(STEP):
        at = slice(i * dims, (i + 1) * dims)
        pf[0, at], pf[1, at] = pw[i + 1]
        pf[2, at], pf[3, at] = pw[STEP - 1 - i]

    def one(j, carry):
        inr = jnp.where(last, broadcast_row(in_ref, j), 0.0)
        ini = jnp.where(last, broadcast_row(in_ref, dims + j), 0.0)
        ends, _ = reverse_states(groups, dims, j, g_ref, qs, cont_ref, mkr_ref, inr, ini)
        qr = jnp.zeros((8, LANES), F32)
        qi = jnp.zeros((8, LANES), F32)
        for g in range(groups):
            yr, yi = ends[g]
            la[(g * dims + j) * 2] = yr
            la[(g * dims + j) * 2 + 1] = yi
            keep = cont_ref[g]
            sr, si = s_ref[(g * dims + j) * 2], s_ref[(g * dims + j) * 2 + 1]
            qr = qr + keep * (yr * sr + yi * si)
            qi = qi + keep * (yi * sr - yr * si)
        red[0, pl.ds(j, 1), :] = jnp.sum(qr, axis=0, keepdims=True)
        red[1, pl.ds(j, 1), :] = jnp.sum(qi, axis=0, keepdims=True)
        return carry

    lax.fori_loop(0, dims, one, 0)
    total = jnp.zeros((8, LANES), F32)
    for at in range(groups * STEP):
        h = h_ref[pl.ds(at, 8, stride=groups * STEP), :]
        d = de_ref[pl.ds(at, 8, stride=groups * STEP), :]
        hs[at] = h
        ds[at] = d
        total = total + h * d
    gs_ref[...] = jnp.sum(total, axis=0, keepdims=True)
    position_sums(groups, dims, tb, la, kend_ref, hs, groups * STEP, 1)
    tap0 = taps[0] + jnp.broadcast_to(skip_ref[...], (8, LANES))
    kacc = [jnp.zeros((8, LANES), F32) for _ in range(STEP)]
    kacc[0] = total
    for g in range(groups):
        for s in range(STEP):
            at = g * STEP + s
            seg = seg_ref[at]
            h = hs[at]
            out = hs[groups * STEP + at] + tap0 * ds[at]
            for t in range(s + 1, STEP):
                d = jnp.where(seg_ref[g * STEP + t] == seg, ds[g * STEP + t], 0.0)
                out = out + taps[t - s] * d
                kacc[t - s] = kacc[t - s] + h * d
            dh_ref[pl.ds(at, 8, stride=groups * STEP), :] = out

    hn[...] = h_ref[...] * rkend_ref[...]
    dn[...] = de_ref[...] * rk0_ref[...]
    width = 4
    place = (lax.broadcasted_iota(jnp.int32, (STEP, LANES), 0) + 1).astype(F32)

    def tables(jq, carry):
        def chunk(n, acc):
            sub, g = n // groups, n % groups
            d0, d1 = (dn[pl.ds(pl.multiple_of(n * STEP + 8 * p, 8), 8), :] for p in range(2))
            h0, h1 = (hn[pl.ds(pl.multiple_of(n * STEP + 8 * p, 8), 8), :] for p in range(2))
            out = []
            for k in range(width):
                at = (g * dims + jq * width + k) * 2
                sr, si = (s_ref[at + p, pl.ds(sub, 8, stride=0), :] for p in range(2))
                yr, yi = (la[at + p, pl.ds(sub, 8, stride=0), :] for p in range(2))
                a = acc[8 * k : 8 * k + 8]
                out += [a[0] + d0 * sr, a[1] + d1 * sr, a[2] - d0 * si, a[3] - d1 * si]
                out += [a[4] + h0 * yr, a[5] + h1 * yr, a[6] + h0 * yi, a[7] + h1 * yi]
            return tuple(out)

        acc = lax.fori_loop(0, 8 * groups, chunk, (jnp.zeros((8, LANES), F32),) * (8 * width))
        for k in range(width):
            j = jq * width + k
            ar, ai, br, bi = (
                jnp.concatenate([acc[8 * k + 2 * p], acc[8 * k + 2 * p + 1]], axis=0) for p in range(4)
            )
            pr, pi, wr, wi = (pf[p, pl.ds(j, STEP, stride=dims), :] for p in range(4))
            ur, ui = ar * pr + ai * pi, ai * pr - ar * pi
            vr, vi = br * wr + bi * wi, bi * wr - br * wi
            rest = STEP - place
            sums = (ur, ui, place * ur, place * ui, vr, rest * vr, rest * vi)
            for p, v in enumerate(sums):
                red[2 + p, pl.ds(j, 1), :] = jnp.sum(v, axis=0, keepdims=True)
        return carry

    lax.fori_loop(0, dims // width, tables, 0)
    e0, e1, f = e_ref[:dims], e_ref[dims:], f_ref[...]
    zero = jnp.zeros((dims, LANES), F32)
    tr, ti, ur, ui = zero, zero, zero, zero
    for d in range(STEP):
        tap = jnp.broadcast_to(jnp.sum(kacc[d], axis=0, keepdims=True), (dims, LANES))
        r, m = tap * pw[d][0], tap * pw[d][1]
        tr, ti = tr + r, ti - m
        if d > 0:
            ur, ui = ur + d * r, ui - d * m
    ge_ref[:dims] = red[2] + f * tr
    ge_ref[dims:] = red[3] + f * ti
    gf = red[6] + e0 * tr + e1 * ti
    xr, xi = red[4] + f * ur, red[5] + f * ui
    lr = e0 * xr + e1 * xi + f * red[7]
    li = e0 * xi - e1 * xr + f * red[8]
    zr, zi = pw[STEP]
    lr = lr + STEP * (red[0] * zr + red[1] * zi)
    li = li + STEP * (red[1] * zr - red[0] * zi)
    root = root_ref[...]
    gf_ref[...] = gf * root
    gr_ref[...] = gf * feed_ref[...] * (1.0 - root * root) / root - lr
    ga_ref[...] = li


def col(rows):
    return pl.BlockSpec((rows, LANES), lambda i: (0, i))


def col3(a, b):
    return pl.BlockSpec((a, b, LANES), lambda i: (0, 0, i))


def whole(*shape):
    return pl.BlockSpec(shape, lambda i: (0,) * len(shape))


def ema_call(body, rows, dims, width, ins, outs, scratch, name, flops):
    specs = [s for _, s in ins]
    return pl.pallas_call(
        functools.partial(body, rows, dims),
        grid=(width // LANES,),
        in_specs=specs,
        out_specs=[s for _, s in outs],
        out_shape=[o for o, _ in outs],
        scratch_shapes=scratch,
        compiler_params=pltpu.CompilerParams(vmem_limit_bytes=48 << 20),
        cost_estimate=pl.CostEstimate(flops=flops, bytes_accessed=16 << 20, transcendentals=0),
        name=name,
    )(*[a for a, _ in ins])


def spread(v):
    return jnp.broadcast_to(v[..., None], v.shape + (LANES,))


def row_masks(seg, before):
    rows = seg.shape[0]
    groups = rows // (8 * STEP)
    cube = seg.reshape(8, groups, STEP)
    chunk_last = cube[:, :, -1]
    prior = jnp.concatenate([before[None], chunk_last.reshape(-1)[:-1]]).reshape(8, groups)
    keep0 = (cube == prior[:, :, None]).astype(F32)
    kend = (cube == chunk_last[:, :, None]).astype(F32)
    order = lambda v: spread(v.transpose(1, 2, 0).reshape(groups * STEP, 8))
    cont = spread((chunk_last == prior).astype(F32).transpose(1, 0))
    ends = jnp.concatenate([before[None], chunk_last[:, -1]])
    sub = jnp.arange(8)
    ahead, behind = [], []
    for k in range(3):
        w = 1 << k
        a = jnp.take(ends, jnp.maximum(sub + 1 - w, 0))
        ahead.append(((ends[1:] == a) & (sub >= w)).astype(F32))
        b = jnp.take(ends, jnp.minimum(sub + w, 8))
        behind.append(((ends[:8] == b) & (sub + w <= 7)).astype(F32))
    return dict(
        seg=order(cube.astype(F32)), keep0=order(keep0), kend=order(kend), cont=cont,
        mk=spread(jnp.stack(ahead)), mkr=spread(jnp.stack(behind)),
        rk0=spread(keep0.reshape(rows)), rkend=spread(kend.reshape(rows)),
    )


def merged(ref):
    v = ref[...]
    return v.reshape(-1, v.shape[-1])


def attend_kernel(
    halo, q_ref, k_ref, seg_ref, segk_ref, h_ref, m_ref, x_ref, gain_ref, wv_ref, wg_ref, wo_ref,
    p_ref, vp_ref, v_ref, gp_ref, o_ref, g_ref, y_ref, n_ref, pb_ref,
):
    t = pl.program_id(0)

    @pl.when(t == 0)
    def _():
        rows, keys = pb_ref.shape
        scores = dot32(q_ref[...], k_ref[...], NT) * (1.0 / math.sqrt(q_ref.shape[1]))
        at_row = lax.broadcasted_iota(jnp.int32, (rows, keys), 0)
        at_key = lax.broadcasted_iota(jnp.int32, (rows, keys), 1)
        allowed = (at_key <= at_row + halo) & (segk_ref[...] == seg_ref[...])
        scores = jnp.where(allowed, scores, -1e30)
        raw = jnp.exp(scores - jnp.max(scores, axis=1, keepdims=True))
        p = raw / jnp.sum(raw, axis=1, keepdims=True)
        p_ref[...] = p
        pb_ref[...] = p.astype(BF16)
        y_ref[...] = x_ref[...].astype(F32)

    vp = dot32(h_ref[...], merged(wv_ref))
    v = silu_of(vp).astype(BF16)
    vp_ref[...] = vp.astype(BF16)
    v_ref[...] = v
    gp = dot32(m_ref[...], merged(wg_ref))
    gp_ref[...] = gp.astype(BF16)
    o = dot32(pb_ref[...], v)
    o_ref[...] = o.astype(BF16)
    g = (silu_of(gp) * o).astype(BF16)
    g_ref[...] = g
    y_ref[...] += dot32(g, merged(wo_ref), NT)

    @pl.when(t == pl.num_programs(0) - 1)
    def _():
        y = y_ref[...]
        rr = lax.rsqrt(jnp.mean(y * y, axis=1, keepdims=True) + EPSILON)
        n_ref[...] = (y * rr * gain_ref[...]).astype(BF16)


def ffn_kernel(
    y_ref, n_ref, og_ref, gain_ref, w1_ref, w3_ref, w2_ref, out_ref, dy_ref, branch_ref, gain_grad_ref, grads_ref,
    acc, dn,
):
    t = pl.program_id(0)

    @pl.when(t == 0)
    def _():
        acc[...] = y_ref[...]
        dn[...] = jnp.zeros_like(dn)

    w1, w3, w2 = merged(w1_ref), merged(w3_ref), merged(w2_ref)
    nn, og = n_ref[...], og_ref[...]
    u1, u3 = dot32(nn, w1), dot32(nn, w3)
    sg = jax.nn.sigmoid(u1)
    act = u1 * sg
    hd = (act * u3).astype(BF16)
    acc[...] += dot32(hd, w2, NT)
    dh = dot32(og, w2)
    d1 = (dh * u3 * (sg * (1.0 + u1 * (1.0 - sg)))).astype(BF16)
    d3 = (dh * act).astype(BF16)
    dn[...] += dot32(d1, w1, NT) + dot32(d3, w3, NT)
    depth = grads_ref.shape[3]
    for k, (a, b) in enumerate(((nn, d1), (nn, d3), (og, hd))):
        grads_ref[:, 0, k] = dot32(a, b, TN).astype(BF16).reshape(-1, depth, b.shape[1])

    @pl.when(t == pl.num_programs(0) - 1)
    def _():
        out_ref[...] = acc[...].astype(BF16)
        y = y_ref[...]
        rr = lax.rsqrt(jnp.mean(y * y, axis=1, keepdims=True) + EPSILON)
        nh = y * rr
        g = dn[...]
        gain_grad_ref[...] = jnp.sum(nh * g, axis=0, keepdims=True)
        scaled = g * gain_ref[...]
        dy = og.astype(F32) + rr * (scaled - nh * jnp.mean(nh * scaled, axis=1, keepdims=True))
        dy_ref[...] = dy
        branch_ref[...] = dy.astype(BF16)


def attend_back_kernel(
    halo, br_ref, p_ref, h_ref, m_ref, q_ref, k_ref, vp_ref, v_ref, gp_ref, o_ref, g_ref, wv_ref, wg_ref, wo_ref,
    dq_ref, dkn_ref, dk_ref, dhn_ref, dh_ref, dm_ref, grads_ref, dp, dhv, pb_ref,
):
    t = pl.program_id(0)

    @pl.when(t == 0)
    def _():
        pb_ref[...] = p_ref[...].astype(BF16)
        dp[...] = jnp.zeros_like(dp)
        dhv[...] = jnp.zeros_like(dhv)
        dm_ref[...] = jnp.zeros_like(dm_ref)

    branch, pb = br_ref[...], pb_ref[...]
    dg = dot32(branch, merged(wo_ref))
    gp = gp_ref[...].astype(F32)
    sg = jax.nn.sigmoid(gp)
    da = (dg * (gp * sg)).astype(BF16)
    dr = (dg * o_ref[...].astype(F32) * (sg * (1.0 + gp * (1.0 - sg)))).astype(BF16)
    dp[...] += dot32(da, v_ref[...], NT)
    dv = dot32(pb, da, TN)
    dvp = (dv * silu_slope(vp_ref[...].astype(F32))).astype(BF16)
    dhv[...] += dot32(dvp, merged(wv_ref), NT)
    dm_ref[...] += dot32(dr, merged(wg_ref), NT)
    depth = grads_ref.shape[3]
    for k, (a, b) in enumerate(((h_ref[...], dvp), (m_ref[...], dr), (branch, g_ref[...]))):
        grads_ref[:, 0, k] = dot32(a, b, TN).astype(BF16).reshape(-1, depth, b.shape[1])

    @pl.when(t == pl.num_programs(0) - 1)
    def _():
        scale = 1.0 / math.sqrt(q_ref.shape[1])
        p = p_ref[...]
        d = dp[...]
        ds = (p * (d - jnp.sum(p * d, axis=1, keepdims=True))).astype(BF16)
        dq_ref[...] = dot32(ds, k_ref[...]) * scale
        dk = dot32(ds, q_ref[...], TN) * scale
        dkn_ref[...] = dk[:halo].astype(BF16)
        dk_ref[...] = dk[halo:]
        dhn_ref[...] = dhv[:halo, :].astype(BF16)
        dh_ref[...] = dhv[halo:, :]


def stage_call(body, steps, ins, outs, scratch, name, flops):
    def spec(v, how):
        if how == "all":
            return pl.BlockSpec(v.shape, lambda t: (0,) * v.ndim)
        if how == "col":
            return pl.BlockSpec((v.shape[0], v.shape[1] // steps), lambda t: (0, t))
        return how

    outs = [(jax.ShapeDtypeStruct(s, d), how) for s, d, how in outs]
    return pl.pallas_call(
        body,
        grid=(steps,),
        in_specs=[spec(v, how) for v, how in ins],
        out_specs=[spec(v, how) for v, how in outs],
        out_shape=[v for v, _ in outs],
        scratch_shapes=scratch,
        compiler_params=pltpu.CompilerParams(vmem_limit_bytes=60 << 20),
        cost_estimate=pl.CostEstimate(flops=flops, bytes_accessed=48 << 20, transcendentals=0),
        name=name,
    )(*[v for v, _ in ins])


def small_sums_kernel(bits, small_ref, block_ref, out_ref, own_ref, acc, cube, buf, cbuf, sems):
    d, t = lax.axis_index("dp"), lax.axis_index("tensor")

    def mine(axis, k):
        return ((d if axis == "dp" else t) // (1 << k)) % 2

    def partner(axis, k):
        step = (1 - 2 * mine(axis, k)) * (1 << k)
        return (d + step, t) if axis == "dp" else (d, t + step)

    barrier = pltpu.get_barrier_semaphore()
    for bit in bits:
        pl.semaphore_signal(barrier, inc=1, device_id=partner(*bit), device_id_type=pl.DeviceIdType.MESH)
    pl.semaphore_wait(barrier, len(bits))

    def send(n, which, src, dst, bit):
        copy = pltpu.make_async_remote_copy(
            src_ref=src, dst_ref=dst, send_sem=sems.at[0, which, n], recv_sem=sems.at[1, which, n],
            device_id=partner(*bit), device_id_type=pl.DeviceIdType.MESH,
        )
        copy.start()
        return copy

    acc[...] = small_ref[...]
    cube[...] = block_ref[...]
    start, length, cstart, clength = 0, acc.shape[0], 0, cube.shape[0]
    at, cat = 0, 0
    trail = []
    for n, bit in enumerate(bits):
        axis, k = bit
        half = length // 2
        keep = pl.multiple_of(start + mine(axis, k) * half, 8)
        give = pl.multiple_of(start + (1 - mine(axis, k)) * half, 8)
        copies = [send(n, 0, acc.at[pl.ds(give, half)], buf.at[pl.ds(at, half)], bit)]
        if axis == "dp":
            chalf = clength // 2
            ckeep = pl.multiple_of(cstart + mine(axis, k) * chalf, 8)
            cgive = pl.multiple_of(cstart + (1 - mine(axis, k)) * chalf, 8)
        else:
            chalf, ckeep, cgive = clength, cstart, cstart
        copies.append(send(n, 1, cube.at[pl.ds(cgive, chalf)], cbuf.at[pl.ds(cat, chalf)], bit))
        for copy in copies:
            copy.wait()
        acc[pl.ds(keep, half)] += buf[pl.ds(at, half)]
        cube[pl.ds(ckeep, chalf)] += cbuf[pl.ds(cat, chalf)]
        trail.append((start, length))
        start, length, cstart, clength = keep, half, ckeep, chalf
        at, cat = at + half, cat + chalf
    own_ref[...] = cube[pl.ds(cstart, clength)]
    out_ref[pl.ds(start, length)] = acc[pl.ds(start, length)]
    for n, bit in reversed(list(enumerate(bits))):
        copy = send(n, 2, out_ref.at[pl.ds(start, length)], out_ref.at[pl.ds(start, length)], bit)
        copy.wait()
        start, length = trail[n]


def small_sums_call(small, block, replicas, parts):
    bits = [("dp", k) for k in range(replicas.bit_length() - 1)]
    bits += [("tensor", k) for k in range(parts.bit_length() - 1)]
    own = block.shape[0] // replicas
    got = sum(block.shape[0] >> (k + 1) for k in range(replicas.bit_length() - 1))
    got += own * (parts.bit_length() - 1)
    vmem = pl.BlockSpec(memory_space=pltpu.VMEM)
    return pl.pallas_call(
        functools.partial(small_sums_kernel, bits),
        in_specs=[vmem, vmem],
        out_specs=[vmem, vmem],
        out_shape=[jax.ShapeDtypeStruct(small.shape, F32), jax.ShapeDtypeStruct((own, block.shape[1]), F32)],
        scratch_shapes=[
            pltpu.VMEM(small.shape, F32), pltpu.VMEM(block.shape, F32), pltpu.VMEM(small.shape, F32),
            pltpu.VMEM((got, block.shape[1]), F32), pltpu.SemaphoreType.DMA((2, 3, len(bits))),
        ],
        compiler_params=pltpu.CompilerParams(collective_id=0, has_side_effects=True, vmem_limit_bytes=24 << 20),
        name="small_sums",
    )(small, block)


def on_device(
    block_in, segments, norm_gain, ema_rate, ema_angle, ema_input, ema_output, ema_skip, w_shared, query_gain,
    query_bias, key_gain, w_value, w_gate, w_out, ffn_gain, w_swish, w_up, w_down, out_grad,
):
    parts = lax.axis_size("tensor")
    replicas = lax.axis_size("dp")
    rank = lax.axis_index("tensor")
    rows, width = block_in.shape
    dims = ema_rate.shape[0]
    length = segments.shape[1]
    groups = TN_GROUPS
    span = width // groups
    latent_width = w_shared.shape[1]
    value_width = w_value.shape[1] * parts
    ffn_width = w_swish.shape[1] * parts
    depth = w_value.shape[0]
    halo = -(-REACH // LANES) * LANES
    hops = [min(rows, halo - h * rows) for h in range(-(-halo // rows))]

    def from_earlier(x, hop):
        return lax.ppermute(x, "tensor", [(i, i + hop) for i in range(parts - hop)])

    def from_later(x, hop):
        return lax.ppermute(x, "tensor", [(i + hop, i) for i in range(parts - hop)])

    def halo_of(x):
        pieces = [from_earlier(x[rows - n :], h + 1) for h, n in enumerate(hops)]
        return jnp.concatenate(pieces[::-1] + [x], axis=0)

    def give_back(total, x):
        end = halo
        for h, n in enumerate(hops):
            got = from_later(x[end - n : end], h + 1).astype(F32)
            total = total.at[rows - n :].add(got)
            end -= n
        return total

    piece = depth // parts
    shared_piece = lax.dynamic_slice_in_dim(w_shared, rank * piece, piece, 0)
    low = lambda w: w.astype(BF16)
    vw, fw = value_width // parts, ffn_width // parts
    pack_a = jnp.concatenate(
        [low(w_value), low(w_gate), low(w_out.T), low(shared_piece).reshape(-1, vw)], axis=0
    )
    pack_f = jnp.concatenate([low(w_swish), low(w_up), low(w_down.T)], axis=0)
    all_a = lax.all_gather(pack_a, BOTH, axis=0)
    all_a = all_a.reshape(replicas, parts, -1, vw)
    pack_f = with_layout_constraint(pack_f, Layout((0, 1)))
    all_f = lax.all_gather(pack_f, BOTH, axis=0).reshape(replicas, parts, 3 * depth, fw)
    shared_b = all_a[:, :, 3 * depth :].reshape(width, latent_width)

    def part(k, columns):
        return pl.BlockSpec((replicas, 1, depth, columns), lambda t: (0, t, k, 0))

    seg_all = segments[0]
    padded = jnp.concatenate([jnp.full((halo,), -1, jnp.int32), seg_all, jnp.full((halo,), -2, jnp.int32)])
    near = lax.dynamic_slice_in_dim(padded, rank * rows, halo + rows + halo, 0)
    seg_keys = near[: halo + rows]
    seg = near[halo : halo + rows]
    before = near[halo - 1]
    masks = row_masks(seg, before)
    index = rank * rows + jnp.arange(rows, dtype=jnp.int32)
    start = jnp.sum((seg_all[None, :] < seg[:, None]).astype(jnp.int32), axis=1)
    count = (index - start + 1).astype(F32)[:, None] * span
    tri = jnp.arange(rows)
    same = seg[:, None] == seg[None, :]
    lower = (same & (tri[:, None] >= tri[None, :])).astype(F32)
    link1 = (seg[0] == before).astype(F32)
    link2 = (before == near[halo - rows - 1]).astype(F32)
    last = seg[-1]
    next1 = (near[halo + rows] == last).astype(F32)
    next2 = ((near[halo + 2 * rows - 1] == last) & (near[halo + 2 * rows] == last)).astype(F32) if halo > rows else 0.0
    heads = (seg == before).astype(F32)[:, None]
    tails = (seg == last).astype(F32)[:, None]

    x = block_in.astype(F32)
    gather = (jnp.arange(width)[:, None] // span == jnp.arange(groups)[None, :]).astype(F32)
    sums_of = lambda v: dot32(v, gather, precision=HIGHEST)
    spread_of = lambda v: dot32(v, gather, NT, precision=HIGHEST)
    sums = jnp.concatenate([dot32(block_in, gather.astype(BF16)), sums_of(x * x)], axis=1)
    running = dot32(lower, sums, precision=HIGHEST)
    tail = running[-1:]
    carry = from_earlier(tail, 1) + link2 * from_earlier(tail, 2)
    running = running + heads * carry
    mean = running[:, :groups] / count
    var = running[:, groups:] / count - mean * mean
    rho = lax.rsqrt(var + EPSILON)
    mean_full, rho_full = spread_of(mean), spread_of(rho)
    centred = (x - mean_full) * rho_full
    hidden = centred * norm_gain
    hidden_b = low(hidden)

    size = jnp.exp(-ema_rate)
    unit = jnp.concatenate([size * jnp.cos(ema_angle), size * jnp.sin(ema_angle)])
    root = jnp.sqrt(1.0 - size * size)
    feed = ema_input * root
    reads = ema_output.reshape(2 * dims, width)
    skip = ema_skip[None]
    gcount = rows // (8 * STEP)
    nstate = gcount * dims * 2
    at_rows = gcount * STEP
    state_shape = (jax.ShapeDtypeStruct((nstate, 8, width), F32), col3(nstate, 8))
    edge_shape = (jax.ShapeDtypeStruct((2 * dims, width), F32), col(2 * dims))
    dim_shape = (jax.ShapeDtypeStruct((dims, width), F32), col(dims))
    rows_shape = (jax.ShapeDtypeStruct((rows, width), F32), col(rows))
    mask_spec = whole(at_rows, 8, LANES)
    cont, mk, mkr = (
        (masks["cont"], whole(gcount, 8, LANES)), (masks["mk"], whole(3, 8, LANES)), (masks["mkr"], whole(3, 8, LANES))
    )
    kend, keep0, seg8 = ((masks[k], mask_spec) for k in ("kend", "keep0", "seg"))
    pair, single = col(2 * dims), col(dims)
    vm = lambda n: pltpu.VMEM((n, 8, LANES), F32)
    flat_vm = lambda *n: pltpu.VMEM((*n, LANES), F32)
    table_vm, scale_vm = flat_vm(2, STEP * dims), flat_vm(8 * dims)
    mac = rows * width * dims * 4
    entering, end, turn = ema_call(
        ema_enter, rows, dims, width,
        [(hidden, col(rows)), kend, (unit, pair), (feed, single), cont, mk],
        [state_shape, edge_shape, edge_shape], [vm(at_rows), table_vm, scale_vm], "ema_enter", mac,
    )

    def turned(v, sign):
        r, i = times(turn[:dims], sign * turn[dims:], v[:dims], v[dims:])
        return jnp.concatenate([r, i])

    state_in = from_earlier(end, 1) + link2 * turned(from_earlier(end, 2), 1.0)
    ema_out, mixed, states = ema_call(
        ema_read, rows, dims, width,
        [(hidden, col(rows)), seg8, keep0, (unit, pair), (feed, single), (reads, pair), cont, mk,
         (entering, col3(nstate, 8)), (state_in, pair), (skip, col(1))],
        [rows_shape, (jax.ShapeDtypeStruct((rows, width), BF16), col(rows)), state_shape],
        [vm(2 * at_rows), table_vm, scale_vm], "ema_read", mac,
    )

    hidden_near = halo_of(hidden_b)
    near_rows = halo + rows
    latent = dot32(mixed, shared_b)
    queries = low(latent * query_gain + query_bias)
    keys_near = halo_of(low(latent * key_gain))
    one = lambda v: v[None]
    matmul = rows * width * vw * 2 * parts
    col_v = lambda n: ((n, value_width), BF16, "col")
    probs, value_pre, values, gate_pre, attended, gated, residual, norm_in = stage_call(
        functools.partial(attend_kernel, halo), parts,
        [(queries, "all"), (keys_near, "all"), (seg[:, None], "all"), (one(seg_keys), "all"), (hidden_near, "all"),
         (mixed, "all"), (block_in, "all"), (one(ffn_gain), "all"), (all_a, part(0, vw)), (all_a, part(1, vw)),
         (all_a, part(2, vw))],
        [((rows, near_rows), F32, "all"), col_v(near_rows), col_v(near_rows), col_v(rows), col_v(rows), col_v(rows),
         ((rows, width), F32, "all"), ((rows, width), BF16, "all")],
        [pltpu.VMEM((rows, near_rows), BF16)], "attend", 6 * matmul,
    )

    row_vm = lambda n: pltpu.VMEM((n, width), F32)
    block_out, grad_residual, branch, grad_ffn_gain, ffn_grads = stage_call(
        ffn_kernel, parts,
        [(residual, "all"), (norm_in, "all"), (out_grad, "all"), (one(ffn_gain), "all"), (all_f, part(0, fw)),
         (all_f, part(1, fw)), (all_f, part(2, fw))],
        [((rows, width), BF16, "all"), ((rows, width), F32, "all"), ((rows, width), BF16, "all"),
         ((1, width), F32, "all"),
         ((replicas, parts, 3, depth, fw), BF16,
          pl.BlockSpec((replicas, 1, 3, depth, fw), lambda t: (0, t, 0, 0, 0)))],
        [row_vm(rows), row_vm(rows)], "ffn", 11 * matmul,
    )

    def summed(g):
        g = g.reshape(replicas, parts, -1, g.shape[-1])
        g = lax.psum_scatter(g, "dp", scatter_dimension=0, tiled=False)
        return lax.psum_scatter(g, "tensor", scatter_dimension=0, tiled=False).astype(F32)

    ffn_sum = summed(ffn_grads)

    grad_queries, keys_back, keys_own, hidden_back, hidden_own, grad_mixed, attn_grads = stage_call(
        functools.partial(attend_back_kernel, halo), parts,
        [(branch, "all"), (probs, "all"), (hidden_near, "all"), (mixed, "all"), (queries, "all"), (keys_near, "all"),
         (value_pre, "col"), (values, "col"), (gate_pre, "col"), (attended, "col"), (gated, "col"),
         (all_a, part(0, vw)), (all_a, part(1, vw)), (all_a, part(2, vw))],
        [((rows, latent_width), F32, "all"), ((halo, latent_width), BF16, "all"), ((rows, latent_width), F32, "all"),
         ((halo, width), BF16, "all"), ((rows, width), F32, "all"), ((rows, width), F32, "all"),
         ((replicas, parts, 3, depth, vw), BF16,
          pl.BlockSpec((replicas, 1, 3, depth, vw), lambda t: (0, t, 0, 0, 0)))],
        [pltpu.VMEM((rows, near_rows), F32), row_vm(near_rows), pltpu.VMEM((rows, near_rows), BF16)], "attend_back", 12 * matmul,
    )
    grad_keys = give_back(keys_own, keys_back)
    grad_hidden = give_back(hidden_own, hidden_back)
    grad_query_gain = jnp.sum(latent * grad_queries, axis=0)
    grad_query_bias = jnp.sum(grad_queries, axis=0)
    grad_key_gain = jnp.sum(latent * grad_keys, axis=0)
    grad_latent = low(grad_queries * query_gain + grad_keys * key_gain)
    grad_shared = dot32(mixed, grad_latent, TN)
    attn_sum = summed(attn_grads)
    grad_ema = (dot32(grad_latent, shared_b, NT) + grad_mixed) * silu_slope(ema_out)

    pulls, head = ema_call(
        ema_leave, rows, dims, width,
        [(grad_ema, col(rows)), keep0, (unit, pair), (reads, pair), cont, mkr],
        [state_shape, edge_shape], [vm(at_rows), table_vm, scale_vm], "ema_leave", mac,
    )
    cross = (near[halo + 2 * rows - 1] == last).astype(F32)
    pull_in = from_later(head, 1) + cross * turned(from_later(head, 2), -1.0)
    grad_hidden_ema, output_grad, input_grad, rate_grad, angle_grad, grad_skip = ema_call(
        ema_grads, rows, dims, width,
        [(hidden, col(rows)), (grad_ema, col(rows)), seg8, kend, (masks["rk0"], whole(rows, LANES)),
         (masks["rkend"], whole(rows, LANES)), (unit, pair), (feed, single), (reads, pair), (root, single),
         (ema_input, single), cont, mkr, (pulls, col3(nstate, 8)), (pull_in, pair), (states, col3(nstate, 8)),
         (skip, col(1))],
        [rows_shape, edge_shape, dim_shape, dim_shape, dim_shape, (jax.ShapeDtypeStruct((1, width), F32), col(1))],
        [vm(2 * at_rows), vm(at_rows), vm(nstate), table_vm, scale_vm, flat_vm(4, STEP * dims), flat_vm(9, dims),
         flat_vm(rows), flat_vm(rows)], "ema_grads", 3 * mac,
    )

    grad_hidden = grad_hidden + grad_hidden_ema
    gain_grad = jnp.sum(centred * grad_hidden, axis=0)
    spread_grad = grad_hidden * norm_gain
    sum_a = rho * sums_of(spread_grad)
    sum_b = sums_of(spread_grad * (x - mean_full))
    cube = sum_b * rho * rho * rho
    push = jnp.concatenate([(cube * mean - sum_a) / count, -cube / (2.0 * count)], axis=1)
    backed = dot32(lower, push, TN, precision=HIGHEST)
    first = backed[:1]
    carry = next1 * from_later(first, 1) + next2 * from_later(first, 2)
    backed = backed + tails * carry
    grad_x = spread_grad * rho_full + spread_of(backed[:, :groups]) + 2.0 * x * spread_of(backed[:, groups:])
    in_grad = grad_residual + grad_x

    small = [gain_grad, rate_grad, angle_grad, input_grad, output_grad, grad_skip, grad_query_gain,
             grad_query_bias, grad_key_gain, grad_ffn_gain]
    sizes = [v.size for v in small]
    total = sum(sizes)
    members = parts * replicas
    unit = members * 8 * LANES
    packed = jnp.concatenate([v.reshape(-1) for v in small] + [jnp.zeros((-total % unit,), F32)])
    packed = packed.reshape(-1, LANES)
    levels = replicas.bit_length() - 1
    mirror = lambda v: v.transpose(tuple(reversed(range(levels))) + (levels, levels + 1))
    block = mirror(grad_shared.reshape((2,) * levels + (depth, latent_width)))
    packed, shared_sum = small_sums_call(packed, block.reshape(width, latent_width), replicas, parts)
    packed = packed.reshape(-1)
    small_sums, at = [], 0
    for n in sizes:
        small_sums.append(packed[at : at + n])
        at += n
    shape = lambda k, like: small_sums[k].reshape(like.shape)

    cut = lambda g, k: g[k * depth : (k + 1) * depth]
    return (
        block_out, in_grad, shape(0, norm_gain), shape(1, ema_rate), shape(2, ema_angle), shape(3, ema_input),
        shape(4, ema_output), shape(5, ema_skip), shared_sum, shape(6, query_gain), shape(7, query_bias),
        shape(8, key_gain), cut(attn_sum, 0), cut(attn_sum, 1), cut(attn_sum, 2).T, shape(9, ffn_gain),
        cut(ffn_sum, 0), cut(ffn_sum, 1), cut(ffn_sum, 2).T,
    )


def solution(mesh):
    rows, dp, copy = P(BOTH, None), P("dp", None), P()
    wide, tall = P("dp", "tensor"), P("tensor", "dp")
    return jax.shard_map(
        on_device,
        mesh=mesh,
        in_specs=(
            rows, dp, copy, copy, copy, copy, copy, copy, dp, copy, copy, copy, wide, wide, tall, copy, wide, wide,
            tall, rows,
        ),
        out_specs=(
            rows, rows, copy, copy, copy, copy, copy, copy, dp, copy, copy, copy, wide, wide, tall, copy, wide, wide,
            tall,
        ),
        check_vma=False,
    )
```

```python
import functools
import math

import jax
import jax.numpy as jnp
from jax import lax
from jax.experimental import pallas as pl
from jax.experimental.pallas import tpu as pltpu
from jax.experimental.layout import Layout, with_layout_constraint
from jax.sharding import PartitionSpec as P

TN_GROUPS = 16
EPSILON = 1e-05
REACH = 800
STEP = 16
LANES = 128
F32 = jnp.float32
BF16 = jnp.bfloat16
HIGHEST = lax.Precision.HIGHEST
BOTH = ("dp", "tensor")


def dot32(a, b, dims=((1,), (0,)), precision=None):
    return lax.dot_general(a, b, (dims, ((), ())), precision=precision, preferred_element_type=F32)


NT = ((1,), (1,))
TN = ((0,), (0,))


def silu_of(v):
    return v * jax.nn.sigmoid(v)


def silu_slope(v):
    sg = jax.nn.sigmoid(v)
    return sg * (1.0 + v * (1.0 - sg))


def broadcast_row(ref, row):
    return ref[pl.ds(row, 8, stride=0), :]


def rotate(x, shift):
    return pltpu.roll(x, shift % 8, axis=0)


def times(ar, ai, br, bi):
    return ar * br - ai * bi, ar * bi + ai * br


def power_list(dims, q_ref):
    qr, qi = q_ref[:dims], q_ref[dims:]
    out = [(jnp.ones_like(qr), jnp.zeros_like(qr))]
    for n in range(STEP):
        out.append(times(*out[-1], qr, qi))
    return out


def fill_scales(groups, dims, pw, qs):
    step = pw[STEP]
    qs[:dims], qs[dims : 2 * dims] = step
    turn = step
    for _ in range(groups - 1):
        turn = times(*turn, *step)
    for k in range(3):
        base = 2 * dims * (k + 1)
        qs[base : base + dims], qs[base + dims : base + 2 * dims] = turn
        turn = times(*turn, *turn)
    return turn


def fill_read(dims, pw, e_ref, ta):
    e0, e1 = e_ref[:dims], e_ref[dims:]
    for i in range(STEP):
        ta[0, i * dims : (i + 1) * dims], ta[1, i * dims : (i + 1) * dims] = times(e0, e1, *pw[i + 1])


def fill_feed(dims, pw, f_ref, tb):
    f = f_ref[...]
    for i in range(STEP):
        r, m = pw[STEP - 1 - i]
        tb[0, i * dims : (i + 1) * dims], tb[1, i * dims : (i + 1) * dims] = f * r, f * m


def tap_list(dims, pw, e_ref, f_ref):
    e0, e1, f = e_ref[:dims], e_ref[dims:], f_ref[...]
    out = []
    for d in range(STEP):
        row = jnp.sum(f * (e0 * pw[d][0] - e1 * pw[d][1]), axis=0, keepdims=True)
        out.append(jnp.broadcast_to(row, (8, LANES)))
    return out


def chunk_sums(groups, dims, table, source, out, sign):
    def pair(jp, carry):
        acc = [None] * groups
        for i in range(STEP):
            c = [broadcast_row(table.at[p], i * dims + jp * 2 + k) for k in range(2) for p in range(2)]
            for g in range(groups):
                h = source[g * STEP + i]
                terms = [v * h for v in c]
                acc[g] = terms if i == 0 else [u + v for u, v in zip(acc[g], terms)]
        for g in range(groups):
            for k in range(2):
                at = (g * dims + jp * 2 + k) * 2
                out[at] = acc[g][2 * k]
                out[at + 1] = acc[g][2 * k + 1] if sign > 0 else -acc[g][2 * k + 1]
        return carry

    lax.fori_loop(0, dims // 2, pair, 0)


def position_sums(groups, dims, table, states, mask, out, base, sign):
    block = 4

    def some(iq, carry):
        acc = [[None] * block for _ in range(groups)]
        for j in range(dims):
            here = [(states[(g * dims + j) * 2], states[(g * dims + j) * 2 + 1]) for g in range(groups)]
            for i in range(block):
                cr = broadcast_row(table.at[0], (iq * block + i) * dims + j)
                ci = broadcast_row(table.at[1], (iq * block + i) * dims + j)
                for g in range(groups):
                    u, v = cr * here[g][0], ci * here[g][1]
                    term = u - v if sign < 0 else u + v
                    acc[g][i] = term if j == 0 else acc[g][i] + term
        for g in range(groups):
            for i in range(block):
                at = g * STEP + iq * block + i
                out[base + at] = acc[g][i] * mask[at]
        return carry

    lax.fori_loop(0, STEP // block, some, 0)


def ema_enter(rows, dims, h_ref, kend_ref, q_ref, f_ref, cont_ref, mk_ref, l_ref, end_ref, turn_ref, hm, tb, qs):
    groups = rows // (8 * STEP)
    pw = power_list(dims, q_ref)
    turn_ref[:dims], turn_ref[dims:] = fill_scales(groups, dims, pw, qs)
    fill_feed(dims, pw, f_ref, tb)
    for at in range(groups * STEP):
        hm[at] = h_ref[pl.ds(at, 8, stride=groups * STEP), :] * kend_ref[at]
    chunk_sums(groups, dims, tb, hm, l_ref, 1)

    def one(j, carry):
        zero = jnp.zeros((8, LANES), F32)
        _, ends = scan_states(groups, dims, j, l_ref, qs, cont_ref, mk_ref, zero, zero)
        end_ref[pl.ds(j, 1), :] = ends[0][7:8]
        end_ref[pl.ds(dims + j, 1), :] = ends[1][7:8]
        return carry

    lax.fori_loop(0, dims, one, 0)


def scan_states(groups, dims, j, l_ref, qs, cont_ref, mk_ref, inr, ini):
    qr, qi = broadcast_row(qs, j), broadcast_row(qs, dims + j)
    part = [(l_ref[(g * dims + j) * 2], l_ref[(g * dims + j) * 2 + 1]) for g in range(groups)]

    def through(sr, si):
        starts = []
        for g in range(groups):
            starts.append((sr, si))
            keep = cont_ref[g]
            tr, ti = times(qr, qi, sr, si)
            sr, si = keep * tr + part[g][0], keep * ti + part[g][1]
        return starts, sr, si

    _, er, ei = through(inr, ini)
    for k in range(3):
        base = 2 * dims * (k + 1)
        wr, wi = broadcast_row(qs, base + j), broadcast_row(qs, base + dims + j)
        pr, pi = times(wr, wi, rotate(er, 1 << k), rotate(ei, 1 << k))
        keep = mk_ref[k]
        er, ei = er + keep * pr, ei + keep * pi
    first = lax.broadcasted_iota(jnp.int32, (8, LANES), 0) == 0
    starts, _, _ = through(jnp.where(first, inr, rotate(er, 1)), jnp.where(first, ini, rotate(ei, 1)))
    return starts, (er, ei)


def ema_read(
    rows, dims, h_ref, seg_ref, k0_ref, q_ref, f_ref, e_ref, cont_ref, mk_ref, l_ref, in_ref, skip_ref,
    out_ref, m_ref, s_ref, hs, ta, qs
):
    groups = rows // (8 * STEP)
    first = lax.broadcasted_iota(jnp.int32, (8, LANES), 0) == 0
    pw = power_list(dims, q_ref)
    fill_scales(groups, dims, pw, qs)
    fill_read(dims, pw, e_ref, ta)
    taps = tap_list(dims, pw, e_ref, f_ref)

    def one(j, carry):
        inr = jnp.where(first, broadcast_row(in_ref, j), 0.0)
        ini = jnp.where(first, broadcast_row(in_ref, dims + j), 0.0)
        starts, _ = scan_states(groups, dims, j, l_ref, qs, cont_ref, mk_ref, inr, ini)
        for g in range(groups):
            s_ref[(g * dims + j) * 2] = starts[g][0]
            s_ref[(g * dims + j) * 2 + 1] = starts[g][1]
        return carry

    lax.fori_loop(0, dims, one, 0)
    for at in range(groups * STEP):
        hs[at] = h_ref[pl.ds(at, 8, stride=groups * STEP), :]
    position_sums(groups, dims, ta, s_ref, k0_ref, hs, groups * STEP, -1)
    tap0 = taps[0] + jnp.broadcast_to(skip_ref[...], (8, LANES))
    for g in range(groups):
        for i in range(STEP):
            at = g * STEP + i
            seg = seg_ref[at]
            out = hs[groups * STEP + at] + tap0 * hs[at]
            for s in range(i):
                src = g * STEP + s
                out = out + taps[i - s] * jnp.where(seg_ref[src] == seg, hs[src], 0.0)
            out_ref[pl.ds(at, 8, stride=groups * STEP), :] = out
    m_ref[...] = silu_of(out_ref[...]).astype(m_ref.dtype)


def reverse_states(groups, dims, j, g_ref, qs, cont_ref, mkr_ref, inr, ini):
    qr, qi = broadcast_row(qs, j), broadcast_row(qs, dims + j)
    part = [(g_ref[(g * dims + j) * 2], g_ref[(g * dims + j) * 2 + 1]) for g in range(groups)]

    def through(yr, yi):
        ends = [None] * groups
        for g in reversed(range(groups)):
            ends[g] = (yr, yi)
            keep = cont_ref[g]
            tr, ti = qr * yr + qi * yi, qr * yi - qi * yr
            yr, yi = keep * tr + part[g][0], keep * ti + part[g][1]
        return ends, yr, yi

    _, fr, fi = through(inr, ini)
    for k in range(3):
        base = 2 * dims * (k + 1)
        wr, wi = broadcast_row(qs, base + j), broadcast_row(qs, base + dims + j)
        pr, pi = rotate(fr, -(1 << k)), rotate(fi, -(1 << k))
        keep = mkr_ref[k]
        fr, fi = fr + keep * (wr * pr + wi * pi), fi + keep * (wr * pi - wi * pr)
    last = lax.broadcasted_iota(jnp.int32, (8, LANES), 0) == 7
    ends, _, _ = through(jnp.where(last, inr, rotate(fr, -1)), jnp.where(last, ini, rotate(fi, -1)))
    return ends, (fr, fi)


def ema_leave(rows, dims, de_ref, k0_ref, q_ref, e_ref, cont_ref, mkr_ref, g_ref, head_ref, dm, ta, qs):
    groups = rows // (8 * STEP)
    pw = power_list(dims, q_ref)
    fill_scales(groups, dims, pw, qs)
    fill_read(dims, pw, e_ref, ta)
    for at in range(groups * STEP):
        dm[at] = de_ref[pl.ds(at, 8, stride=groups * STEP), :] * k0_ref[at]
    chunk_sums(groups, dims, ta, dm, g_ref, -1)

    def one(j, carry):
        zero = jnp.zeros((8, LANES), F32)
        _, heads = reverse_states(groups, dims, j, g_ref, qs, cont_ref, mkr_ref, zero, zero)
        head_ref[pl.ds(j, 1), :] = heads[0][0:1]
        head_ref[pl.ds(dims + j, 1), :] = heads[1][0:1]
        return carry

    lax.fori_loop(0, dims, one, 0)


REDUCE_PLAN = (
    (0, 1, False), (1, 2, False), (2, 1, False), (3, 2, False), (4, 1, False), (5, 2, False), (6, 1, False), (7, 0, True)
)


def ema_grads_reduce(parts, ins, outs, held, rows, dims, *refs):
    own = list(refs)
    pack_ref, sum_ref = own.pop(ins), own.pop(ins + outs)
    stages = reduce_stages(parts, pack_ref, sum_ref, *own[ins + outs + held :])
    step = pl.program_id(0)
    run_stages(stages, step, REDUCE_PLAN, False)
    ema_grads(rows, dims, *own[: ins + outs + held])
    run_stages(stages, step, REDUCE_PLAN, True)


def ema_grads(
    rows, dims, h_ref, de_ref, seg_ref, kend_ref, rk0_ref, rkend_ref, q_ref, f_ref, e_ref, root_ref, feed_ref, cont_ref,
    mkr_ref, g_ref, in_ref, s_ref, skip_ref, dh_ref, ge_ref, gf_ref, gr_ref, ga_ref, gs_ref, hs, ds, la, tb, qs, pf, red, hn, dn
):
    groups = rows // (8 * STEP)
    last = lax.broadcasted_iota(jnp.int32, (8, LANES), 0) == 7
    pw = power_list(dims, q_ref)
    fill_scales(groups, dims, pw, qs)
    fill_feed(dims, pw, f_ref, tb)
    taps = tap_list(dims, pw, e_ref, f_ref)
    for i in range(STEP):
        at = slice(i * dims, (i + 1) * dims)
        pf[0, at], pf[1, at] = pw[i + 1]
        pf[2, at], pf[3, at] = pw[STEP - 1 - i]

    def one(j, carry):
        inr = jnp.where(last, broadcast_row(in_ref, j), 0.0)
        ini = jnp.where(last, broadcast_row(in_ref, dims + j), 0.0)
        ends, _ = reverse_states(groups, dims, j, g_ref, qs, cont_ref, mkr_ref, inr, ini)
        qr = jnp.zeros((8, LANES), F32)
        qi = jnp.zeros((8, LANES), F32)
        for g in range(groups):
            yr, yi = ends[g]
            la[(g * dims + j) * 2] = yr
            la[(g * dims + j) * 2 + 1] = yi
            keep = cont_ref[g]
            sr, si = s_ref[(g * dims + j) * 2], s_ref[(g * dims + j) * 2 + 1]
            qr = qr + keep * (yr * sr + yi * si)
            qi = qi + keep * (yi * sr - yr * si)
        red[0, pl.ds(j, 1), :] = jnp.sum(qr, axis=0, keepdims=True)
        red[1, pl.ds(j, 1), :] = jnp.sum(qi, axis=0, keepdims=True)
        return carry

    lax.fori_loop(0, dims, one, 0)
    total = jnp.zeros((8, LANES), F32)
    for at in range(groups * STEP):
        h = h_ref[pl.ds(at, 8, stride=groups * STEP), :]
        d = de_ref[pl.ds(at, 8, stride=groups * STEP), :]
        hs[at] = h
        ds[at] = d
        total = total + h * d
    gs_ref[...] = jnp.sum(total, axis=0, keepdims=True)
    position_sums(groups, dims, tb, la, kend_ref, hs, groups * STEP, 1)
    tap0 = taps[0] + jnp.broadcast_to(skip_ref[...], (8, LANES))
    kacc = [jnp.zeros((8, LANES), F32) for _ in range(STEP)]
    kacc[0] = total
    for g in range(groups):
        for s in range(STEP):
            at = g * STEP + s
            seg = seg_ref[at]
            h = hs[at]
            out = hs[groups * STEP + at] + tap0 * ds[at]
            for t in range(s + 1, STEP):
                d = jnp.where(seg_ref[g * STEP + t] == seg, ds[g * STEP + t], 0.0)
                out = out + taps[t - s] * d
                kacc[t - s] = kacc[t - s] + h * d
            dh_ref[pl.ds(at, 8, stride=groups * STEP), :] = out

    hn[...] = h_ref[...] * rkend_ref[...]
    dn[...] = de_ref[...] * rk0_ref[...]
    width = 4
    place = (lax.broadcasted_iota(jnp.int32, (STEP, LANES), 0) + 1).astype(F32)

    def tables(jq, carry):
        def chunk(n, acc):
            sub, g = n // groups, n % groups
            d0, d1 = (dn[pl.ds(pl.multiple_of(n * STEP + 8 * p, 8), 8), :] for p in range(2))
            h0, h1 = (hn[pl.ds(pl.multiple_of(n * STEP + 8 * p, 8), 8), :] for p in range(2))
            out = []
            for k in range(width):
                at = (g * dims + jq * width + k) * 2
                sr, si = (s_ref[at + p, pl.ds(sub, 8, stride=0), :] for p in range(2))
                yr, yi = (la[at + p, pl.ds(sub, 8, stride=0), :] for p in range(2))
                a = acc[8 * k : 8 * k + 8]
                out += [a[0] + d0 * sr, a[1] + d1 * sr, a[2] - d0 * si, a[3] - d1 * si]
                out += [a[4] + h0 * yr, a[5] + h1 * yr, a[6] + h0 * yi, a[7] + h1 * yi]
            return tuple(out)

        acc = lax.fori_loop(0, 8 * groups, chunk, (jnp.zeros((8, LANES), F32),) * (8 * width))
        for k in range(width):
            j = jq * width + k
            ar, ai, br, bi = (
                jnp.concatenate([acc[8 * k + 2 * p], acc[8 * k + 2 * p + 1]], axis=0) for p in range(4)
            )
            pr, pi, wr, wi = (pf[p, pl.ds(j, STEP, stride=dims), :] for p in range(4))
            ur, ui = ar * pr + ai * pi, ai * pr - ar * pi
            vr, vi = br * wr + bi * wi, bi * wr - br * wi
            rest = STEP - place
            sums = (ur, ui, place * ur, place * ui, vr, rest * vr, rest * vi)
            for p, v in enumerate(sums):
                red[2 + p, pl.ds(j, 1), :] = jnp.sum(v, axis=0, keepdims=True)
        return carry

    lax.fori_loop(0, dims // width, tables, 0)
    e0, e1, f = e_ref[:dims], e_ref[dims:], f_ref[...]
    zero = jnp.zeros((dims, LANES), F32)
    tr, ti, ur, ui = zero, zero, zero, zero
    for d in range(STEP):
        tap = jnp.broadcast_to(jnp.sum(kacc[d], axis=0, keepdims=True), (dims, LANES))
        r, m = tap * pw[d][0], tap * pw[d][1]
        tr, ti = tr + r, ti - m
        if d > 0:
            ur, ui = ur + d * r, ui - d * m
    ge_ref[:dims] = red[2] + f * tr
    ge_ref[dims:] = red[3] + f * ti
    gf = red[6] + e0 * tr + e1 * ti
    xr, xi = red[4] + f * ur, red[5] + f * ui
    lr = e0 * xr + e1 * xi + f * red[7]
    li = e0 * xi - e1 * xr + f * red[8]
    zr, zi = pw[STEP]
    lr = lr + STEP * (red[0] * zr + red[1] * zi)
    li = li + STEP * (red[1] * zr - red[0] * zi)
    root = root_ref[...]
    gf_ref[...] = gf * root
    gr_ref[...] = gf * feed_ref[...] * (1.0 - root * root) / root - lr
    ga_ref[...] = li


def col(rows):
    return pl.BlockSpec((rows, LANES), lambda i: (0, i))


def col3(a, b):
    return pl.BlockSpec((a, b, LANES), lambda i: (0, 0, i))


def whole(*shape):
    return pl.BlockSpec(shape, lambda i: (0,) * len(shape))


def ema_call(body, rows, dims, width, ins, outs, scratch, name, flops, collective_id=None):
    specs = [s for _, s in ins]
    return pl.pallas_call(
        functools.partial(body, rows, dims),
        grid=(width // LANES,),
        in_specs=specs,
        out_specs=[s for _, s in outs],
        out_shape=[o for o, _ in outs],
        scratch_shapes=scratch,
        compiler_params=pltpu.CompilerParams(
            vmem_limit_bytes=60 << 20, collective_id=collective_id, has_side_effects=collective_id is not None
        ),
        cost_estimate=pl.CostEstimate(flops=flops // 1000, bytes_accessed=1024, transcendentals=0),
        name=name,
    )(*[a for a, _ in ins])


def spread(v):
    return jnp.broadcast_to(v[..., None], v.shape + (LANES,))


def row_masks(seg, before):
    rows = seg.shape[0]
    groups = rows // (8 * STEP)
    cube = seg.reshape(8, groups, STEP)
    chunk_last = cube[:, :, -1]
    prior = jnp.concatenate([before[None], chunk_last.reshape(-1)[:-1]]).reshape(8, groups)
    keep0 = (cube == prior[:, :, None]).astype(F32)
    kend = (cube == chunk_last[:, :, None]).astype(F32)
    order = lambda v: spread(v.transpose(1, 2, 0).reshape(groups * STEP, 8))
    cont = spread((chunk_last == prior).astype(F32).transpose(1, 0))
    ends = jnp.concatenate([before[None], chunk_last[:, -1]])
    sub = jnp.arange(8)
    ahead, behind = [], []
    for k in range(3):
        w = 1 << k
        a = jnp.take(ends, jnp.maximum(sub + 1 - w, 0))
        ahead.append(((ends[1:] == a) & (sub >= w)).astype(F32))
        b = jnp.take(ends, jnp.minimum(sub + w, 8))
        behind.append(((ends[:8] == b) & (sub + w <= 7)).astype(F32))
    return dict(
        seg=order(cube.astype(F32)), keep0=order(keep0), kend=order(kend), cont=cont,
        mk=spread(jnp.stack(ahead)), mkr=spread(jnp.stack(behind)),
        rk0=spread(keep0.reshape(rows)), rkend=spread(kend.reshape(rows)),
    )


def merged(ref):
    v = ref[...]
    return v.reshape(-1, v.shape[-1])


GATHER_PLAN = ((0, 2, False), (1, 1, False), (2, 1, False), (3, 1, False), (3, 0, True))


def attend_gather_kernel(halo, parts, ins, outs, *refs):
    own = list(refs)
    pack_ref, all_ref = own.pop(ins), own.pop(ins + outs)
    stages = gather_stages(parts, pack_ref, all_ref, *own[ins + outs + 1 :])
    step = pl.program_id(0)
    run_stages(stages, step, GATHER_PLAN, False)
    attend_kernel(halo, *own[: ins + outs + 1])
    run_stages(stages, step, GATHER_PLAN, True)


def attend_kernel(
    halo, q_ref, k_ref, seg_ref, segk_ref, h_ref, m_ref, x_ref, gain_ref, wv_ref, wg_ref, wo_ref,
    p_ref, vp_ref, v_ref, gp_ref, o_ref, g_ref, y_ref, n_ref, pb_ref,
):
    t = pl.program_id(0)

    @pl.when(t == 0)
    def _():
        rows, keys = pb_ref.shape
        scores = dot32(q_ref[...], k_ref[...], NT) * (1.0 / math.sqrt(q_ref.shape[1]))
        at_row = lax.broadcasted_iota(jnp.int32, (rows, keys), 0)
        at_key = lax.broadcasted_iota(jnp.int32, (rows, keys), 1)
        allowed = (at_key <= at_row + halo) & (segk_ref[...] == seg_ref[...])
        scores = jnp.where(allowed, scores, -1e30)
        raw = jnp.exp(scores - jnp.max(scores, axis=1, keepdims=True))
        p = raw / jnp.sum(raw, axis=1, keepdims=True)
        p_ref[...] = p
        pb_ref[...] = p.astype(BF16)
        y_ref[...] = x_ref[...].astype(F32)

    vp = dot32(h_ref[...], merged(wv_ref))
    v = silu_of(vp).astype(BF16)
    vp_ref[...] = vp.astype(BF16)
    v_ref[...] = v
    gp = dot32(m_ref[...], merged(wg_ref))
    gp_ref[...] = gp.astype(BF16)
    o = dot32(pb_ref[...], v)
    o_ref[...] = o.astype(BF16)
    g = (silu_of(gp) * o).astype(BF16)
    g_ref[...] = g
    y_ref[...] += dot32(g, merged(wo_ref), NT)

    @pl.when(t == pl.num_programs(0) - 1)
    def _():
        y = y_ref[...]
        rr = lax.rsqrt(jnp.mean(y * y, axis=1, keepdims=True) + EPSILON)
        n_ref[...] = (y * rr * gain_ref[...]).astype(BF16)


def ffn_kernel(
    y_ref, n_ref, og_ref, gain_ref, w1_ref, w3_ref, w2_ref, out_ref, dy_ref, branch_ref, gain_grad_ref, grads_ref,
    acc, dn,
):
    t = pl.program_id(0)

    @pl.when(t == 0)
    def _():
        acc[...] = y_ref[...]
        dn[...] = jnp.zeros_like(dn)

    w1, w3, w2 = merged(w1_ref), merged(w3_ref), merged(w2_ref)
    nn, og = n_ref[...], og_ref[...]
    u1, u3 = dot32(nn, w1), dot32(nn, w3)
    sg = jax.nn.sigmoid(u1)
    act = u1 * sg
    hd = (act * u3).astype(BF16)
    acc[...] += dot32(hd, w2, NT)
    dh = dot32(og, w2)
    d1 = (dh * u3 * (sg * (1.0 + u1 * (1.0 - sg)))).astype(BF16)
    d3 = (dh * act).astype(BF16)
    dn[...] += dot32(d1, w1, NT) + dot32(d3, w3, NT)
    depth = grads_ref.shape[3]
    for k, (a, b) in enumerate(((nn, d1), (nn, d3), (og, hd))):
        grads_ref[:, 0, k] = dot32(a, b, TN).astype(BF16).reshape(-1, depth, b.shape[1])

    @pl.when(t == pl.num_programs(0) - 1)
    def _():
        out_ref[...] = acc[...].astype(BF16)
        y = y_ref[...]
        rr = lax.rsqrt(jnp.mean(y * y, axis=1, keepdims=True) + EPSILON)
        nh = y * rr
        g = dn[...]
        gain_grad_ref[...] = jnp.sum(nh * g, axis=0, keepdims=True)
        scaled = g * gain_ref[...]
        dy = og.astype(F32) + rr * (scaled - nh * jnp.mean(nh * scaled, axis=1, keepdims=True))
        dy_ref[...] = dy
        branch_ref[...] = dy.astype(BF16)


def attend_back_kernel(
    halo, br_ref, p_ref, h_ref, m_ref, q_ref, k_ref, vp_ref, v_ref, gp_ref, o_ref, g_ref, wv_ref, wg_ref, wo_ref,
    dq_ref, dkn_ref, dk_ref, dhn_ref, dh_ref, dm_ref, grads_ref, dp, dhv, pb_ref,
):
    t = pl.program_id(0)

    @pl.when(t == 0)
    def _():
        pb_ref[...] = p_ref[...].astype(BF16)
        dp[...] = jnp.zeros_like(dp)
        dhv[...] = jnp.zeros_like(dhv)
        dm_ref[...] = jnp.zeros_like(dm_ref)

    branch, pb = br_ref[...], pb_ref[...]
    dg = dot32(branch, merged(wo_ref))
    gp = gp_ref[...].astype(F32)
    sg = jax.nn.sigmoid(gp)
    da = (dg * (gp * sg)).astype(BF16)
    dr = (dg * o_ref[...].astype(F32) * (sg * (1.0 + gp * (1.0 - sg)))).astype(BF16)
    dp[...] += dot32(da, v_ref[...], NT)
    dv = dot32(pb, da, TN)
    dvp = (dv * silu_slope(vp_ref[...].astype(F32))).astype(BF16)
    dhv[...] += dot32(dvp, merged(wv_ref), NT)
    dm_ref[...] += dot32(dr, merged(wg_ref), NT)
    depth = grads_ref.shape[3]
    for k, (a, b) in enumerate(((h_ref[...], dvp), (m_ref[...], dr), (branch, g_ref[...]))):
        grads_ref[:, 0, k] = dot32(a, b, TN).astype(BF16).reshape(-1, depth, b.shape[1])

    @pl.when(t == pl.num_programs(0) - 1)
    def _():
        scale = 1.0 / math.sqrt(q_ref.shape[1])
        p = p_ref[...]
        d = dp[...]
        ds = (p * (d - jnp.sum(p * d, axis=1, keepdims=True))).astype(BF16)
        dq_ref[...] = dot32(ds, k_ref[...]) * scale
        dk = dot32(ds, q_ref[...], TN) * scale
        dkn_ref[...] = dk[:halo].astype(BF16)
        dk_ref[...] = dk[halo:]
        dhn_ref[...] = dhv[:halo, :].astype(BF16)
        dh_ref[...] = dhv[halo:, :]


def stage_call(body, steps, ins, outs, scratch, name, flops, collective_id=None):
    def spec(v, how):
        if how == "all":
            return pl.BlockSpec(v.shape, lambda t: (0,) * v.ndim)
        if how == "col":
            return pl.BlockSpec((v.shape[0], v.shape[1] // steps), lambda t: (0, t))
        return how

    outs = [(jax.ShapeDtypeStruct(s, d), how) for s, d, how in outs]
    return pl.pallas_call(
        body,
        grid=(steps,),
        in_specs=[spec(v, how) for v, how in ins],
        out_specs=[spec(v, how) for v, how in outs],
        out_shape=[v for v, _ in outs],
        scratch_shapes=scratch,
        compiler_params=pltpu.CompilerParams(
            vmem_limit_bytes=60 << 20, collective_id=collective_id, has_side_effects=collective_id is not None
        ),
        cost_estimate=pl.CostEstimate(flops=flops // 1000, bytes_accessed=1024, transcendentals=0),
        name=name,
    )(*[v for v, _ in ins])


def gather_stages(parts, pack_ref, out_ref, sems, own_sem):
    d, z = lax.axis_index("dp"), lax.axis_index("tensor")
    total = pack_ref.shape[0]
    cut = total // 32 * 16
    upper, lower, full = pl.ds(0, cut), pl.ds(cut, total - cut), pl.ds(0, total)
    flip = lambda k: d + (1 - 2 * ((d // (1 << k)) % 2)) * (1 << k)
    core, first, second = flip(0), flip(1), flip(2)
    across = first + second - d
    MESH = pl.DeviceIdType.MESH

    LINE, TO_FIRST, TO_SECOND, UP, DOWN, C_OWN, C_FIRST, C_SECOND, C_UP, C_DOWN = range(10)

    def copy(kind, b, source, part, dp_to, z_to):
        here = out_ref.at[source, b, part]
        return pltpu.make_async_remote_copy(
            src_ref=here, dst_ref=here, send_sem=sems.at[0, kind, b], recv_sem=sems.at[1, kind, b],
            device_id=(dp_to, z_to), device_id_type=MESH,
        )

    def begin():
        mine = pltpu.make_async_copy(pack_ref, out_ref.at[d, z], own_sem)
        mine.start()
        barrier = pltpu.get_barrier_semaphore()
        for other in (core, first, second):
            pl.semaphore_signal(barrier, inc=1, device_id=(other, z), device_id_type=MESH)
        for step in (-1, 1):
            @pl.when((z + step >= 0) & (z + step < parts))
            def _():
                pl.semaphore_signal(barrier, inc=1, device_id=(d, z + step), device_id_type=MESH)
        pl.semaphore_wait(barrier, 3 + jnp.minimum(z, 1) + jnp.minimum(parts - 1 - z, 1))
        mine.wait()

    def spread_block(b):
        copy(TO_FIRST, b, d, full, first, z).start()
        copy(TO_SECOND, b, d, full, second, z).start()
        copy(C_OWN, b, d, full, core, z).start()

    def along(b, step):
        @pl.when((z + step >= 0) & (z + step < parts))
        def _():
            here = out_ref.at[d, b]
            pltpu.make_async_remote_copy(
                src_ref=here, dst_ref=here, send_sem=sems.at[0, LINE + (10 if step > 0 else 11), b],
                recv_sem=sems.at[1, LINE, b], device_id=(d, z + step), device_id_type=MESH,
            ).start()

    def relay(b):
        copy(TO_FIRST, b, first, full, first, z).wait_recv()
        copy(UP, b, first, upper, second, z).start()
        copy(C_FIRST, b, first, full, core, z).start()
        copy(TO_SECOND, b, second, full, second, z).wait_recv()
        copy(DOWN, b, second, lower, first, z).start()
        copy(C_SECOND, b, second, full, core, z).start()

    def corner(b):
        copy(UP, b, across, upper, second, z).wait_recv()
        copy(C_UP, b, across, upper, core, z).start()
        copy(DOWN, b, across, lower, first, z).wait_recv()
        copy(C_DOWN, b, across, lower, core, z).start()

    def at_distance(dist, action):
        for side in ((0,) if dist == 0 else (-1, 1)):
            b = z + side * dist
            @pl.when((b >= 0) & (b < parts))
            def _():
                action(b, side)

    def arrive(b, side):
        if side != 0:
            copy(LINE, b, d, full, d, z).wait_recv()
        if side <= 0:
            along(b, 1)
        if side >= 0:
            along(b, -1)
        spread_block(b)

    def finish():
        other_first, other_second = core + first - d, core + second - d
        for b in range(parts):
            for kind, source, part in ((C_OWN, core, full), (C_FIRST, other_first, full), (C_SECOND, other_second, full),
                                       (C_UP, core + across - d, upper), (C_DOWN, core + across - d, lower)):
                copy(kind, b, source, part, core, z).wait_recv()
            for kind, source, part in ((TO_FIRST, d, full), (TO_SECOND, d, full), (C_OWN, d, full), (UP, first, upper),
                                       (DOWN, second, lower), (C_FIRST, first, full), (C_SECOND, second, full),
                                       (C_UP, across, upper), (C_DOWN, across, lower)):
                copy(kind, b, source, part, core, z).wait_send()
            for step, slot in ((1, 10), (-1, 11)):
                @pl.when((z + step >= 0) & (z + step < parts) & (step * (z - b) >= 0))
                def _():
                    copy(slot, b, d, full, core, z).wait_send()

    stages = [begin]
    for dist in range(parts + 2):
        if dist < parts:
            stages.append(functools.partial(at_distance, dist, arrive))
        if 1 <= dist < parts + 1:
            stages.append(functools.partial(at_distance, dist - 1, lambda b, side: relay(b)))
        if dist >= 2:
            stages.append(functools.partial(at_distance, dist - 2, lambda b, side: corner(b)))
    return stages + [finish]


def gather_scratch(parts):
    return [pltpu.SemaphoreType.DMA((2, 12, parts)), pltpu.SemaphoreType.DMA]


def run_stages(stages, step, plan, late):
    at = 0
    for when, count, end in plan:
        here = stages[at : at + count] if count else stages[at:]
        at += len(here)
        if end == late:
            @pl.when(step == when)
            def _():
                for stage in here:
                    stage()


R_CORE, R_FIRST, R_FIRST2, R_SECOND, R_SECOND2, R_UP, R_DOWN, R_RIGHT, R_LEFT = range(9)


def reduce_scratch(parts, rows, columns):
    upper = rows // 32 * 16
    vm = lambda *n: pltpu.VMEM((*n, columns), BF16)
    return [
        vm(parts, 4, rows), vm(parts, 4, rows), vm(parts, 2, upper), vm(parts, 2, rows - upper), vm(parts, upper),
        vm(parts, rows - upper), vm(2, parts, rows), pltpu.SemaphoreType.DMA((2, 9, parts)),
        pltpu.SemaphoreType.DMA((parts,)),
    ]


def reduce_stages(parts, pack, out, acc, got_core, got_first, got_second, got_up, got_down, got_line, sems, load_sems):
    d, z = lax.axis_index("dp"), lax.axis_index("tensor")
    MESH = pl.DeviceIdType.MESH
    rows = acc.shape[2]
    cut = rows // 32 * 16
    upper, lower = pl.ds(0, cut), pl.ds(cut, rows - cut)
    me, core = d // 2, d % 2
    bit = lambda k: (me // (1 << k)) % 2
    first = me + (1 - 2 * bit(0))
    second = me + 2 * (1 - 2 * bit(1))
    across = first + second - me
    on = lambda p: 2 * p + core
    far = z // (parts // 2)
    near_end = z + far * (parts - 1 - 2 * z)

    def unit(s):
        t = (parts - 1 - s) + near_end * ((3, 0, 2, 1)[s] - (parts - 1 - s))
        return t + far * (parts - 1 - 2 * t)

    def copy(kind, t, src, dst, where):
        return pltpu.make_async_remote_copy(
            src_ref=src, dst_ref=dst, send_sem=sems.at[0, kind, t], recv_sem=sems.at[1, kind, t], device_id=where,
            device_id_type=MESH,
        )

    def copies(s):
        t = unit(s)
        to_first, to_second = (on(first), z), (on(second), z)
        table = {
            R_CORE: (pack.at[:, 1 - core, t], got_core.at[t], (2 * me + 1 - core, z)),
            R_FIRST: (acc.at[t, first, upper], got_first.at[t, 0], to_first),
            R_FIRST2: (acc.at[t, across, upper], got_first.at[t, 1], to_first),
            R_SECOND: (acc.at[t, second, lower], got_second.at[t, 0], to_second),
            R_SECOND2: (acc.at[t, across, lower], got_second.at[t, 1], to_second),
            R_UP: (acc.at[t, second, upper], got_up.at[t], to_second),
            R_DOWN: (acc.at[t, first, lower], got_down.at[t], to_first),
            R_RIGHT: (acc.at[t, me], got_line.at[0, t], (d, jnp.minimum(z + 1, parts - 1))),
            R_LEFT: (acc.at[t, me], got_line.at[1, t], (d, jnp.maximum(z - 1, 0))),
        }
        return lambda kind: copy(kind, t, *table[kind])

    def load(s):
        t = unit(s)
        return pltpu.make_async_copy(pack.at[:, core, t], acc.at[t], load_sems.at[t])

    def add(target, at, count, source):
        tile = 32 if count % 32 == 0 else 16

        def some(i, carry):
            here = pl.ds(pl.multiple_of(at + i * tile, 16), tile)
            there = pl.ds(pl.multiple_of(i * tile, 16), tile)
            target[here, :] = (target[here, :].astype(F32) + source[there, :].astype(F32)).astype(BF16)
            return carry

        lax.fori_loop(0, count // tile, some, 0)

    def begin():
        barrier = pltpu.get_barrier_semaphore()
        for where in ((2 * me + 1 - core, z), (on(first), z), (on(second), z)):
            pl.semaphore_signal(barrier, inc=1, device_id=where, device_id_type=MESH)
        for step in (-1, 1):
            @pl.when((z + step >= 0) & (z + step < parts))
            def _():
                pl.semaphore_signal(barrier, inc=1, device_id=(d, z + step), device_id_type=MESH)
        pl.semaphore_wait(barrier, 3 + jnp.minimum(z, 1) + jnp.minimum(parts - 1 - z, 1))
        for s in range(parts):
            load(s).start()
            copies(s)(R_CORE).start()

    def cores(s):
        t, c = unit(s), copies(s)
        load(s).wait()
        c(R_CORE).wait_recv()
        for p in (first, across, second, me):
            add(acc.at[t, p], 0, rows, got_core.at[t, p])
        for kind in (R_FIRST, R_FIRST2, R_SECOND, R_SECOND2):
            c(kind).start()

    def chips(s):
        t, c = unit(s), copies(s)
        for kind in (R_FIRST2, R_SECOND2, R_FIRST, R_SECOND):
            c(kind).wait_recv()
        add(acc.at[t, second], 0, cut, got_first.at[t, 1])
        c(R_UP).start()
        add(acc.at[t, first], cut, rows - cut, got_second.at[t, 1])
        c(R_DOWN).start()
        add(acc.at[t, me], 0, cut, got_first.at[t, 0])
        add(acc.at[t, me], cut, rows - cut, got_second.at[t, 0])

    def line(s):
        t, c = unit(s), copies(s)
        c(R_UP).wait_recv()
        add(acc.at[t, me], 0, cut, got_up.at[t])
        c(R_DOWN).wait_recv()
        add(acc.at[t, me], cut, rows - cut, got_down.at[t])

        @pl.when((z <= t) & (z > 0))
        def _():
            c(R_RIGHT).wait_recv()
            add(acc.at[t, me], 0, rows, got_line.at[0, t])

        @pl.when((z >= t) & (z < parts - 1))
        def _():
            c(R_LEFT).wait_recv()
            add(acc.at[t, me], 0, rows, got_line.at[1, t])

        @pl.when(z < t)
        def _():
            c(R_RIGHT).start()

        @pl.when(z > t)
        def _():
            c(R_LEFT).start()

    def finish():
        out[...] = acc[z, me].astype(F32)
        for s in range(parts):
            t, c = unit(s), copies(s)
            for kind in range(R_RIGHT):
                c(kind).wait_send()

            @pl.when(z < t)
            def _():
                c(R_RIGHT).wait_send()

            @pl.when(z > t)
            def _():
                c(R_LEFT).wait_send()

    stages = [begin]
    for s in range(parts + 2):
        if s < parts:
            stages.append(functools.partial(cores, s))
        if 1 <= s <= parts:
            stages.append(functools.partial(chips, s - 1))
        if s >= 2:
            stages.append(functools.partial(line, s - 2))
    return stages + [finish]


def small_sums_kernel(bits, small_ref, block_ref, out_ref, own_ref, acc, cube, buf, cbuf, sems):
    d, t = lax.axis_index("dp"), lax.axis_index("tensor")

    def mine(axis, k):
        return ((d if axis == "dp" else t) // (1 << k)) % 2

    def partner(axis, k):
        step = (1 - 2 * mine(axis, k)) * (1 << k)
        return (d + step, t) if axis == "dp" else (d, t + step)

    barrier = pltpu.get_barrier_semaphore()
    for bit in bits:
        pl.semaphore_signal(barrier, inc=1, device_id=partner(*bit), device_id_type=pl.DeviceIdType.MESH)
    pl.semaphore_wait(barrier, len(bits))

    def send(n, which, src, dst, bit):
        copy = pltpu.make_async_remote_copy(
            src_ref=src, dst_ref=dst, send_sem=sems.at[0, which, n], recv_sem=sems.at[1, which, n],
            device_id=partner(*bit), device_id_type=pl.DeviceIdType.MESH,
        )
        copy.start()
        return copy

    acc[...] = small_ref[...]
    cube[...] = block_ref[...]
    start, length, cstart, clength = 0, acc.shape[0], 0, cube.shape[0]
    at, cat = 0, 0
    trail = []
    for n, bit in enumerate(bits):
        axis, k = bit
        half = length // 2
        keep = pl.multiple_of(start + mine(axis, k) * half, 8)
        give = pl.multiple_of(start + (1 - mine(axis, k)) * half, 8)
        copies = [send(n, 0, acc.at[pl.ds(give, half)], buf.at[pl.ds(at, half)], bit)]
        if axis == "dp":
            chalf = clength // 2
            ckeep = pl.multiple_of(cstart + mine(axis, k) * chalf, 8)
            cgive = pl.multiple_of(cstart + (1 - mine(axis, k)) * chalf, 8)
        else:
            chalf, ckeep, cgive = clength, cstart, cstart
        copies.append(send(n, 1, cube.at[pl.ds(cgive, chalf)], cbuf.at[pl.ds(cat, chalf)], bit))
        for copy in copies:
            copy.wait()
        acc[pl.ds(keep, half)] += buf[pl.ds(at, half)]
        cube[pl.ds(ckeep, chalf)] += cbuf[pl.ds(cat, chalf)]
        trail.append((start, length))
        start, length, cstart, clength = keep, half, ckeep, chalf
        at, cat = at + half, cat + chalf
    own_ref[...] = cube[pl.ds(cstart, clength)]
    out_ref[pl.ds(start, length)] = acc[pl.ds(start, length)]
    for n, bit in reversed(list(enumerate(bits))):
        copy = send(n, 2, out_ref.at[pl.ds(start, length)], out_ref.at[pl.ds(start, length)], bit)
        copy.wait()
        start, length = trail[n]


def small_sums_call(small, block, replicas, parts):
    bits = [("dp", k) for k in range(replicas.bit_length() - 1)]
    bits += [("tensor", k) for k in range(parts.bit_length() - 1)]
    own = block.shape[0] // replicas
    got = sum(block.shape[0] >> (k + 1) for k in range(replicas.bit_length() - 1))
    got += own * (parts.bit_length() - 1)
    vmem = pl.BlockSpec(memory_space=pltpu.VMEM)
    return pl.pallas_call(
        functools.partial(small_sums_kernel, bits),
        in_specs=[vmem, vmem],
        out_specs=[vmem, vmem],
        out_shape=[jax.ShapeDtypeStruct(small.shape, F32), jax.ShapeDtypeStruct((own, block.shape[1]), F32)],
        scratch_shapes=[
            pltpu.VMEM(small.shape, F32), pltpu.VMEM(block.shape, F32), pltpu.VMEM(small.shape, F32),
            pltpu.VMEM((got, block.shape[1]), F32), pltpu.SemaphoreType.DMA((2, 3, len(bits))),
        ],
        compiler_params=pltpu.CompilerParams(collective_id=0, has_side_effects=True, vmem_limit_bytes=24 << 20),
        name="small_sums",
    )(small, block)


def on_device(
    block_in, segments, norm_gain, ema_rate, ema_angle, ema_input, ema_output, ema_skip, w_shared, query_gain,
    query_bias, key_gain, w_value, w_gate, w_out, ffn_gain, w_swish, w_up, w_down, out_grad,
):
    parts = lax.axis_size("tensor")
    replicas = lax.axis_size("dp")
    rank = lax.axis_index("tensor")
    rows, width = block_in.shape
    dims = ema_rate.shape[0]
    length = segments.shape[1]
    groups = TN_GROUPS
    span = width // groups
    latent_width = w_shared.shape[1]
    value_width = w_value.shape[1] * parts
    ffn_width = w_swish.shape[1] * parts
    depth = w_value.shape[0]
    halo = -(-REACH // LANES) * LANES
    hops = [min(rows, REACH - h * rows) for h in range(-(-REACH // rows))]

    def from_earlier(x, hop):
        return lax.ppermute(x, "tensor", [(i, i + hop) for i in range(parts - hop)])

    def from_later(x, hop):
        return lax.ppermute(x, "tensor", [(i + hop, i) for i in range(parts - hop)])

    def halo_of(x):
        pieces = [from_earlier(x[rows - n :], h + 1) for h, n in enumerate(hops)]
        ahead = jnp.zeros((halo - sum(hops), x.shape[1]), x.dtype)
        return jnp.concatenate([ahead] + pieces[::-1] + [x], axis=0)

    def give_back(total, x):
        end = halo
        for h, n in enumerate(hops):
            got = from_later(x[end - n : end], h + 1).astype(F32)
            total = total.at[rows - n :].add(got)
            end -= n
        return total

    chip_links = replicas == 8 and parts == 4

    piece = depth // parts
    shared_piece = lax.dynamic_slice_in_dim(w_shared, rank * piece, piece, 0)
    low = lambda w: w.astype(BF16)
    vw, fw = value_width // parts, ffn_width // parts
    pack_a = jnp.concatenate(
        [low(w_value), low(w_gate), low(w_out.T), low(shared_piece).reshape(-1, vw)], axis=0
    )
    pack_f = jnp.concatenate([low(w_swish), low(w_up), low(w_down.T)], axis=0)
    all_a = lax.all_gather(pack_a, BOTH, axis=0).reshape(replicas, parts, -1, vw)
    pack_f = with_layout_constraint(pack_f, Layout((0, 1)))
    shared_b = all_a[:, :, 3 * depth :].reshape(width, latent_width)

    def part(k, columns):
        return pl.BlockSpec((replicas, 1, depth, columns), lambda t: (0, t, k, 0))

    seg_all = segments[0]
    padded = jnp.concatenate([jnp.full((halo,), -1, jnp.int32), seg_all, jnp.full((halo,), -2, jnp.int32)])
    near = lax.dynamic_slice_in_dim(padded, rank * rows, halo + rows + halo, 0)
    seg_keys = near[: halo + rows]
    seg = near[halo : halo + rows]
    before = near[halo - 1]
    masks = row_masks(seg, before)
    index = rank * rows + jnp.arange(rows, dtype=jnp.int32)
    start = jnp.sum((seg_all[None, :] < seg[:, None]).astype(jnp.int32), axis=1)
    count = (index - start + 1).astype(F32)[:, None] * span
    tri = jnp.arange(rows)
    same = seg[:, None] == seg[None, :]
    lower = (same & (tri[:, None] >= tri[None, :])).astype(F32)
    link1 = (seg[0] == before).astype(F32)
    link2 = (before == near[halo - rows - 1]).astype(F32)
    last = seg[-1]
    next1 = (near[halo + rows] == last).astype(F32)
    next2 = ((near[halo + 2 * rows - 1] == last) & (near[halo + 2 * rows] == last)).astype(F32) if halo > rows else 0.0
    heads = (seg == before).astype(F32)[:, None]
    tails = (seg == last).astype(F32)[:, None]

    x = block_in.astype(F32)
    gather = (jnp.arange(width)[:, None] // span == jnp.arange(groups)[None, :]).astype(F32)
    sums_of = lambda v: dot32(v, gather, precision=HIGHEST)
    spread_of = lambda v: dot32(v, gather, NT, precision=HIGHEST)
    sums = jnp.concatenate([dot32(block_in, gather.astype(BF16)), sums_of(x * x)], axis=1)
    running = dot32(lower, sums, precision=HIGHEST)
    tail = running[-1:]
    carry = from_earlier(tail, 1) + link2 * from_earlier(tail, 2)
    running = running + heads * carry
    mean = running[:, :groups] / count
    var = running[:, groups:] / count - mean * mean
    rho = lax.rsqrt(var + EPSILON)
    mean_full, rho_full = spread_of(mean), spread_of(rho)
    centred = (x - mean_full) * rho_full
    hidden = centred * norm_gain
    hidden_b = low(hidden)

    size = jnp.exp(-ema_rate)
    unit = jnp.concatenate([size * jnp.cos(ema_angle), size * jnp.sin(ema_angle)])
    root = jnp.sqrt(1.0 - size * size)
    feed = ema_input * root
    reads = ema_output.reshape(2 * dims, width)
    skip = ema_skip[None]
    gcount = rows // (8 * STEP)
    nstate = gcount * dims * 2
    at_rows = gcount * STEP
    state_shape = (jax.ShapeDtypeStruct((nstate, 8, width), F32), col3(nstate, 8))
    edge_shape = (jax.ShapeDtypeStruct((2 * dims, width), F32), col(2 * dims))
    dim_shape = (jax.ShapeDtypeStruct((dims, width), F32), col(dims))
    rows_shape = (jax.ShapeDtypeStruct((rows, width), F32), col(rows))
    mask_spec = whole(at_rows, 8, LANES)
    cont, mk, mkr = (
        (masks["cont"], whole(gcount, 8, LANES)), (masks["mk"], whole(3, 8, LANES)), (masks["mkr"], whole(3, 8, LANES))
    )
    kend, keep0, seg8 = ((masks[k], mask_spec) for k in ("kend", "keep0", "seg"))
    pair, single = col(2 * dims), col(dims)
    vm = lambda n: pltpu.VMEM((n, 8, LANES), F32)
    flat_vm = lambda *n: pltpu.VMEM((*n, LANES), F32)
    table_vm, scale_vm = flat_vm(2, STEP * dims), flat_vm(8 * dims)
    mac = rows * width * dims * 4
    entering, end, turn = ema_call(
        ema_enter, rows, dims, width,
        [(hidden, col(rows)), kend, (unit, pair), (feed, single), cont, mk],
        [state_shape, edge_shape, edge_shape], [vm(at_rows), table_vm, scale_vm], "ema_enter", mac,
    )

    def turned(v, sign):
        r, i = times(turn[:dims], sign * turn[dims:], v[:dims], v[dims:])
        return jnp.concatenate([r, i])

    state_in = from_earlier(end, 1) + link2 * turned(from_earlier(end, 2), 1.0)
    ema_out, mixed, states = ema_call(
        ema_read, rows, dims, width,
        [(hidden, col(rows)), seg8, keep0, (unit, pair), (feed, single), (reads, pair), cont, mk,
         (entering, col3(nstate, 8)), (state_in, pair), (skip, col(1))],
        [rows_shape, (jax.ShapeDtypeStruct((rows, width), BF16), col(rows)), state_shape],
        [vm(2 * at_rows), table_vm, scale_vm], "ema_read", mac,
    )

    hidden_near = halo_of(lax.optimization_barrier((hidden_b, state_in))[0])
    near_rows = halo + rows
    latent = dot32(mixed, shared_b)
    queries = low(latent * query_gain + query_bias)
    keys_near = halo_of(low(latent * key_gain))
    one = lambda v: v[None]
    matmul = rows * width * vw * 2 * parts
    col_v = lambda n: ((n, value_width), BF16, "col")
    anywhere = pl.BlockSpec(memory_space=pl.ANY)
    ins = [(queries, "all"), (keys_near, "all"), (seg[:, None], "all"), (one(seg_keys), "all"), (hidden_near, "all"),
           (mixed, "all"), (block_in, "all"), (one(ffn_gain), "all"), (all_a, part(0, vw)), (all_a, part(1, vw)),
           (all_a, part(2, vw))]
    outs = [((rows, near_rows), F32, "all"), col_v(near_rows), col_v(near_rows), col_v(rows), col_v(rows), col_v(rows),
            ((rows, width), F32, "all"), ((rows, width), BF16, "all")]
    scratch = [pltpu.VMEM((rows, near_rows), BF16)]
    if chip_links:
        results = stage_call(
            functools.partial(attend_gather_kernel, halo, parts, len(ins), len(outs)), parts,
            ins + [(pack_f, anywhere)], outs + [((replicas, parts) + pack_f.shape, BF16, anywhere)],
            scratch + gather_scratch(parts), "attend", 6 * matmul, collective_id=1,
        )
        all_f = results[-1]
    else:
        results = stage_call(functools.partial(attend_kernel, halo), parts, ins, outs, scratch, "attend", 6 * matmul)
        all_f = lax.all_gather(pack_f, BOTH, axis=0).reshape(replicas, parts, 3 * depth, fw)
    probs, value_pre, values, gate_pre, attended, gated, residual, norm_in = results[:8]

    row_vm = lambda n: pltpu.VMEM((n, width), F32)
    block_out, grad_residual, branch, grad_ffn_gain, ffn_grads = stage_call(
        ffn_kernel, parts,
        [(residual, "all"), (norm_in, "all"), (out_grad, "all"), (one(ffn_gain), "all"), (all_f, part(0, fw)),
         (all_f, part(1, fw)), (all_f, part(2, fw))],
        [((rows, width), BF16, "all"), ((rows, width), F32, "all"), ((rows, width), BF16, "all"),
         ((1, width), F32, "all"),
         ((replicas, parts, 3, depth, fw), BF16,
          pl.BlockSpec((replicas, 1, 3, depth, fw), lambda t: (0, t, 0, 0, 0)))],
        [row_vm(rows), row_vm(rows)], "ffn", 11 * matmul,
    )

    def summed(g):
        g = g.reshape(replicas, parts, -1, g.shape[-1])
        return lax.psum_scatter(g, "dp", scatter_dimension=0, tiled=False)

    def summed_along(g, after):
        g = lax.optimization_barrier((g, after))[0]
        return lax.psum_scatter(g, "tensor", scatter_dimension=0, tiled=False).astype(F32)

    ffn_sum = summed(ffn_grads)

    grad_queries, keys_back, keys_own, hidden_back, hidden_own, grad_mixed, attn_grads = stage_call(
        functools.partial(attend_back_kernel, halo), parts,
        [(branch, "all"), (probs, "all"), (hidden_near, "all"), (mixed, "all"), (queries, "all"), (keys_near, "all"),
         (value_pre, "col"), (values, "col"), (gate_pre, "col"), (attended, "col"), (gated, "col"),
         (all_a, part(0, vw)), (all_a, part(1, vw)), (all_a, part(2, vw))],
        [((rows, latent_width), F32, "all"), ((halo, latent_width), BF16, "all"), ((rows, latent_width), F32, "all"),
         ((halo, width), BF16, "all"), ((rows, width), F32, "all"), ((rows, width), F32, "all"),
         ((replicas, parts, 3, depth, vw), BF16,
          pl.BlockSpec((replicas, 1, 3, depth, vw), lambda t: (0, t, 0, 0, 0)))],
        [pltpu.VMEM((rows, near_rows), F32), row_vm(near_rows), pltpu.VMEM((rows, near_rows), BF16)], "attend_back", 12 * matmul,
    )
    grad_keys = give_back(keys_own, keys_back)
    grad_hidden = give_back(hidden_own, lax.optimization_barrier((hidden_back, grad_keys))[0])
    grad_query_gain = jnp.sum(latent * grad_queries, axis=0)
    grad_query_bias = jnp.sum(grad_queries, axis=0)
    grad_key_gain = jnp.sum(latent * grad_keys, axis=0)
    grad_latent = low(grad_queries * query_gain + grad_keys * key_gain)
    grad_shared = dot32(mixed, grad_latent, TN)
    grad_ema = (dot32(grad_latent, shared_b, NT) + grad_mixed) * silu_slope(ema_out)

    pulls, head = ema_call(
        ema_leave, rows, dims, width,
        [(grad_ema, col(rows)), keep0, (unit, pair), (reads, pair), cont, mkr],
        [state_shape, edge_shape], [vm(at_rows), table_vm, scale_vm], "ema_leave", mac,
    )
    cross = (near[halo + 2 * rows - 1] == last).astype(F32)
    pull_in = from_later(head, 1) + cross * turned(from_later(head, 2), -1.0)
    ins = [(hidden, col(rows)), (grad_ema, col(rows)), seg8, kend, (masks["rk0"], whole(rows, LANES)),
           (masks["rkend"], whole(rows, LANES)), (unit, pair), (feed, single), (reads, pair), (root, single),
           (ema_input, single), cont, mkr, (pulls, col3(nstate, 8)), (pull_in, pair), (states, col3(nstate, 8)),
           (skip, col(1))]
    outs = [rows_shape, edge_shape, dim_shape, dim_shape, dim_shape, (jax.ShapeDtypeStruct((1, width), F32), col(1))]
    scratch = [vm(2 * at_rows), vm(at_rows), vm(nstate), table_vm, scale_vm, flat_vm(4, STEP * dims), flat_vm(9, dims),
               flat_vm(rows), flat_vm(rows)]
    if chip_links:
        results = ema_call(
            functools.partial(ema_grads_reduce, parts, len(ins), len(outs), len(scratch)), rows, dims, width,
            ins + [(attn_grads.reshape(replicas // 2, 2, parts, 3 * depth, vw), anywhere)],
            outs + [(jax.ShapeDtypeStruct((3 * depth, vw), F32), whole(3 * depth, vw))],
            scratch + reduce_scratch(parts, 3 * depth, vw), "ema_grads", 3 * mac, collective_id=2,
        )
        attn_sum = results[-1]
    else:
        results = ema_call(ema_grads, rows, dims, width, ins, outs, scratch, "ema_grads", 3 * mac)
        attn_sum = summed_along(summed(attn_grads), results[-1])
    grad_hidden_ema, output_grad, input_grad, rate_grad, angle_grad, grad_skip = results[:6]

    ffn_sum = summed_along(ffn_sum, grad_skip)

    grad_hidden = grad_hidden + grad_hidden_ema
    gain_grad = jnp.sum(centred * grad_hidden, axis=0)
    spread_grad = grad_hidden * norm_gain
    sum_a = rho * sums_of(spread_grad)
    sum_b = sums_of(spread_grad * (x - mean_full))
    cube = sum_b * rho * rho * rho
    push = jnp.concatenate([(cube * mean - sum_a) / count, -cube / (2.0 * count)], axis=1)
    backed = dot32(lower, push, TN, precision=HIGHEST)
    first = backed[:1]
    carry = next1 * from_later(first, 1) + next2 * from_later(first, 2)
    backed = backed + tails * carry
    grad_x = spread_grad * rho_full + spread_of(backed[:, :groups]) + 2.0 * x * spread_of(backed[:, groups:])
    in_grad = grad_residual + grad_x

    small = [gain_grad, rate_grad, angle_grad, input_grad, output_grad, grad_skip, grad_query_gain,
             grad_query_bias, grad_key_gain, grad_ffn_gain]
    sizes = [v.size for v in small]
    total = sum(sizes)
    members = parts * replicas
    unit = members * 8 * LANES
    packed = jnp.concatenate([v.reshape(-1) for v in small] + [jnp.zeros((-total % unit,), F32)])
    packed = packed.reshape(-1, LANES)
    levels = replicas.bit_length() - 1
    mirror = lambda v: v.transpose(tuple(reversed(range(levels))) + (levels, levels + 1))
    block = mirror(grad_shared.reshape((2,) * levels + (depth, latent_width)))
    packed, shared_sum = small_sums_call(packed, block.reshape(width, latent_width), replicas, parts)
    packed = packed.reshape(-1)
    small_sums, at = [], 0
    for n in sizes:
        small_sums.append(packed[at : at + n])
        at += n
    shape = lambda k, like: small_sums[k].reshape(like.shape)

    cut = lambda g, k: g[k * depth : (k + 1) * depth]
    return (
        block_out, in_grad, shape(0, norm_gain), shape(1, ema_rate), shape(2, ema_angle), shape(3, ema_input),
        shape(4, ema_output), shape(5, ema_skip), shared_sum, shape(6, query_gain), shape(7, query_bias),
        shape(8, key_gain), cut(attn_sum, 0), cut(attn_sum, 1), cut(attn_sum, 2).T, shape(9, ffn_gain),
        cut(ffn_sum, 0), cut(ffn_sum, 1), cut(ffn_sum, 2).T,
    )


def solution(mesh):
    rows, dp, copy = P(BOTH, None), P("dp", None), P()
    wide, tall = P("dp", "tensor"), P("tensor", "dp")
    return jax.shard_map(
        on_device,
        mesh=mesh,
        in_specs=(
            rows, dp, copy, copy, copy, copy, copy, copy, dp, copy, copy, copy, wide, wide, tall, copy, wide, wide,
            tall, rows,
        ),
        out_specs=(
            rows, rows, copy, copy, copy, copy, copy, copy, dp, copy, copy, copy, wide, wide, tall, copy, wide, wide,
            tall,
        ),
        check_vma=False,
    )
```

```python
import functools
import math

import jax
import jax.numpy as jnp
from jax import lax
from jax.experimental import pallas as pl
from jax.experimental.pallas import tpu as pltpu
from jax.experimental.layout import Layout, with_layout_constraint
from jax.sharding import PartitionSpec as P

TN_GROUPS = 16
EPSILON = 1e-05
REACH = 800
STEP = 16
LANES = 128
F32 = jnp.float32
BF16 = jnp.bfloat16
HIGHEST = lax.Precision.HIGHEST
BOTH = ("dp", "tensor")


def dot32(a, b, dims=((1,), (0,)), precision=None):
    return lax.dot_general(a, b, (dims, ((), ())), precision=precision, preferred_element_type=F32)


NT = ((1,), (1,))
TN = ((0,), (0,))


def silu_of(v):
    return v * jax.nn.sigmoid(v)


def silu_slope(v):
    sg = jax.nn.sigmoid(v)
    return sg * (1.0 + v * (1.0 - sg))


def broadcast_row(ref, row):
    return ref[pl.ds(row, 8, stride=0), :]


def rotate(x, shift):
    return pltpu.roll(x, shift % 8, axis=0)


def times(ar, ai, br, bi):
    return ar * br - ai * bi, ar * bi + ai * br


def power_list(dims, q_ref):
    qr, qi = q_ref[:dims], q_ref[dims:]
    out = [(jnp.ones_like(qr), jnp.zeros_like(qr))]
    for n in range(STEP):
        out.append(times(*out[-1], qr, qi))
    return out


def fill_scales(groups, dims, pw, qs):
    step = pw[STEP]
    qs[:dims], qs[dims : 2 * dims] = step
    turn = step
    for _ in range(groups - 1):
        turn = times(*turn, *step)
    for k in range(3):
        base = 2 * dims * (k + 1)
        qs[base : base + dims], qs[base + dims : base + 2 * dims] = turn
        turn = times(*turn, *turn)
    return turn


def fill_read(dims, pw, e_ref, ta):
    e0, e1 = e_ref[:dims], e_ref[dims:]
    for i in range(STEP):
        ta[0, i * dims : (i + 1) * dims], ta[1, i * dims : (i + 1) * dims] = times(e0, e1, *pw[i + 1])


def fill_feed(dims, pw, f_ref, tb):
    f = f_ref[...]
    for i in range(STEP):
        r, m = pw[STEP - 1 - i]
        tb[0, i * dims : (i + 1) * dims], tb[1, i * dims : (i + 1) * dims] = f * r, f * m


def tap_list(dims, pw, e_ref, f_ref):
    e0, e1, f = e_ref[:dims], e_ref[dims:], f_ref[...]
    out = []
    for d in range(STEP):
        row = jnp.sum(f * (e0 * pw[d][0] - e1 * pw[d][1]), axis=0, keepdims=True)
        out.append(jnp.broadcast_to(row, (8, LANES)))
    return out


def chunk_sums(groups, dims, table, source, out, sign):
    def pair(jp, carry):
        acc = [None] * groups
        for i in range(STEP):
            c = [broadcast_row(table.at[p], i * dims + jp * 2 + k) for k in range(2) for p in range(2)]
            for g in range(groups):
                h = source[g * STEP + i]
                terms = [v * h for v in c]
                acc[g] = terms if i == 0 else [u + v for u, v in zip(acc[g], terms)]
        for g in range(groups):
            for k in range(2):
                at = (g * dims + jp * 2 + k) * 2
                out[at] = acc[g][2 * k]
                out[at + 1] = acc[g][2 * k + 1] if sign > 0 else -acc[g][2 * k + 1]
        return carry

    lax.fori_loop(0, dims // 2, pair, 0)


def position_sums(groups, dims, table, states, mask, out, base, sign):
    block = 4

    def some(iq, carry):
        acc = [[None] * block for _ in range(groups)]
        for j in range(dims):
            here = [(states[(g * dims + j) * 2], states[(g * dims + j) * 2 + 1]) for g in range(groups)]
            for i in range(block):
                cr = broadcast_row(table.at[0], (iq * block + i) * dims + j)
                ci = broadcast_row(table.at[1], (iq * block + i) * dims + j)
                for g in range(groups):
                    u, v = cr * here[g][0], ci * here[g][1]
                    term = u - v if sign < 0 else u + v
                    acc[g][i] = term if j == 0 else acc[g][i] + term
        for g in range(groups):
            for i in range(block):
                at = g * STEP + iq * block + i
                out[base + at] = acc[g][i] * mask[at]
        return carry

    lax.fori_loop(0, STEP // block, some, 0)


def scan_states(groups, dims, j, l_ref, qs, cont_ref, mk_ref, inr, ini):
    qr, qi = broadcast_row(qs, j), broadcast_row(qs, dims + j)
    part = [(l_ref[(g * dims + j) * 2], l_ref[(g * dims + j) * 2 + 1]) for g in range(groups)]

    def through(sr, si):
        starts = []
        for g in range(groups):
            starts.append((sr, si))
            keep = cont_ref[g]
            tr, ti = times(qr, qi, sr, si)
            sr, si = keep * tr + part[g][0], keep * ti + part[g][1]
        return starts, sr, si

    _, er, ei = through(inr, ini)
    for k in range(3):
        base = 2 * dims * (k + 1)
        wr, wi = broadcast_row(qs, base + j), broadcast_row(qs, base + dims + j)
        pr, pi = times(wr, wi, rotate(er, 1 << k), rotate(ei, 1 << k))
        keep = mk_ref[k]
        er, ei = er + keep * pr, ei + keep * pi
    first = lax.broadcasted_iota(jnp.int32, (8, LANES), 0) == 0
    starts, _, _ = through(jnp.where(first, inr, rotate(er, 1)), jnp.where(first, ini, rotate(ei, 1)))
    return starts, (er, ei)


ENTER_PLAN = (
    (0, 2, False), (8, 1, False), (9, 1, False), (10, 1, False), (11, 2, False), (12, 1, False), (13, 1, False),
    (14, 2, False), (15, 0, True),
)


def shifted_rows(parts, halo, hops, rows, source, near, zeros, sems, local_sems):
    z = lax.axis_index("tensor")
    moves, fills, end = [], [], halo
    for h, n in enumerate(hops):
        place = near.at[pl.ds(end - n, n)]
        moves.append(Along(parts, h + 1, source.at[pl.ds(rows - n, n)], place, sems.at[0, h], sems.at[1, h]))
        fills.append((z <= h, zeros.at[pl.ds(0, n)], place, local_sems.at[h]))
        end -= n
    own = [(source, near.at[pl.ds(halo, rows)], local_sems.at[len(hops)])]
    if end > 0:
        own.append((zeros.at[pl.ds(0, end)], near.at[pl.ds(0, end)], local_sems.at[len(hops) + 1]))

    def each(action):
        for copy in own:
            action(pltpu.make_async_copy(*copy))
        for condition, *copy in fills:
            @pl.when(condition)
            def _():
                action(pltpu.make_async_copy(*copy))

    def start():
        for move in moves:
            move.start()
        each(lambda c: c.start())

    def wait():
        for move in moves:
            move.wait_recv()
            move.wait_send()
        each(lambda c: c.wait())

    return start, wait


def ema_forward(
    rows, dims, parts, halo, hops, hosted, h_ref, kend_ref, seg_ref, k0_ref, q_ref, f_ref, e_ref, cont_ref, mk_ref,
    link_ref, skip_ref, low_ref, zeros_ref, *refs
):
    refs = list(refs)
    pack_ref = refs.pop(0) if hosted else None
    out_ref, m_ref, s_ref, near_ref = (refs.pop(0) for _ in range(4))
    all_ref = refs.pop(0) if hosted else None
    hs, table, qs, parts_all, ends, got, entry, state_sems, near_sems, local_sems, *rest = refs
    groups = rows // (8 * STEP)
    step = pl.program_id(0)
    blocks = parts_all.shape[0]
    k = step % blocks
    stages = gather_stages(parts, pack_ref, all_ref, *rest) if hosted else []
    near_start, near_wait = shifted_rows(parts, halo, hops, rows, low_ref, near_ref, zeros_ref, near_sems, local_sems)
    states = lambda hop, at: Along(
        parts, hop, ends.at[at], got.at[hop - 1, at], state_sems.at[0, hop - 1, at], state_sems.at[1, hop - 1, at]
    )

    @pl.when(step == 0)
    def _():
        greet(parts, 3 if hosted else 0)

    @pl.when(step == blocks)
    def _():
        near_start()

    if hosted:
        run_stages(stages, step, ENTER_PLAN, False)
    pw = power_list(dims, q_ref)
    turn = fill_scales(groups, dims, pw, qs)

    @pl.when(step < blocks)
    def _():
        fill_feed(dims, pw, f_ref, table)
        for at in range(groups * STEP):
            hs[at] = h_ref[pl.ds(at, 8, stride=groups * STEP), :] * kend_ref[at]
        chunk_sums(groups, dims, table, hs, parts_all.at[k], 1)

        def one(j, carry):
            zero = jnp.zeros((8, LANES), F32)
            _, last = scan_states(groups, dims, j, parts_all.at[k], qs, cont_ref, mk_ref, zero, zero)
            ends[k, pl.ds(j, 1), :] = last[0][7:8]
            ends[k, pl.ds(dims + j, 1), :] = last[1][7:8]
            return carry

        lax.fori_loop(0, dims, one, 0)
        for hop in (1, 2):
            states(hop, k).start()

    @pl.when(step >= blocks)
    def _():
        entry[...] = jnp.zeros_like(entry)

        def near_one():
            entry[...] = got[0, k]

        def far_one():
            link = link_ref[...]
            r, i = times(*turn, got[1, k, :dims], got[1, k, dims:])
            entry[:dims] += link * r
            entry[dims:] += link * i

        states(1, k).wait_recv(near_one)
        states(2, k).wait_recv(far_one)
        ema_read(
            groups, dims, h_ref, seg_ref, k0_ref, pw, f_ref, e_ref, cont_ref, mk_ref, parts_all.at[k], entry, skip_ref,
            out_ref, m_ref, s_ref, hs, table, qs,
        )

    @pl.when(step == 2 * blocks - 1)
    def _():
        for at in range(blocks):
            for hop in (1, 2):
                states(hop, at).wait_send()
        near_wait()

    if hosted:
        run_stages(stages, step, ENTER_PLAN, True)


def ema_read(
    groups, dims, h_ref, seg_ref, k0_ref, pw, f_ref, e_ref, cont_ref, mk_ref, l_ref, in_ref, skip_ref, out_ref, m_ref,
    s_ref, hs, ta, qs
):
    first = lax.broadcasted_iota(jnp.int32, (8, LANES), 0) == 0
    fill_read(dims, pw, e_ref, ta)
    taps = tap_list(dims, pw, e_ref, f_ref)

    def one(j, carry):
        inr = jnp.where(first, broadcast_row(in_ref, j), 0.0)
        ini = jnp.where(first, broadcast_row(in_ref, dims + j), 0.0)
        starts, _ = scan_states(groups, dims, j, l_ref, qs, cont_ref, mk_ref, inr, ini)
        for g in range(groups):
            s_ref[(g * dims + j) * 2] = starts[g][0]
            s_ref[(g * dims + j) * 2 + 1] = starts[g][1]
        return carry

    lax.fori_loop(0, dims, one, 0)
    for at in range(groups * STEP):
        hs[at] = h_ref[pl.ds(at, 8, stride=groups * STEP), :]
    position_sums(groups, dims, ta, s_ref, k0_ref, hs, groups * STEP, -1)
    tap0 = taps[0] + jnp.broadcast_to(skip_ref[...], (8, LANES))
    for g in range(groups):
        for i in range(STEP):
            at = g * STEP + i
            seg = seg_ref[at]
            out = hs[groups * STEP + at] + tap0 * hs[at]
            for s in range(i):
                src = g * STEP + s
                out = out + taps[i - s] * jnp.where(seg_ref[src] == seg, hs[src], 0.0)
            out_ref[pl.ds(at, 8, stride=groups * STEP), :] = out
    m_ref[...] = silu_of(out_ref[...]).astype(m_ref.dtype)


def reverse_states(groups, dims, j, g_ref, qs, cont_ref, mkr_ref, inr, ini):
    qr, qi = broadcast_row(qs, j), broadcast_row(qs, dims + j)
    part = [(g_ref[(g * dims + j) * 2], g_ref[(g * dims + j) * 2 + 1]) for g in range(groups)]

    def through(yr, yi):
        ends = [None] * groups
        for g in reversed(range(groups)):
            ends[g] = (yr, yi)
            keep = cont_ref[g]
            tr, ti = qr * yr + qi * yi, qr * yi - qi * yr
            yr, yi = keep * tr + part[g][0], keep * ti + part[g][1]
        return ends, yr, yi

    _, fr, fi = through(inr, ini)
    for k in range(3):
        base = 2 * dims * (k + 1)
        wr, wi = broadcast_row(qs, base + j), broadcast_row(qs, base + dims + j)
        pr, pi = rotate(fr, -(1 << k)), rotate(fi, -(1 << k))
        keep = mkr_ref[k]
        fr, fi = fr + keep * (wr * pr + wi * pi), fi + keep * (wr * pi - wi * pr)
    last = lax.broadcasted_iota(jnp.int32, (8, LANES), 0) == 7
    ends, _, _ = through(jnp.where(last, inr, rotate(fr, -1)), jnp.where(last, ini, rotate(fi, -1)))
    return ends, (fr, fi)


REDUCE_PLAN = (
    (0, 1, False), (4, 1, False), (5, 1, False), (7, 1, False), (8, 2, False), (9, 1, False), (10, 1, False),
    (11, 1, False), (12, 1, False), (13, 1, False), (14, 1, False), (15, 0, True),
)


def ema_backward(
    rows, dims, parts, halo, hops, hosted, h_ref, de_ref, seg_ref, kend_ref, k0_ref, rk0_ref, rkend_ref, q_ref, f_ref,
    e_ref, root_ref, feed_ref, cont_ref, mkr_ref, s_ref, cross_ref, skip_ref, back_ref, zeros_ref, *refs
):
    refs = list(refs)
    pack_ref = refs.pop(0) if hosted else None
    outs = [refs.pop(0) for _ in range(6)]
    back = [refs.pop(0) for _ in hops]
    sum_ref = refs.pop(0) if hosted else None
    pulls, heads, got, entry, state_sems, back_sems, local_sems, *rest = refs
    held, rest = rest[:9], rest[9:]
    hs, ds, la, table, qs = held[:5]
    groups = rows // (8 * STEP)
    step = pl.program_id(0)
    z = lax.axis_index("tensor")
    blocks = pulls.shape[0]
    k = step % blocks
    stages = reduce_stages(parts, pack_ref, sum_ref, *rest) if hosted else []
    states = lambda hop, at: Along(
        parts, -hop, heads.at[at], got.at[hop - 1, at], state_sems.at[0, hop - 1, at], state_sems.at[1, hop - 1, at]
    )
    moves, fills, end = [], [], halo
    for h, n in enumerate(hops):
        moves.append(Along(parts, -h - 1, back_ref.at[pl.ds(end - n, n)], back[h], back_sems.at[0, h], back_sems.at[1, h]))
        fills.append((z + h + 1 >= parts, (zeros_ref.at[pl.ds(0, n)], back[h], local_sems.at[h])))
        end -= n

    def filling(action):
        for condition, copy in fills:
            @pl.when(condition)
            def _():
                action(pltpu.make_async_copy(*copy))

    @pl.when(step == 0)
    def _():
        greet(parts, 3 if hosted else 0)
        filling(lambda c: c.start())

    @pl.when(step == blocks)
    def _():
        for move in moves:
            move.start()

    if hosted:
        run_stages(stages, step, REDUCE_PLAN, False)
    pw = power_list(dims, q_ref)
    turn = fill_scales(groups, dims, pw, qs)

    @pl.when(step < blocks)
    def _():
        fill_read(dims, pw, e_ref, table)
        for at in range(groups * STEP):
            ds[at] = de_ref[pl.ds(at, 8, stride=groups * STEP), :] * k0_ref[at]
        chunk_sums(groups, dims, table, ds, pulls.at[k], -1)

        def one(j, carry):
            zero = jnp.zeros((8, LANES), F32)
            _, head = reverse_states(groups, dims, j, pulls.at[k], qs, cont_ref, mkr_ref, zero, zero)
            heads[k, pl.ds(j, 1), :] = head[0][0:1]
            heads[k, pl.ds(dims + j, 1), :] = head[1][0:1]
            return carry

        lax.fori_loop(0, dims, one, 0)
        for hop in (1, 2):
            states(hop, k).start()

    @pl.when(step >= blocks)
    def _():
        entry[...] = jnp.zeros_like(entry)

        def near_one():
            entry[...] = got[0, k]

        def far_one():
            cross = cross_ref[...]
            r, i = times(turn[0], -turn[1], got[1, k, :dims], got[1, k, dims:])
            entry[:dims] += cross * r
            entry[dims:] += cross * i

        states(1, k).wait_recv(near_one)
        states(2, k).wait_recv(far_one)
        ema_grads(
            groups, dims, h_ref, de_ref, seg_ref, kend_ref, rk0_ref, rkend_ref, pw, f_ref, e_ref, root_ref, feed_ref,
            cont_ref, mkr_ref, pulls.at[k], entry, s_ref, skip_ref, *outs, *held,
        )

    @pl.when(step == 2 * blocks - 1)
    def _():
        for at in range(blocks):
            for hop in (1, 2):
                states(hop, at).wait_send()
        for move in moves:
            move.wait_recv()
            move.wait_send()
        filling(lambda c: c.wait())

    if hosted:
        run_stages(stages, step, REDUCE_PLAN, True)


def ema_grads(
    groups, dims, h_ref, de_ref, seg_ref, kend_ref, rk0_ref, rkend_ref, pw, f_ref, e_ref, root_ref, feed_ref, cont_ref,
    mkr_ref, g_ref, in_ref, s_ref, skip_ref, dh_ref, ge_ref, gf_ref, gr_ref, ga_ref, gs_ref, hs, ds, la, tb, qs, pf,
    red, hn, dn
):
    last = lax.broadcasted_iota(jnp.int32, (8, LANES), 0) == 7
    fill_feed(dims, pw, f_ref, tb)
    taps = tap_list(dims, pw, e_ref, f_ref)
    for i in range(STEP):
        at = slice(i * dims, (i + 1) * dims)
        pf[0, at], pf[1, at] = pw[i + 1]
        pf[2, at], pf[3, at] = pw[STEP - 1 - i]

    def one(j, carry):
        inr = jnp.where(last, broadcast_row(in_ref, j), 0.0)
        ini = jnp.where(last, broadcast_row(in_ref, dims + j), 0.0)
        ends, _ = reverse_states(groups, dims, j, g_ref, qs, cont_ref, mkr_ref, inr, ini)
        qr = jnp.zeros((8, LANES), F32)
        qi = jnp.zeros((8, LANES), F32)
        for g in range(groups):
            yr, yi = ends[g]
            la[(g * dims + j) * 2] = yr
            la[(g * dims + j) * 2 + 1] = yi
            keep = cont_ref[g]
            sr, si = s_ref[(g * dims + j) * 2], s_ref[(g * dims + j) * 2 + 1]
            qr = qr + keep * (yr * sr + yi * si)
            qi = qi + keep * (yi * sr - yr * si)
        red[0, pl.ds(j, 1), :] = jnp.sum(qr, axis=0, keepdims=True)
        red[1, pl.ds(j, 1), :] = jnp.sum(qi, axis=0, keepdims=True)
        return carry

    lax.fori_loop(0, dims, one, 0)
    total = jnp.zeros((8, LANES), F32)
    for at in range(groups * STEP):
        h = h_ref[pl.ds(at, 8, stride=groups * STEP), :]
        d = de_ref[pl.ds(at, 8, stride=groups * STEP), :]
        hs[at] = h
        ds[at] = d
        total = total + h * d
    gs_ref[...] = jnp.sum(total, axis=0, keepdims=True)
    position_sums(groups, dims, tb, la, kend_ref, hs, groups * STEP, 1)
    tap0 = taps[0] + jnp.broadcast_to(skip_ref[...], (8, LANES))
    kacc = [jnp.zeros((8, LANES), F32) for _ in range(STEP)]
    kacc[0] = total
    for g in range(groups):
        for s in range(STEP):
            at = g * STEP + s
            seg = seg_ref[at]
            h = hs[at]
            out = hs[groups * STEP + at] + tap0 * ds[at]
            for t in range(s + 1, STEP):
                d = jnp.where(seg_ref[g * STEP + t] == seg, ds[g * STEP + t], 0.0)
                out = out + taps[t - s] * d
                kacc[t - s] = kacc[t - s] + h * d
            dh_ref[pl.ds(at, 8, stride=groups * STEP), :] = out

    hn[...] = h_ref[...] * rkend_ref[...]
    dn[...] = de_ref[...] * rk0_ref[...]
    width = 4
    place = (lax.broadcasted_iota(jnp.int32, (STEP, LANES), 0) + 1).astype(F32)

    def tables(jq, carry):
        def chunk(n, acc):
            sub, g = n // groups, n % groups
            d0, d1 = (dn[pl.ds(pl.multiple_of(n * STEP + 8 * p, 8), 8), :] for p in range(2))
            h0, h1 = (hn[pl.ds(pl.multiple_of(n * STEP + 8 * p, 8), 8), :] for p in range(2))
            out = []
            for k in range(width):
                at = (g * dims + jq * width + k) * 2
                sr, si = (s_ref[at + p, pl.ds(sub, 8, stride=0), :] for p in range(2))
                yr, yi = (la[at + p, pl.ds(sub, 8, stride=0), :] for p in range(2))
                a = acc[8 * k : 8 * k + 8]
                out += [a[0] + d0 * sr, a[1] + d1 * sr, a[2] - d0 * si, a[3] - d1 * si]
                out += [a[4] + h0 * yr, a[5] + h1 * yr, a[6] + h0 * yi, a[7] + h1 * yi]
            return tuple(out)

        acc = lax.fori_loop(0, 8 * groups, chunk, (jnp.zeros((8, LANES), F32),) * (8 * width))
        for k in range(width):
            j = jq * width + k
            ar, ai, br, bi = (
                jnp.concatenate([acc[8 * k + 2 * p], acc[8 * k + 2 * p + 1]], axis=0) for p in range(4)
            )
            pr, pi, wr, wi = (pf[p, pl.ds(j, STEP, stride=dims), :] for p in range(4))
            ur, ui = ar * pr + ai * pi, ai * pr - ar * pi
            vr, vi = br * wr + bi * wi, bi * wr - br * wi
            rest = STEP - place
            sums = (ur, ui, place * ur, place * ui, vr, rest * vr, rest * vi)
            for p, v in enumerate(sums):
                red[2 + p, pl.ds(j, 1), :] = jnp.sum(v, axis=0, keepdims=True)
        return carry

    lax.fori_loop(0, dims // width, tables, 0)
    e0, e1, f = e_ref[:dims], e_ref[dims:], f_ref[...]
    zero = jnp.zeros((dims, LANES), F32)
    tr, ti, ur, ui = zero, zero, zero, zero
    for d in range(STEP):
        tap = jnp.broadcast_to(jnp.sum(kacc[d], axis=0, keepdims=True), (dims, LANES))
        r, m = tap * pw[d][0], tap * pw[d][1]
        tr, ti = tr + r, ti - m
        if d > 0:
            ur, ui = ur + d * r, ui - d * m
    ge_ref[:dims] = red[2] + f * tr
    ge_ref[dims:] = red[3] + f * ti
    gf = red[6] + e0 * tr + e1 * ti
    xr, xi = red[4] + f * ur, red[5] + f * ui
    lr = e0 * xr + e1 * xi + f * red[7]
    li = e0 * xi - e1 * xr + f * red[8]
    zr, zi = pw[STEP]
    lr = lr + STEP * (red[0] * zr + red[1] * zi)
    li = li + STEP * (red[1] * zr - red[0] * zi)
    root = root_ref[...]
    gf_ref[...] = gf * root
    gr_ref[...] = gf * feed_ref[...] * (1.0 - root * root) / root - lr
    ga_ref[...] = li


def whole(*shape):
    return pl.BlockSpec(shape, lambda i: (0,) * len(shape))


def ema_call(body, width, ins, outs, scratch, name, flops, collective_id):
    return pl.pallas_call(
        body,
        grid=(2 * (width // LANES),),
        in_specs=[s for _, s in ins],
        out_specs=[s for _, s in outs],
        out_shape=[o for o, _ in outs],
        scratch_shapes=scratch,
        compiler_params=pltpu.CompilerParams(
            vmem_limit_bytes=60 << 20, collective_id=collective_id, has_side_effects=True
        ),
        cost_estimate=pl.CostEstimate(flops=flops // 1000, bytes_accessed=1024, transcendentals=0),
        name=name,
    )(*[a for a, _ in ins])


def spread(v):
    return jnp.broadcast_to(v[..., None], v.shape + (LANES,))


def row_masks(seg, before):
    rows = seg.shape[0]
    groups = rows // (8 * STEP)
    cube = seg.reshape(8, groups, STEP)
    chunk_last = cube[:, :, -1]
    prior = jnp.concatenate([before[None], chunk_last.reshape(-1)[:-1]]).reshape(8, groups)
    keep0 = (cube == prior[:, :, None]).astype(F32)
    kend = (cube == chunk_last[:, :, None]).astype(F32)
    order = lambda v: spread(v.transpose(1, 2, 0).reshape(groups * STEP, 8))
    cont = spread((chunk_last == prior).astype(F32).transpose(1, 0))
    ends = jnp.concatenate([before[None], chunk_last[:, -1]])
    sub = jnp.arange(8)
    ahead, behind = [], []
    for k in range(3):
        w = 1 << k
        a = jnp.take(ends, jnp.maximum(sub + 1 - w, 0))
        ahead.append(((ends[1:] == a) & (sub >= w)).astype(F32))
        b = jnp.take(ends, jnp.minimum(sub + w, 8))
        behind.append(((ends[:8] == b) & (sub + w <= 7)).astype(F32))
    return dict(
        seg=order(cube.astype(F32)), keep0=order(keep0), kend=order(kend), cont=cont,
        mk=spread(jnp.stack(ahead)), mkr=spread(jnp.stack(behind)),
        rk0=spread(keep0.reshape(rows)), rkend=spread(kend.reshape(rows)),
    )


def merged(ref):
    v = ref[...]
    return v.reshape(-1, v.shape[-1])


GATHER_PLAN = ((0, 2, False), (1, 1, False), (2, 1, False), (3, 1, False), (3, 0, True))


def attend_gather_kernel(halo, parts, ins, outs, *refs):
    own = list(refs)
    pack_ref, all_ref = own.pop(ins), own.pop(ins + outs)
    stages = gather_stages(parts, pack_ref, all_ref, *own[ins + outs + 1 :])
    step = pl.program_id(0)

    @pl.when(step == 0)
    def _():
        greet(parts, 3)

    run_stages(stages, step, GATHER_PLAN, False)
    attend_kernel(halo, *own[: ins + outs + 1])
    run_stages(stages, step, GATHER_PLAN, True)


def attend_kernel(
    halo, q_ref, k_ref, seg_ref, segk_ref, h_ref, m_ref, x_ref, gain_ref, wv_ref, wg_ref, wo_ref,
    p_ref, vp_ref, v_ref, gp_ref, o_ref, g_ref, y_ref, n_ref, pb_ref,
):
    t = pl.program_id(0)

    @pl.when(t == 0)
    def _():
        rows, keys = pb_ref.shape
        scores = dot32(q_ref[...], k_ref[...], NT) * (1.0 / math.sqrt(q_ref.shape[1]))
        at_row = lax.broadcasted_iota(jnp.int32, (rows, keys), 0)
        at_key = lax.broadcasted_iota(jnp.int32, (rows, keys), 1)
        allowed = (at_key <= at_row + halo) & (segk_ref[...] == seg_ref[...])
        scores = jnp.where(allowed, scores, -1e30)
        raw = jnp.exp(scores - jnp.max(scores, axis=1, keepdims=True))
        p = raw / jnp.sum(raw, axis=1, keepdims=True)
        p_ref[...] = p
        pb_ref[...] = p.astype(BF16)
        y_ref[...] = x_ref[...].astype(F32)

    vp = dot32(h_ref[...], merged(wv_ref))
    v = silu_of(vp).astype(BF16)
    vp_ref[...] = vp.astype(BF16)
    v_ref[...] = v
    gp = dot32(m_ref[...], merged(wg_ref))
    gp_ref[...] = gp.astype(BF16)
    o = dot32(pb_ref[...], v)
    o_ref[...] = o.astype(BF16)
    g = (silu_of(gp) * o).astype(BF16)
    g_ref[...] = g
    y_ref[...] += dot32(g, merged(wo_ref), NT)

    @pl.when(t == pl.num_programs(0) - 1)
    def _():
        y = y_ref[...]
        rr = lax.rsqrt(jnp.mean(y * y, axis=1, keepdims=True) + EPSILON)
        n_ref[...] = (y * rr * gain_ref[...]).astype(BF16)


def ffn_kernel(
    y_ref, n_ref, og_ref, gain_ref, w1_ref, w3_ref, w2_ref, out_ref, dy_ref, branch_ref, gain_grad_ref, grads_ref,
    acc, dn,
):
    t = pl.program_id(0)

    @pl.when(t == 0)
    def _():
        acc[...] = y_ref[...]
        dn[...] = jnp.zeros_like(dn)

    w1, w3, w2 = merged(w1_ref), merged(w3_ref), merged(w2_ref)
    nn, og = n_ref[...], og_ref[...]
    u1, u3 = dot32(nn, w1), dot32(nn, w3)
    sg = jax.nn.sigmoid(u1)
    act = u1 * sg
    hd = (act * u3).astype(BF16)
    acc[...] += dot32(hd, w2, NT)
    dh = dot32(og, w2)
    d1 = (dh * u3 * (sg * (1.0 + u1 * (1.0 - sg)))).astype(BF16)
    d3 = (dh * act).astype(BF16)
    dn[...] += dot32(d1, w1, NT) + dot32(d3, w3, NT)
    depth = grads_ref.shape[3]
    for k, (a, b) in enumerate(((nn, d1), (nn, d3), (og, hd))):
        grads_ref[:, 0, k] = dot32(a, b, TN).astype(BF16).reshape(-1, depth, b.shape[1])

    @pl.when(t == pl.num_programs(0) - 1)
    def _():
        out_ref[...] = acc[...].astype(BF16)
        y = y_ref[...]
        rr = lax.rsqrt(jnp.mean(y * y, axis=1, keepdims=True) + EPSILON)
        nh = y * rr
        g = dn[...]
        gain_grad_ref[...] = jnp.sum(nh * g, axis=0, keepdims=True)
        scaled = g * gain_ref[...]
        dy = og.astype(F32) + rr * (scaled - nh * jnp.mean(nh * scaled, axis=1, keepdims=True))
        dy_ref[...] = dy
        branch_ref[...] = dy.astype(BF16)


def attend_back_kernel(
    halo, br_ref, p_ref, h_ref, m_ref, q_ref, k_ref, vp_ref, v_ref, gp_ref, o_ref, g_ref, wv_ref, wg_ref, wo_ref,
    dq_ref, dkn_ref, dk_ref, dhn_ref, dh_ref, dm_ref, grads_ref, dp, dhv, pb_ref,
):
    t = pl.program_id(0)

    @pl.when(t == 0)
    def _():
        pb_ref[...] = p_ref[...].astype(BF16)
        dp[...] = jnp.zeros_like(dp)
        dhv[...] = jnp.zeros_like(dhv)
        dm_ref[...] = jnp.zeros_like(dm_ref)

    branch, pb = br_ref[...], pb_ref[...]
    dg = dot32(branch, merged(wo_ref))
    gp = gp_ref[...].astype(F32)
    sg = jax.nn.sigmoid(gp)
    da = (dg * (gp * sg)).astype(BF16)
    dr = (dg * o_ref[...].astype(F32) * (sg * (1.0 + gp * (1.0 - sg)))).astype(BF16)
    dp[...] += dot32(da, v_ref[...], NT)
    dv = dot32(pb, da, TN)
    dvp = (dv * silu_slope(vp_ref[...].astype(F32))).astype(BF16)
    dhv[...] += dot32(dvp, merged(wv_ref), NT)
    dm_ref[...] += dot32(dr, merged(wg_ref), NT)
    depth = grads_ref.shape[3]
    for k, (a, b) in enumerate(((h_ref[...], dvp), (m_ref[...], dr), (branch, g_ref[...]))):
        grads_ref[:, 0, k] = dot32(a, b, TN).astype(BF16).reshape(-1, depth, b.shape[1])

    @pl.when(t == pl.num_programs(0) - 1)
    def _():
        scale = 1.0 / math.sqrt(q_ref.shape[1])
        p = p_ref[...]
        d = dp[...]
        ds = (p * (d - jnp.sum(p * d, axis=1, keepdims=True))).astype(BF16)
        dq_ref[...] = dot32(ds, k_ref[...]) * scale
        dk = dot32(ds, q_ref[...], TN) * scale
        dkn_ref[...] = dk[:halo].astype(BF16)
        dk_ref[...] = dk[halo:]
        dhn_ref[...] = dhv[:halo, :].astype(BF16)
        dh_ref[...] = dhv[halo:, :]


def stage_call(body, steps, ins, outs, scratch, name, flops, collective_id=None):
    def spec(v, how):
        if how == "all":
            return pl.BlockSpec(v.shape, lambda t: (0,) * v.ndim)
        if how == "col":
            return pl.BlockSpec((v.shape[0], v.shape[1] // steps), lambda t: (0, t))
        return how

    outs = [(jax.ShapeDtypeStruct(s, d), how) for s, d, how in outs]
    return pl.pallas_call(
        body,
        grid=(steps,),
        in_specs=[spec(v, how) for v, how in ins],
        out_specs=[spec(v, how) for v, how in outs],
        out_shape=[v for v, _ in outs],
        scratch_shapes=scratch,
        compiler_params=pltpu.CompilerParams(
            vmem_limit_bytes=60 << 20, collective_id=collective_id, has_side_effects=collective_id is not None
        ),
        cost_estimate=pl.CostEstimate(flops=flops // 1000, bytes_accessed=1024, transcendentals=0),
        name=name,
    )(*[v for v, _ in ins])


def flipped(d, k):
    return d + (1 - 2 * ((d // (1 << k)) % 2)) * (1 << k)


def greet(parts, dp_bits):
    d, z = lax.axis_index("dp"), lax.axis_index("tensor")
    barrier = pltpu.get_barrier_semaphore()
    for k in range(dp_bits):
        pl.semaphore_signal(barrier, inc=1, device_id=(flipped(d, k), z), device_id_type=pl.DeviceIdType.MESH)
    for step in (-2, -1, 1, 2):
        @pl.when((z + step >= 0) & (z + step < parts))
        def _():
            pl.semaphore_signal(barrier, inc=1, device_id=(d, z + step), device_id_type=pl.DeviceIdType.MESH)
    pl.semaphore_wait(barrier, dp_bits + jnp.minimum(z, 2) + jnp.minimum(parts - 1 - z, 2))


class Along:
    def __init__(self, parts, hop, src, dst, send_sem, recv_sem):
        d, z = lax.axis_index("dp"), lax.axis_index("tensor")
        to = z + hop
        self.sends = (to >= 0) & (to < parts)
        self.gets = (z - hop >= 0) & (z - hop < parts)
        self.make = lambda: pltpu.make_async_remote_copy(
            src_ref=src, dst_ref=dst, send_sem=send_sem, recv_sem=recv_sem,
            device_id=(d, jnp.clip(to, 0, parts - 1)), device_id_type=pl.DeviceIdType.MESH,
        )

    def start(self):
        @pl.when(self.sends)
        def _():
            self.make().start()

    def wait_send(self):
        @pl.when(self.sends)
        def _():
            self.make().wait_send()

    def wait_recv(self, then=lambda: None):
        @pl.when(self.gets)
        def _():
            self.make().wait_recv()
            then()


def gather_stages(parts, pack_ref, out_ref, sems, own_sem):
    d, z = lax.axis_index("dp"), lax.axis_index("tensor")
    total = pack_ref.shape[0]
    cut = total // 32 * 16
    upper, lower, full = pl.ds(0, cut), pl.ds(cut, total - cut), pl.ds(0, total)
    core, first, second = (flipped(d, k) for k in range(3))
    across = first + second - d
    MESH = pl.DeviceIdType.MESH

    LINE, TO_FIRST, TO_SECOND, UP, DOWN, C_OWN, C_FIRST, C_SECOND, C_UP, C_DOWN = range(10)

    def copy(kind, b, source, part, dp_to, z_to):
        here = out_ref.at[source, b, part]
        return pltpu.make_async_remote_copy(
            src_ref=here, dst_ref=here, send_sem=sems.at[0, kind, b], recv_sem=sems.at[1, kind, b],
            device_id=(dp_to, z_to), device_id_type=MESH,
        )

    def begin():
        mine = pltpu.make_async_copy(pack_ref, out_ref.at[d, z], own_sem)
        mine.start()
        mine.wait()

    def spread_block(b):
        copy(TO_FIRST, b, d, full, first, z).start()
        copy(TO_SECOND, b, d, full, second, z).start()
        copy(C_OWN, b, d, full, core, z).start()

    def along(b, step):
        @pl.when((z + step >= 0) & (z + step < parts))
        def _():
            here = out_ref.at[d, b]
            pltpu.make_async_remote_copy(
                src_ref=here, dst_ref=here, send_sem=sems.at[0, LINE + (10 if step > 0 else 11), b],
                recv_sem=sems.at[1, LINE, b], device_id=(d, z + step), device_id_type=MESH,
            ).start()

    def relay(b):
        copy(TO_FIRST, b, first, full, first, z).wait_recv()
        copy(UP, b, first, upper, second, z).start()
        copy(C_FIRST, b, first, full, core, z).start()
        copy(TO_SECOND, b, second, full, second, z).wait_recv()
        copy(DOWN, b, second, lower, first, z).start()
        copy(C_SECOND, b, second, full, core, z).start()

    def corner(b):
        copy(UP, b, across, upper, second, z).wait_recv()
        copy(C_UP, b, across, upper, core, z).start()
        copy(DOWN, b, across, lower, first, z).wait_recv()
        copy(C_DOWN, b, across, lower, core, z).start()

    def at_distance(dist, action):
        for side in ((0,) if dist == 0 else (-1, 1)):
            b = z + side * dist
            @pl.when((b >= 0) & (b < parts))
            def _():
                action(b, side)

    def arrive(b, side):
        if side != 0:
            copy(LINE, b, d, full, d, z).wait_recv()
        if side <= 0:
            along(b, 1)
        if side >= 0:
            along(b, -1)
        spread_block(b)

    def finish():
        other_first, other_second = core + first - d, core + second - d
        for b in range(parts):
            for kind, source, part in ((C_OWN, core, full), (C_FIRST, other_first, full), (C_SECOND, other_second, full),
                                       (C_UP, core + across - d, upper), (C_DOWN, core + across - d, lower)):
                copy(kind, b, source, part, core, z).wait_recv()
            for kind, source, part in ((TO_FIRST, d, full), (TO_SECOND, d, full), (C_OWN, d, full), (UP, first, upper),
                                       (DOWN, second, lower), (C_FIRST, first, full), (C_SECOND, second, full),
                                       (C_UP, across, upper), (C_DOWN, across, lower)):
                copy(kind, b, source, part, core, z).wait_send()
            for step, slot in ((1, 10), (-1, 11)):
                @pl.when((z + step >= 0) & (z + step < parts) & (step * (z - b) >= 0))
                def _():
                    copy(slot, b, d, full, core, z).wait_send()

    stages = [begin]
    for dist in range(parts + 2):
        if dist < parts:
            stages.append(functools.partial(at_distance, dist, arrive))
        if 1 <= dist < parts + 1:
            stages.append(functools.partial(at_distance, dist - 1, lambda b, side: relay(b)))
        if dist >= 2:
            stages.append(functools.partial(at_distance, dist - 2, lambda b, side: corner(b)))
    return stages + [finish]


def gather_scratch(parts):
    return [pltpu.SemaphoreType.DMA((2, 12, parts)), pltpu.SemaphoreType.DMA]


def run_stages(stages, step, plan, late):
    at = 0
    for when, count, end in plan:
        here = stages[at : at + count] if count else stages[at:]
        at += len(here)
        if end == late:
            @pl.when(step == when)
            def _():
                for stage in here:
                    stage()


R_CORE, R_FIRST, R_FIRST2, R_SECOND, R_SECOND2, R_UP, R_DOWN, R_RIGHT, R_LEFT = range(9)


def reduce_scratch(parts, rows, columns):
    upper = rows // 32 * 16
    vm = lambda *n: pltpu.VMEM((*n, columns), BF16)
    return [
        vm(parts, 4, rows), vm(parts, 4, rows), vm(parts, 2, upper), vm(parts, 2, rows - upper), vm(parts, upper),
        vm(parts, rows - upper), vm(2, parts, rows), pltpu.SemaphoreType.DMA((2, 9, parts)),
        pltpu.SemaphoreType.DMA((parts,)),
    ]


def reduce_stages(parts, pack, out, acc, got_core, got_first, got_second, got_up, got_down, got_line, sems, load_sems):
    d, z = lax.axis_index("dp"), lax.axis_index("tensor")
    MESH = pl.DeviceIdType.MESH
    rows = acc.shape[2]
    cut = rows // 32 * 16
    upper, lower = pl.ds(0, cut), pl.ds(cut, rows - cut)
    me, core = d // 2, d % 2
    bit = lambda k: (me // (1 << k)) % 2
    first = me + (1 - 2 * bit(0))
    second = me + 2 * (1 - 2 * bit(1))
    across = first + second - me
    on = lambda p: 2 * p + core
    far = z // (parts // 2)
    near_end = z + far * (parts - 1 - 2 * z)

    def unit(s):
        t = (parts - 1 - s) + near_end * ((3, 0, 2, 1)[s] - (parts - 1 - s))
        return t + far * (parts - 1 - 2 * t)

    def copy(kind, t, src, dst, where):
        return pltpu.make_async_remote_copy(
            src_ref=src, dst_ref=dst, send_sem=sems.at[0, kind, t], recv_sem=sems.at[1, kind, t], device_id=where,
            device_id_type=MESH,
        )

    def copies(s):
        t = unit(s)
        to_first, to_second = (on(first), z), (on(second), z)
        table = {
            R_CORE: (pack.at[:, 1 - core, t], got_core.at[t], (2 * me + 1 - core, z)),
            R_FIRST: (acc.at[t, first, upper], got_first.at[t, 0], to_first),
            R_FIRST2: (acc.at[t, across, upper], got_first.at[t, 1], to_first),
            R_SECOND: (acc.at[t, second, lower], got_second.at[t, 0], to_second),
            R_SECOND2: (acc.at[t, across, lower], got_second.at[t, 1], to_second),
            R_UP: (acc.at[t, second, upper], got_up.at[t], to_second),
            R_DOWN: (acc.at[t, first, lower], got_down.at[t], to_first),
            R_RIGHT: (acc.at[t, me], got_line.at[0, t], (d, jnp.minimum(z + 1, parts - 1))),
            R_LEFT: (acc.at[t, me], got_line.at[1, t], (d, jnp.maximum(z - 1, 0))),
        }
        return lambda kind: copy(kind, t, *table[kind])

    def load(s):
        t = unit(s)
        return pltpu.make_async_copy(pack.at[:, core, t], acc.at[t], load_sems.at[t])

    def add(target, at, count, source):
        tile = 32 if count % 32 == 0 else 16

        def some(i, carry):
            here = pl.ds(pl.multiple_of(at + i * tile, 16), tile)
            there = pl.ds(pl.multiple_of(i * tile, 16), tile)
            target[here, :] = (target[here, :].astype(F32) + source[there, :].astype(F32)).astype(BF16)
            return carry

        lax.fori_loop(0, count // tile, some, 0)

    def begin():
        for s in range(parts):
            load(s).start()
            copies(s)(R_CORE).start()

    def cores(s):
        t, c = unit(s), copies(s)
        load(s).wait()
        c(R_CORE).wait_recv()
        for p in (first, across, second, me):
            add(acc.at[t, p], 0, rows, got_core.at[t, p])
        for kind in (R_FIRST, R_FIRST2, R_SECOND, R_SECOND2):
            c(kind).start()

    def chips(s):
        t, c = unit(s), copies(s)
        for kind in (R_FIRST2, R_SECOND2, R_FIRST, R_SECOND):
            c(kind).wait_recv()
        add(acc.at[t, second], 0, cut, got_first.at[t, 1])
        c(R_UP).start()
        add(acc.at[t, first], cut, rows - cut, got_second.at[t, 1])
        c(R_DOWN).start()
        add(acc.at[t, me], 0, cut, got_first.at[t, 0])
        add(acc.at[t, me], cut, rows - cut, got_second.at[t, 0])

    def line(s):
        t, c = unit(s), copies(s)
        c(R_UP).wait_recv()
        add(acc.at[t, me], 0, cut, got_up.at[t])
        c(R_DOWN).wait_recv()
        add(acc.at[t, me], cut, rows - cut, got_down.at[t])

        @pl.when((z <= t) & (z > 0))
        def _():
            c(R_RIGHT).wait_recv()
            add(acc.at[t, me], 0, rows, got_line.at[0, t])

        @pl.when((z >= t) & (z < parts - 1))
        def _():
            c(R_LEFT).wait_recv()
            add(acc.at[t, me], 0, rows, got_line.at[1, t])

        @pl.when(z < t)
        def _():
            c(R_RIGHT).start()

        @pl.when(z > t)
        def _():
            c(R_LEFT).start()

    def finish():
        out[...] = acc[z, me].astype(F32)
        for s in range(parts):
            t, c = unit(s), copies(s)
            for kind in range(R_RIGHT):
                c(kind).wait_send()

            @pl.when(z < t)
            def _():
                c(R_RIGHT).wait_send()

            @pl.when(z > t)
            def _():
                c(R_LEFT).wait_send()

    order = [(cores, 0), (cores, 1), (cores, 2), (chips, 0), (cores, 3), (chips, 1), (line, 0), (chips, 2), (line, 1),
             (chips, 3), (line, 2), (line, 3)]
    return [begin] + [functools.partial(f, s) for f, s in order] + [finish]


def parts_of(v, count):
    out = []
    for _ in range(count):
        out.append(v.astype(BF16))
        v = v - out[-1].astype(F32)
    return out


def group_table(width, groups):
    low = lax.broadcasted_iota(jnp.int32, (width, groups), 1) * (width // groups)
    at = lax.broadcasted_iota(jnp.int32, (width, groups), 0)
    return ((at >= low) & (at < low + width // groups)).astype(BF16)


def add_rows(target, source, other, count, columns):
    def some(i, carry):
        here = pl.ds(pl.multiple_of(i * 32, 32), 32)
        target[here, :] = (source[here, :].astype(F32) + other[here, :].astype(F32)).astype(BF16)
        return carry

    lax.fori_loop(0, count // 32 if count % 32 == 0 else 0, some, 0)
    if count % 32:
        target[...] = (source[...].astype(F32) + other[...].astype(F32)).astype(BF16)


def end_kernel(
    bits, parts, replicas, per_tile, hops, x_ref, mean_ref, rho_ref, count_ref, gain_ref, own_ref, ema_ref, back0_ref,
    back1_ref, res_ref, segc_ref, segr_ref, next_ref, block_ref, *refs
):
    pieces, (ffn_ref, in_ref), outs, (own_sum_ref, ffn_sum_ref), scratch = (
        refs[:6], refs[6:8], refs[8:15], refs[15:17], refs[17:]
    )
    (gh, cen, rf, backed, head, head_got, total, acc, cube, buf, cbuf, summed, chain, chain_got,
     sems, head_sems, chain_sems) = scratch
    d, z = lax.axis_index("dp"), lax.axis_index("tensor")
    MESH = pl.DeviceIdType.MESH
    rows, width = x_ref.shape
    groups = mean_ref.shape[1]
    tiles = width // LANES
    greet(parts, sum(axis == "dp" for axis, _ in bits))

    far = z // (parts // 2)
    near_end = z + far * (parts - 1 - 2 * z)

    def unit(s):
        t = (parts - 1 - s) + near_end * ((3, 0, 2, 1)[s] - (parts - 1 - s))
        return t + far * (parts - 1 - 2 * t)

    def line_copy(s, side):
        t = unit(s)
        to = jnp.clip(z + (1 if side == 0 else -1), 0, parts - 1)
        return pltpu.make_async_remote_copy(
            src_ref=chain.at[t], dst_ref=chain_got.at[side, t], send_sem=chain_sems.at[0, side, t],
            recv_sem=chain_sems.at[1, side, t], device_id=(d, to), device_id_type=MESH,
        )

    def along(s):
        t = unit(s)
        span, columns = chain.shape[1:]
        from_left, from_right = (z <= t) & (z > 0), (z >= t) & (z < parts - 1)

        @pl.when(from_left)
        def _():
            line_copy(s, 0).wait_recv()
            add_rows(chain.at[t], ffn_ref.at[t], chain_got.at[0, t], span, columns)

        @pl.when(jnp.logical_not(from_left))
        def _():
            chain[t] = ffn_ref[t]

        @pl.when(from_right)
        def _():
            line_copy(s, 1).wait_recv()
            add_rows(chain.at[t], chain.at[t], chain_got.at[1, t], span, columns)

        @pl.when(z < t)
        def _():
            line_copy(s, 0).start()

        @pl.when(z > t)
        def _():
            line_copy(s, 1).start()

    def mine(axis, k):
        return ((d if axis == "dp" else z) // (1 << k)) % 2

    def partner(axis, k):
        step = (1 - 2 * mine(axis, k)) * (1 << k)
        return (d + step, z) if axis == "dp" else (d, z + step)

    def copy(n, which, src, dst):
        return pltpu.make_async_remote_copy(
            src_ref=src, dst_ref=dst, send_sem=sems.at[0, which, n], recv_sem=sems.at[1, which, n],
            device_id=partner(*bits[n]), device_id_type=MESH,
        )

    plan = []
    start, length, cstart, clength, at, cat = 0, acc.shape[0], 0, cube.shape[0], 0, 0
    for axis, k in bits:
        half = length // 2
        keep = pl.multiple_of(start + mine(axis, k) * half, 8)
        give = pl.multiple_of(start + (1 - mine(axis, k)) * half, 8)
        if axis == "dp":
            chalf = clength // 2
            ckeep = pl.multiple_of(cstart + mine(axis, k) * chalf, 16)
            cgive = pl.multiple_of(cstart + (1 - mine(axis, k)) * chalf, 16)
        else:
            chalf, ckeep, cgive = clength, cstart, cstart
        plan.append((start, length, half, keep, give, chalf, ckeep, cgive, at, cat))
        start, length, cstart, clength = keep, half, ckeep, chalf
        at, cat = at + half, cat + chalf

    def exchange(n):
        _, _, half, _, give, chalf, _, cgive, at, cat = plan[n]
        return (copy(n, 0, acc.at[pl.ds(give, half)], buf.at[pl.ds(at, half)]),
                copy(n, 1, cube.at[pl.ds(cgive, chalf)], cbuf.at[pl.ds(cat, chalf)]))

    def send(n):
        for c in exchange(n):
            c.start()

    def receive(n):
        for c in exchange(n):
            c.wait()
        _, _, half, keep, _, chalf, ckeep, _, at, cat = plan[n]
        acc[pl.ds(keep, half)] += buf[pl.ds(at, half)]
        both = cube[pl.ds(ckeep, chalf)].astype(F32) + cbuf[pl.ds(cat, chalf)].astype(F32)
        cube[pl.ds(ckeep, chalf)] = both.astype(BF16)

    along(0)

    table = group_table(width, groups)
    spread_of = lambda v: sum(dot32(p, table, NT) for p in parts_of(v, 3))
    sums_of = lambda v: sum(dot32(p, table) for p in parts_of(v, 2))
    gh[...] = own_ref[...] + ema_ref[...] + back0_ref[...].astype(F32)
    gh[rows - hops[1] :, :] += back1_ref[...].astype(F32)
    mean, rho, count = mean_ref[...], rho_ref[...], count_ref[...]
    rf[...] = spread_of(rho)
    cen[...] = x_ref[...].astype(F32) - spread_of(mean)
    gain_grad = jnp.sum(cen[...] * rf[...] * gh[...], axis=0, keepdims=True)
    last_rows = jnp.zeros((per_tile - sum(p.shape[0] for p in pieces) - 1, LANES), F32)
    for tile in range(tiles):
        lanes = slice(tile * LANES, (tile + 1) * LANES)
        row = tile * per_tile
        for p in pieces:
            acc[row : row + p.shape[0], :] = p[:, lanes]
            row += p.shape[0]
        acc[row : row + 1, :] = gain_grad[:, lanes]
        acc[row + 1 : (tile + 1) * per_tile, :] = last_rows
    depth = block_ref.shape[0] // replicas
    levels = replicas.bit_length() - 1
    for b in range(replicas):
        m = sum(((b >> k) & 1) << (levels - 1 - k) for k in range(levels))
        cube[m * depth : (m + 1) * depth, :] = block_ref[b * depth : (b + 1) * depth, :].astype(BF16)
    send(0)

    gh[...] = gh[...] * gain_ref[...]
    sum_a, sum_b = rho * sums_of(gh[...]), sums_of(gh[...] * cen[...])
    third = sum_b * rho * rho * rho
    lower = (segc_ref[...] == segr_ref[...]) & (
        lax.broadcasted_iota(jnp.int32, (rows, rows), 0) >= lax.broadcasted_iota(jnp.int32, (rows, rows), 1)
    )
    lower = lower.astype(F32).astype(BF16)
    back = lambda v: sum(dot32(lower, p, TN) for p in parts_of(v, 3))
    backed[0] = back((third * mean - sum_a) / count)
    backed[1] = back(-third / (2.0 * count))
    for half in range(2):
        head[half, :, :groups] = backed[half, 0:8, :]
    to_heads = [Along(parts, -hop, head, head_got.at[hop - 1], head_sems.at[0, hop - 1], head_sems.at[1, hop - 1])
                for hop in (1, 2)]
    for move in to_heads:
        move.start()
    receive(0)
    send(1)
    along(1)
    total[...] = jnp.zeros_like(total)
    for hop, move in enumerate(to_heads):
        def arrived(hop=hop):
            total[...] += next_ref[hop : hop + 1, :] * head_got[hop]
        move.wait_recv(arrived)
    tails = (segc_ref[...] == segc_ref[rows - 1 : rows, :]).astype(F32)
    first, second = (backed[half] + tails * total[half, 0:1, :groups] for half in range(2))
    in_ref[...] = res_ref[...] + gh[...] * rf[...] + spread_of(first) + 2.0 * x_ref[...].astype(F32) * spread_of(second)

    for n in range(1, len(bits)):
        receive(n)
        if n + 1 < len(bits):
            send(n + 1)
        if n + 1 < parts:
            along(n + 1)
    clast = pl.multiple_of(plan[-1][6], 16)
    own_sum_ref[...] = cube[pl.ds(clast, clength)].astype(F32)
    summed[pl.ds(start, length)] = acc[pl.ds(start, length)]
    for n in reversed(range(len(bits))):
        here = summed.at[pl.ds(start, length)]
        copy(n, 2, here, here).start()
        copy(n, 2, here, here).wait()
        start, length = plan[n][:2]
    for tile in range(tiles):
        lanes = slice(tile * LANES, (tile + 1) * LANES)
        row = tile * per_tile
        for out in outs:
            out[:, lanes] = summed[row : row + out.shape[0], :]
            row += out.shape[0]
    ffn_sum_ref[...] = chain[z].astype(F32)
    for s in range(parts):
        @pl.when(z < unit(s))
        def _():
            line_copy(s, 0).wait_send()

        @pl.when(z > unit(s))
        def _():
            line_copy(s, 1).wait_send()
    for move in to_heads:
        move.wait_send()


def end_call(replicas, parts, hops, per_row, pieces, ffn):
    bits = [("dp", k) for k in range(replicas.bit_length() - 1)]
    bits += [("tensor", k) for k in range(parts.bit_length() - 1)]
    x, block = per_row[0], per_row[-1]
    rows, width = x.shape
    tiles = width // LANES
    wanted = tiles * (sum(p.shape[0] for p in pieces) + 1)
    unit = max(replicas * parts * 8, tiles * 8)
    per_tile = -(-wanted // unit) * unit // tiles
    small = (tiles * per_tile, LANES)
    own = block.shape[0] // replicas
    got = sum(block.shape[0] >> (k + 1) for k in range(replicas.bit_length() - 1))
    got += own * (parts.bit_length() - 1)
    groups = per_row[1].shape[1]
    vm = pltpu.VMEM
    dma = lambda *n: pltpu.SemaphoreType.DMA(n)
    shape = jax.ShapeDtypeStruct
    ins = (*per_row, *pieces, ffn)
    outs = ([shape((rows, width), F32)] + [shape(p.shape, F32) for p in pieces]
            + [shape((1, width), F32), shape((own, block.shape[1]), F32), shape(ffn.shape[1:], F32)])
    return pl.pallas_call(
        functools.partial(end_kernel, bits, parts, replicas, per_tile, hops),
        in_specs=[pl.BlockSpec(memory_space=vm)] * len(ins),
        out_specs=[pl.BlockSpec(memory_space=vm)] * len(outs),
        out_shape=outs,
        scratch_shapes=[
            vm((rows, width), F32), vm((rows, width), F32), vm((rows, width), F32), vm((2, rows, groups), F32),
            vm((2, 8, LANES), F32), vm((2, 2, 8, LANES), F32), vm((2, 8, LANES), F32), vm(small, F32),
            vm(block.shape, BF16), vm(small, F32), vm((got, block.shape[1]), BF16), vm(small, F32),
            vm(ffn.shape, BF16), vm((2,) + ffn.shape, BF16), dma(2, 3, len(bits)), dma(2, 2), dma(2, 2, parts),
        ],
        compiler_params=pltpu.CompilerParams(collective_id=0, has_side_effects=True, vmem_limit_bytes=60 << 20),
        name="ending",
    )(*ins)


def on_device(
    block_in, segments, norm_gain, ema_rate, ema_angle, ema_input, ema_output, ema_skip, w_shared, query_gain,
    query_bias, key_gain, w_value, w_gate, w_out, ffn_gain, w_swish, w_up, w_down, out_grad,
):
    parts = lax.axis_size("tensor")
    replicas = lax.axis_size("dp")
    rank = lax.axis_index("tensor")
    rows, width = block_in.shape
    dims = ema_rate.shape[0]
    length = segments.shape[1]
    groups = TN_GROUPS
    span = width // groups
    latent_width = w_shared.shape[1]
    value_width = w_value.shape[1] * parts
    ffn_width = w_swish.shape[1] * parts
    depth = w_value.shape[0]
    halo = -(-REACH // LANES) * LANES
    hops = [min(rows, REACH - h * rows) for h in range(-(-REACH // rows))]

    def from_earlier(x, hop):
        return lax.ppermute(x, "tensor", [(i, i + hop) for i in range(parts - hop)])

    def from_later(x, hop):
        return lax.ppermute(x, "tensor", [(i + hop, i) for i in range(parts - hop)])

    def halo_of(x):
        pieces = [from_earlier(x[rows - n :], h + 1) for h, n in enumerate(hops)]
        ahead = jnp.zeros((halo - sum(hops), x.shape[1]), x.dtype)
        return jnp.concatenate([ahead] + pieces[::-1] + [x], axis=0)

    def give_back(total, x):
        end = halo
        for h, n in enumerate(hops):
            got = from_later(x[end - n : end], h + 1).astype(F32)
            total = total.at[rows - n :].add(got)
            end -= n
        return total

    chip_links = replicas == 8 and parts == 4

    piece = depth // parts
    shared_piece = lax.dynamic_slice_in_dim(w_shared, rank * piece, piece, 0)
    low = lambda w: w.astype(BF16)
    vw, fw = value_width // parts, ffn_width // parts
    pack_a = jnp.concatenate(
        [low(w_value), low(w_gate), low(w_out.T), low(shared_piece).reshape(-1, vw)], axis=0
    )
    pack_f1 = low(w_swish)
    pack_f2 = jnp.concatenate([low(w_up), low(w_down.T)], axis=0)
    gathered = lambda v: lax.all_gather(v, BOTH, axis=0).reshape(replicas, parts, *v.shape)
    all_f1 = gathered(pack_f1)
    pack_f2 = with_layout_constraint(pack_f2, Layout((0, 1)))

    def part(k, columns):
        return pl.BlockSpec((replicas, 1, depth, columns), lambda t: (0, t, k, 0))

    seg_all = segments[0]
    padded = jnp.concatenate([jnp.full((halo,), -1, jnp.int32), seg_all, jnp.full((halo,), -2, jnp.int32)])
    near = lax.dynamic_slice_in_dim(padded, rank * rows, halo + rows + halo, 0)
    seg_keys = near[: halo + rows]
    seg = near[halo : halo + rows]
    before = near[halo - 1]
    masks = row_masks(seg, before)
    index = rank * rows + jnp.arange(rows, dtype=jnp.int32)
    start = jnp.sum((seg_all[None, :] < seg[:, None]).astype(jnp.int32), axis=1)
    count = (index - start + 1).astype(F32)[:, None] * span
    tri = jnp.arange(rows)
    same = seg[:, None] == seg[None, :]
    lower = (same & (tri[:, None] >= tri[None, :])).astype(F32)
    link1 = (seg[0] == before).astype(F32)
    link2 = (before == near[halo - rows - 1]).astype(F32)
    last = seg[-1]
    next1 = (near[halo + rows] == last).astype(F32)
    next2 = ((near[halo + 2 * rows - 1] == last) & (near[halo + 2 * rows] == last)).astype(F32) if halo > rows else 0.0
    heads = (seg == before).astype(F32)[:, None]
    tails = (seg == last).astype(F32)[:, None]

    x = block_in.astype(F32)
    gather = (jnp.arange(width)[:, None] // span == jnp.arange(groups)[None, :]).astype(F32)
    sums_of = lambda v: dot32(v, gather, precision=HIGHEST)
    spread_of = lambda v: dot32(v, gather, NT, precision=HIGHEST)
    sums = jnp.concatenate([dot32(block_in, gather.astype(BF16)), sums_of(x * x)], axis=1)
    running = dot32(lower, sums, precision=HIGHEST)
    tail = running[-1:]
    carry = from_earlier(tail, 1) + link2 * from_earlier(tail, 2)
    running = running + heads * carry
    mean = running[:, :groups] / count
    var = running[:, groups:] / count - mean * mean
    rho = lax.rsqrt(var + EPSILON)
    mean_full, rho_full = spread_of(mean), spread_of(rho)
    centred = (x - mean_full) * rho_full
    hidden = centred * norm_gain
    hidden_b = low(hidden)

    size = jnp.exp(-ema_rate)
    unit = jnp.concatenate([size * jnp.cos(ema_angle), size * jnp.sin(ema_angle)])
    root = jnp.sqrt(1.0 - size * size)
    feed = ema_input * root
    reads = ema_output.reshape(2 * dims, width)
    skip = ema_skip[None]
    gcount = rows // (8 * STEP)
    nstate = gcount * dims * 2
    at_rows = gcount * STEP
    blocks = width // LANES
    col = lambda n: pl.BlockSpec((n, LANES), lambda i: (0, i % blocks))
    late = lambda n: pl.BlockSpec((n, LANES), lambda i: (0, jnp.maximum(i - blocks, 0)))
    late3 = lambda n, m: pl.BlockSpec((n, m, LANES), lambda i: (0, 0, jnp.maximum(i - blocks, 0)))
    anywhere = pl.BlockSpec(memory_space=pl.ANY)
    shape_of = jax.ShapeDtypeStruct
    mask_spec = whole(at_rows, 8, LANES)
    cont, mk, mkr = (
        (masks["cont"], whole(gcount, 8, LANES)), (masks["mk"], whole(3, 8, LANES)), (masks["mkr"], whole(3, 8, LANES))
    )
    kend, keep0, seg8 = ((masks[k], mask_spec) for k in ("kend", "keep0", "seg"))
    lane = lambda v: (jnp.full((1, LANES), v, F32), whole(1, LANES))
    vm = lambda *n: pltpu.VMEM((*n, 8, LANES), F32)
    flat_vm = lambda *n: pltpu.VMEM((*n, LANES), F32)
    dma = lambda *n: pltpu.SemaphoreType.DMA(n)
    table_vm, scale_vm = flat_vm(2, STEP * dims), flat_vm(8 * dims)
    state_vms = [vm(blocks, nstate), flat_vm(blocks, 2 * dims), flat_vm(2, blocks, 2 * dims), flat_vm(2 * dims),
                 dma(2, 2, blocks), dma(2, 2), dma(4)]
    mac = rows * width * dims * 4
    zeros = (jnp.zeros((rows, width), BF16), anywhere)
    near_rows = halo + rows
    results = ema_call(
        functools.partial(ema_forward, rows, dims, parts, halo, hops, chip_links), width,
        [(hidden, col(rows)), kend, seg8, keep0, (unit, col(2 * dims)), (feed, col(dims)), (reads, col(2 * dims)), cont,
         mk, lane(link2), (skip, col(1)), (hidden_b, anywhere), zeros] + [(pack_a, anywhere)] * chip_links,
        [(shape_of((rows, width), F32), late(rows)), (shape_of((rows, width), BF16), late(rows)),
         (shape_of((nstate, 8, width), F32), late3(nstate, 8)), (shape_of((near_rows, width), BF16), anywhere)]
        + [(shape_of((replicas, parts) + pack_a.shape, BF16), anywhere)] * chip_links,
        [vm(2 * at_rows), table_vm, scale_vm] + state_vms + (gather_scratch(parts) if chip_links else []),
        "ema_forward", 2 * mac, 3,
    )
    ema_out, mixed, states, hidden_near = results[:4]
    all_a = results[-1] if chip_links else gathered(pack_a)
    shared_b = all_a[:, :, 3 * depth :].reshape(width, latent_width)

    latent = dot32(mixed, shared_b)
    queries = low(latent * query_gain + query_bias)
    keys_near = halo_of(low(latent * key_gain))
    one = lambda v: v[None]
    matmul = rows * width * vw * 2 * parts
    col_v = lambda n: ((n, value_width), BF16, "col")
    ins = [(queries, "all"), (keys_near, "all"), (seg[:, None], "all"), (one(seg_keys), "all"), (hidden_near, "all"),
           (mixed, "all"), (block_in, "all"), (one(ffn_gain), "all"), (all_a, part(0, vw)), (all_a, part(1, vw)),
           (all_a, part(2, vw))]
    outs = [((rows, near_rows), F32, "all"), col_v(near_rows), col_v(near_rows), col_v(rows), col_v(rows), col_v(rows),
            ((rows, width), F32, "all"), ((rows, width), BF16, "all")]
    scratch = [pltpu.VMEM((rows, near_rows), BF16)]
    if chip_links:
        results = stage_call(
            functools.partial(attend_gather_kernel, halo, parts, len(ins), len(outs)), parts,
            ins + [(pack_f2, anywhere)], outs + [((replicas, parts) + pack_f2.shape, BF16, anywhere)],
            scratch + gather_scratch(parts), "attend", 6 * matmul, collective_id=1,
        )
        all_f2 = results[-1]
    else:
        results = stage_call(functools.partial(attend_kernel, halo), parts, ins, outs, scratch, "attend", 6 * matmul)
        all_f2 = gathered(pack_f2)
    probs, value_pre, values, gate_pre, attended, gated, residual, norm_in = results[:8]

    row_vm = lambda n: pltpu.VMEM((n, width), F32)
    block_out, grad_residual, branch, grad_ffn_gain, ffn_grads = stage_call(
        ffn_kernel, parts,
        [(residual, "all"), (norm_in, "all"), (out_grad, "all"), (one(ffn_gain), "all"), (all_f1, part(0, fw)),
         (all_f2, part(0, fw)), (all_f2, part(1, fw))],
        [((rows, width), BF16, "all"), ((rows, width), F32, "all"), ((rows, width), BF16, "all"),
         ((1, width), F32, "all"),
         ((replicas, parts, 3, depth, fw), BF16,
          pl.BlockSpec((replicas, 1, 3, depth, fw), lambda t: (0, t, 0, 0, 0)))],
        [row_vm(rows), row_vm(rows)], "ffn", 11 * matmul,
    )

    def summed(g):
        g = g.reshape(replicas, parts, -1, g.shape[-1])
        return lax.psum_scatter(g, "dp", scatter_dimension=0, tiled=False)

    def summed_along(g, after):
        g = lax.optimization_barrier((g, after))[0]
        return lax.psum_scatter(g, "tensor", scatter_dimension=0, tiled=False).astype(F32)

    ffn_sum = summed(ffn_grads)

    grad_queries, keys_back, keys_own, hidden_back, hidden_own, grad_mixed, attn_grads = stage_call(
        functools.partial(attend_back_kernel, halo), parts,
        [(branch, "all"), (probs, "all"), (hidden_near, "all"), (mixed, "all"), (queries, "all"), (keys_near, "all"),
         (value_pre, "col"), (values, "col"), (gate_pre, "col"), (attended, "col"), (gated, "col"),
         (all_a, part(0, vw)), (all_a, part(1, vw)), (all_a, part(2, vw))],
        [((rows, latent_width), F32, "all"), ((halo, latent_width), BF16, "all"), ((rows, latent_width), F32, "all"),
         ((halo, width), BF16, "all"), ((rows, width), F32, "all"), ((rows, width), F32, "all"),
         ((replicas, parts, 3, depth, vw), BF16,
          pl.BlockSpec((replicas, 1, 3, depth, vw), lambda t: (0, t, 0, 0, 0)))],
        [pltpu.VMEM((rows, near_rows), F32), row_vm(near_rows), pltpu.VMEM((rows, near_rows), BF16)], "attend_back", 12 * matmul,
    )
    grad_keys = give_back(keys_own, keys_back)
    grad_query_gain = jnp.sum(latent * grad_queries, axis=0)
    grad_query_bias = jnp.sum(grad_queries, axis=0)
    grad_key_gain = jnp.sum(latent * grad_keys, axis=0)
    grad_latent = low(grad_queries * query_gain + grad_keys * key_gain)
    grad_shared = dot32(mixed, grad_latent, TN)
    grad_ema = (dot32(grad_latent, shared_b, NT) + grad_mixed) * silu_slope(ema_out)

    cross = (near[halo + 2 * rows - 1] == last).astype(F32)
    dim_late = late(dims)
    results = ema_call(
        functools.partial(ema_backward, rows, dims, parts, halo, hops, chip_links), width,
        [(hidden, late(rows)), (grad_ema, col(rows)), seg8, kend, keep0, (masks["rk0"], whole(rows, LANES)),
         (masks["rkend"], whole(rows, LANES)), (unit, col(2 * dims)), (feed, dim_late), (reads, col(2 * dims)),
         (root, dim_late), (ema_input, dim_late), cont, mkr, (states, late3(nstate, 8)), lane(cross), (skip, late(1)),
         (hidden_back, anywhere), zeros]
        + [(attn_grads.reshape(replicas // 2, 2, parts, 3 * depth, vw), anywhere)] * chip_links,
        [(shape_of((rows, width), F32), late(rows)), (shape_of((2 * dims, width), F32), late(2 * dims))]
        + [(shape_of((dims, width), F32), dim_late)] * 3 + [(shape_of((1, width), F32), late(1))]
        + [(shape_of((n, width), BF16), anywhere) for n in hops]
        + [(shape_of((3 * depth, vw), F32), whole(3 * depth, vw))] * chip_links,
        state_vms + [vm(2 * at_rows), vm(at_rows), vm(nstate), table_vm, scale_vm, flat_vm(4, STEP * dims),
                     flat_vm(9, dims), flat_vm(rows), flat_vm(rows)]
        + (reduce_scratch(parts, 3 * depth, vw) if chip_links else []),
        "ema_backward", 4 * mac, 2,
    )
    grad_hidden_ema, output_grad, input_grad, rate_grad, angle_grad, grad_skip = results[:6]
    attn_sum = results[-1] if chip_links else summed_along(summed(attn_grads), grad_skip)
    zero = jnp.zeros((1, width - 3 * latent_width), F32)
    latents = jnp.concatenate([grad_query_gain[None], grad_query_bias[None], grad_key_gain[None], zero], axis=1)
    nexts = jnp.stack([next1, jnp.asarray(next2, F32)])[:, None] * jnp.ones((1, LANES), F32)
    results = end_call(
        replicas, parts, hops,
        (block_in, mean, rho, count, norm_gain[None], hidden_own, grad_hidden_ema, results[6], results[7],
         grad_residual, seg[:, None], seg[None], nexts, grad_shared),
        (output_grad, input_grad, rate_grad, angle_grad, grad_skip,
         jnp.concatenate([grad_ffn_gain, latents], axis=0)),
        ffn_sum,
    )
    in_grad, output_grad, input_grad, rate_grad, angle_grad, skip_grad, two, gain_grad, shared_sum, ffn_sum = results
    latents = two[1].reshape(-1, latent_width)

    cut = lambda g, k: g[k * depth : (k + 1) * depth]
    return (
        block_out, in_grad, gain_grad[0], rate_grad, angle_grad, input_grad, output_grad.reshape(ema_output.shape),
        skip_grad[0], shared_sum, latents[0], latents[1], latents[2], cut(attn_sum, 0), cut(attn_sum, 1),
        cut(attn_sum, 2).T, two[0], cut(ffn_sum, 0), cut(ffn_sum, 1), cut(ffn_sum, 2).T,
    )


def solution(mesh):
    rows, dp, copy = P(BOTH, None), P("dp", None), P()
    wide, tall = P("dp", "tensor"), P("tensor", "dp")
    return jax.shard_map(
        on_device,
        mesh=mesh,
        in_specs=(
            rows, dp, copy, copy, copy, copy, copy, copy, dp, copy, copy, copy, wide, wide, tall, copy, wide, wide,
            tall, rows,
        ),
        out_specs=(
            rows, rows, copy, copy, copy, copy, copy, copy, dp, copy, copy, copy, wide, wide, tall, copy, wide, wide,
            tall,
        ),
        check_vma=False,
    )
```

```python
import functools
import math

import jax
import jax.numpy as jnp
from jax import lax
from jax.experimental import pallas as pl
from jax.experimental.pallas import tpu as pltpu
from jax.experimental.layout import Layout, with_layout_constraint
from jax.sharding import PartitionSpec as P

TN_GROUPS = 16
EPSILON = 1e-05
REACH = 800
STEP = 16
LANES = 128
F32 = jnp.float32
BF16 = jnp.bfloat16
HIGHEST = lax.Precision.HIGHEST
BOTH = ("dp", "tensor")


def dot32(a, b, dims=((1,), (0,)), precision=None):
    return lax.dot_general(a, b, (dims, ((), ())), precision=precision, preferred_element_type=F32)


NT = ((1,), (1,))
TN = ((0,), (0,))


def silu_of(v):
    return v * jax.nn.sigmoid(v)


def silu_slope(v):
    sg = jax.nn.sigmoid(v)
    return sg * (1.0 + v * (1.0 - sg))


def broadcast_row(ref, row):
    return ref[pl.ds(row, 8, stride=0), :]


def rotate(x, shift):
    return pltpu.roll(x, shift % 8, axis=0)


def times(ar, ai, br, bi):
    return ar * br - ai * bi, ar * bi + ai * br


def power_list(dims, q_ref):
    qr, qi = q_ref[:dims], q_ref[dims:]
    out = [(jnp.ones_like(qr), jnp.zeros_like(qr))]
    for n in range(STEP):
        out.append(times(*out[-1], qr, qi))
    return out


def fill_scales(groups, dims, pw, qs):
    step = pw[STEP]
    qs[:dims], qs[dims : 2 * dims] = step
    turn = step
    for _ in range(groups - 1):
        turn = times(*turn, *step)
    for k in range(3):
        base = 2 * dims * (k + 1)
        qs[base : base + dims], qs[base + dims : base + 2 * dims] = turn
        turn = times(*turn, *turn)
    return turn


def fill_read(dims, pw, e_ref, ta):
    e0, e1 = e_ref[:dims], e_ref[dims:]
    for i in range(STEP):
        ta[0, i * dims : (i + 1) * dims], ta[1, i * dims : (i + 1) * dims] = times(e0, e1, *pw[i + 1])


def fill_feed(dims, pw, f_ref, tb):
    f = f_ref[...]
    for i in range(STEP):
        r, m = pw[STEP - 1 - i]
        tb[0, i * dims : (i + 1) * dims], tb[1, i * dims : (i + 1) * dims] = f * r, f * m


def tap_list(dims, pw, e_ref, f_ref):
    e0, e1, f = e_ref[:dims], e_ref[dims:], f_ref[...]
    out = []
    for d in range(STEP):
        row = jnp.sum(f * (e0 * pw[d][0] - e1 * pw[d][1]), axis=0, keepdims=True)
        out.append(jnp.broadcast_to(row, (8, LANES)))
    return out


def chunk_sums(groups, dims, table, source, out, sign):
    def pair(jp, carry):
        acc = [None] * groups
        for i in range(STEP):
            c = [broadcast_row(table.at[p], i * dims + jp * 2 + k) for k in range(2) for p in range(2)]
            for g in range(groups):
                h = source[g * STEP + i]
                terms = [v * h for v in c]
                acc[g] = terms if i == 0 else [u + v for u, v in zip(acc[g], terms)]
        for g in range(groups):
            for k in range(2):
                at = (g * dims + jp * 2 + k) * 2
                out[at] = acc[g][2 * k]
                out[at + 1] = acc[g][2 * k + 1] if sign > 0 else -acc[g][2 * k + 1]
        return carry

    lax.fori_loop(0, dims // 2, pair, 0)


def position_sums(groups, dims, table, states, mask, out, base, sign):
    block = 4

    def some(iq, carry):
        acc = [[None] * block for _ in range(groups)]
        for j in range(dims):
            here = [(states[(g * dims + j) * 2], states[(g * dims + j) * 2 + 1]) for g in range(groups)]
            for i in range(block):
                cr = broadcast_row(table.at[0], (iq * block + i) * dims + j)
                ci = broadcast_row(table.at[1], (iq * block + i) * dims + j)
                for g in range(groups):
                    u, v = cr * here[g][0], ci * here[g][1]
                    term = u - v if sign < 0 else u + v
                    acc[g][i] = term if j == 0 else acc[g][i] + term
        for g in range(groups):
            for i in range(block):
                at = g * STEP + iq * block + i
                out[base + at] = acc[g][i] * mask[at]
        return carry

    lax.fori_loop(0, STEP // block, some, 0)


def scan_states(groups, dims, j, l_ref, qs, cont_ref, mk_ref, inr, ini):
    qr, qi = broadcast_row(qs, j), broadcast_row(qs, dims + j)
    part = [(l_ref[(g * dims + j) * 2], l_ref[(g * dims + j) * 2 + 1]) for g in range(groups)]

    def through(sr, si):
        starts = []
        for g in range(groups):
            starts.append((sr, si))
            keep = cont_ref[g]
            tr, ti = times(qr, qi, sr, si)
            sr, si = keep * tr + part[g][0], keep * ti + part[g][1]
        return starts, sr, si

    _, er, ei = through(inr, ini)
    for k in range(3):
        base = 2 * dims * (k + 1)
        wr, wi = broadcast_row(qs, base + j), broadcast_row(qs, base + dims + j)
        pr, pi = times(wr, wi, rotate(er, 1 << k), rotate(ei, 1 << k))
        keep = mk_ref[k]
        er, ei = er + keep * pr, ei + keep * pi
    first = lax.broadcasted_iota(jnp.int32, (8, LANES), 0) == 0
    starts, _, _ = through(jnp.where(first, inr, rotate(er, 1)), jnp.where(first, ini, rotate(ei, 1)))
    return starts, (er, ei)


def fill_masks(groups, seg_ref, before, seg, kend, keep0, cont, ahead, reverse):
    sub = lax.broadcasted_iota(jnp.int32, (8, LANES), 0)
    for at in range(groups * STEP):
        seg[at] = seg_ref[pl.ds(at, 8, stride=groups * STEP), :]
    ends = [seg[g * STEP + STEP - 1] for g in range(groups)]
    start = jnp.where(sub == 0, before, rotate(ends[-1], 1))
    prior = [start] + ends[:-1]
    same = lambda a, b: (a == b).astype(F32)
    for g in range(groups):
        cont[g] = same(ends[g], prior[g])
        for i in range(STEP):
            here = seg[g * STEP + i]
            keep0[g * STEP + i] = same(here, prior[g])
            kend[g * STEP + i] = same(here, ends[g])
    for k in range(3):
        w = 1 << k
        if reverse:
            ahead[k] = jnp.where(sub + w <= 7, same(start, rotate(start, -w)), 0.0)
        else:
            ahead[k] = jnp.where(sub >= w, same(ends[-1], rotate(ends[-1], w)), 0.0)


ENTER_PLAN = (
    (0, 2, False), (8, 1, False), (9, 1, False), (10, 1, False), (11, 2, False), (12, 1, False), (13, 1, False),
    (14, 2, False), (15, 0, True),
)


def shifted_rows(parts, halo, hops, rows, source, near, zeros, sems, local_sems):
    z = lax.axis_index("tensor")
    late = hops[1]
    early = rows - late
    cut = halo - late
    move = lambda n, src, at, count, first: Along(
        parts, 1, src, near.at[pl.ds(at, count)], sems.at[0, n], sems.at[1, n], first
    )
    last = move(0, source.at[pl.ds(early, late)], cut, late, 0)
    other = move(1, source.at[pl.ds(0, early)], halo - rows, early, 0)
    onward = move(2, near.at[pl.ds(cut, late)], halo - rows - late, late, 1)
    ahead = halo - rows - late
    fills = [(z < 1, rows, halo - rows), (z < 2, late, ahead)]
    if ahead > 0:
        fills.append((z < parts, ahead, 0))

    def each(action):
        action(pltpu.make_async_copy(source, near.at[pl.ds(halo, rows)], local_sems.at[3]))
        for n, (condition, count, at) in enumerate(fills):
            @pl.when(condition)
            def _():
                action(pltpu.make_async_copy(zeros.at[pl.ds(0, count)], near.at[pl.ds(at, count)], local_sems.at[n]))

    def begin():
        last.start()
        each(lambda c: c.start())

    def relay():
        last.wait_recv()
        onward.start()

    def wait():
        other.wait_recv()
        onward.wait_recv()
        for one in (last, other, onward):
            one.wait_send()
        each(lambda c: c.wait())

    return begin, other.start, relay, wait


def normalize(
    parts, x_ref, gain_ref, seg_ref, segc_ref, segr_ref, count_ref, edge_ref, mean_ref, rho_ref, hid, low, tail,
    tail_got, tail_total, tail_sems
):
    rows, width = x_ref.shape
    groups = mean_ref.shape[1]
    table = group_table(width, groups)
    spread_of = lambda v: sum(dot32(p, table, NT) for p in parts_of(v, 3))
    lower = (segc_ref[...] == segr_ref[...]) & (
        lax.broadcasted_iota(jnp.int32, (rows, rows), 0) >= lax.broadcasted_iota(jnp.int32, (rows, rows), 1)
    )
    lower = lower.astype(F32).astype(BF16)
    running_of = lambda v: sum(dot32(lower, p) for p in parts_of(v, 3))
    x = x_ref[...].astype(F32)
    running = [
        running_of(dot32(x_ref[...], table)),
        running_of(sum(dot32(p, table) for p in parts_of(x * x, 2))),
    ]
    for half in range(2):
        tail[half, :, :groups] = running[half][rows - 8 :]
    moves = [Along(parts, hop, tail, tail_got.at[hop - 1], tail_sems.at[0, hop - 1], tail_sems.at[1, hop - 1])
             for hop in (1, 2)]
    for move in moves:
        move.start()
    tail_total[...] = jnp.zeros_like(tail_total)
    for hop, move in enumerate(moves):
        def arrived(hop=hop):
            tail_total[...] += edge_ref[1 + hop : 2 + hop, :] * tail_got[hop]
        move.wait_recv(arrived)
    heads = (seg_ref[:, 0:1] == edge_ref[0:1, 0:1]).astype(F32)
    count = count_ref[...]
    first, second = (running[half] + heads * tail_total[half, 7:8, :groups] for half in range(2))
    mean = first / count
    rho = lax.rsqrt(second / count - mean * mean + EPSILON)
    mean_ref[...] = mean
    rho_ref[...] = rho
    hidden = (x - spread_of(mean)) * spread_of(rho) * gain_ref[...]
    low[...] = hidden.astype(BF16)
    for k in range(width // LANES):
        hid[k] = hidden[:, k * LANES : (k + 1) * LANES]
    for move in moves:
        move.wait_send()


def ema_forward(
    rows, dims, parts, halo, hops, hosted, x_ref, gain_ref, seg_ref, segc_ref, segr_ref, count_ref, edge_ref, q_ref,
    f_ref, e_ref, skip_ref, zeros_ref, *refs
):
    refs = list(refs)
    pack_ref = refs.pop(0) if hosted else None
    out_ref, m_ref, s_ref, hidden_ref, mean_ref, rho_ref, near_ref = (refs.pop(0) for _ in range(7))
    all_ref = refs.pop(0) if hosted else None
    hid, low, tail, tail_got, tail_total, tail_sems, seg, kend, keep0, cont, ahead = (refs.pop(0) for _ in range(11))
    hs, table, qs, parts_all, ends, got, entry, state_sems, near_sems, local_sems, *rest = refs
    groups = rows // (8 * STEP)
    step = pl.program_id(0)
    blocks = parts_all.shape[0]
    k = step % blocks
    stages = gather_stages(parts, pack_ref, all_ref, *rest) if hosted else []
    near_begin, near_more, near_relay, near_wait = shifted_rows(parts, halo, hops, rows, low, near_ref, zeros_ref, near_sems, local_sems)
    states = lambda hop, at: Along(
        parts, hop, ends.at[at], got.at[hop - 1, at], state_sems.at[0, hop - 1, at], state_sems.at[1, hop - 1, at]
    )

    @pl.when(step == 0)
    def _():
        greet(parts, 3 if hosted else 0)

    @pl.when(step == blocks)
    def _():
        near_more()

    @pl.when(step == blocks + 2)
    def _():
        near_relay()

    if hosted:
        run_stages(stages, step, ENTER_PLAN, False)

    @pl.when(step == 0)
    def _():
        normalize(
            parts, x_ref, gain_ref, seg_ref, segc_ref, segr_ref, count_ref, edge_ref, mean_ref, rho_ref, hid, low,
            tail, tail_got, tail_total, tail_sems,
        )
        near_begin()
        fill_masks(groups, seg_ref, edge_ref[0:1, :], seg, kend, keep0, cont, ahead, False)

    pw = power_list(dims, q_ref)
    turn = fill_scales(groups, dims, pw, qs)

    @pl.when(step < blocks)
    def _():
        fill_feed(dims, pw, f_ref, table)
        for at in range(groups * STEP):
            hs[at] = hid[k, pl.ds(at, 8, stride=groups * STEP), :] * kend[at]
        chunk_sums(groups, dims, table, hs, parts_all.at[k], 1)

        def one(j, carry):
            zero = jnp.zeros((8, LANES), F32)
            _, last = scan_states(groups, dims, j, parts_all.at[k], qs, cont, ahead, zero, zero)
            ends[k, pl.ds(j, 1), :] = last[0][7:8]
            ends[k, pl.ds(dims + j, 1), :] = last[1][7:8]
            return carry

        lax.fori_loop(0, dims, one, 0)
        for hop in (1, 2):
            states(hop, k).start()

    @pl.when(step >= blocks)
    def _():
        hidden_ref[...] = hid[k]
        entry[...] = jnp.zeros_like(entry)

        def near_one():
            entry[...] = got[0, k]

        def far_one():
            link = edge_ref[2:3, :]
            r, i = times(*turn, got[1, k, :dims], got[1, k, dims:])
            entry[:dims] += link * r
            entry[dims:] += link * i

        states(1, k).wait_recv(near_one)
        states(2, k).wait_recv(far_one)
        ema_read(
            groups, dims, hid.at[k], seg, keep0, pw, f_ref, e_ref, cont, ahead, parts_all.at[k], entry, skip_ref,
            out_ref, m_ref, s_ref, hs, table, qs,
        )

    @pl.when(step == 2 * blocks - 1)
    def _():
        for at in range(blocks):
            for hop in (1, 2):
                states(hop, at).wait_send()
        near_wait()

    if hosted:
        run_stages(stages, step, ENTER_PLAN, True)


def ema_read(
    groups, dims, h_ref, seg_ref, k0_ref, pw, f_ref, e_ref, cont_ref, mk_ref, l_ref, in_ref, skip_ref, out_ref, m_ref,
    s_ref, hs, ta, qs
):
    first = lax.broadcasted_iota(jnp.int32, (8, LANES), 0) == 0
    fill_read(dims, pw, e_ref, ta)
    taps = tap_list(dims, pw, e_ref, f_ref)

    def one(j, carry):
        inr = jnp.where(first, broadcast_row(in_ref, j), 0.0)
        ini = jnp.where(first, broadcast_row(in_ref, dims + j), 0.0)
        starts, _ = scan_states(groups, dims, j, l_ref, qs, cont_ref, mk_ref, inr, ini)
        for g in range(groups):
            s_ref[(g * dims + j) * 2] = starts[g][0]
            s_ref[(g * dims + j) * 2 + 1] = starts[g][1]
        return carry

    lax.fori_loop(0, dims, one, 0)
    for at in range(groups * STEP):
        hs[at] = h_ref[pl.ds(at, 8, stride=groups * STEP), :]
    position_sums(groups, dims, ta, s_ref, k0_ref, hs, groups * STEP, -1)
    tap0 = taps[0] + jnp.broadcast_to(skip_ref[...], (8, LANES))

    def within(g, carry):
        for i in range(STEP):
            at = g * STEP + i
            seg = seg_ref[at]
            out = hs[groups * STEP + at] + tap0 * hs[at]
            for s in range(i):
                src = g * STEP + s
                out = out + taps[i - s] * jnp.where(seg_ref[src] == seg, hs[src], 0.0)
            out_ref[pl.ds(at, 8, stride=groups * STEP), :] = out
        return carry

    lax.fori_loop(0, groups, within, 0)
    m_ref[...] = silu_of(out_ref[...]).astype(m_ref.dtype)


def reverse_states(groups, dims, j, g_ref, qs, cont_ref, mkr_ref, inr, ini):
    qr, qi = broadcast_row(qs, j), broadcast_row(qs, dims + j)
    part = [(g_ref[(g * dims + j) * 2], g_ref[(g * dims + j) * 2 + 1]) for g in range(groups)]

    def through(yr, yi):
        ends = [None] * groups
        for g in reversed(range(groups)):
            ends[g] = (yr, yi)
            keep = cont_ref[g]
            tr, ti = qr * yr + qi * yi, qr * yi - qi * yr
            yr, yi = keep * tr + part[g][0], keep * ti + part[g][1]
        return ends, yr, yi

    _, fr, fi = through(inr, ini)
    for k in range(3):
        base = 2 * dims * (k + 1)
        wr, wi = broadcast_row(qs, base + j), broadcast_row(qs, base + dims + j)
        pr, pi = rotate(fr, -(1 << k)), rotate(fi, -(1 << k))
        keep = mkr_ref[k]
        fr, fi = fr + keep * (wr * pr + wi * pi), fi + keep * (wr * pi - wi * pr)
    last = lax.broadcasted_iota(jnp.int32, (8, LANES), 0) == 7
    ends, _, _ = through(jnp.where(last, inr, rotate(fr, -1)), jnp.where(last, ini, rotate(fi, -1)))
    return ends, (fr, fi)


REDUCE_PLAN = (
    (0, 1, False), (4, 1, False), (5, 1, False), (7, 1, False), (8, 2, False), (9, 1, False), (10, 1, False),
    (11, 1, False), (12, 1, False), (13, 1, False), (14, 1, False), (15, 0, True),
)


def ema_backward(
    rows, dims, parts, halo, hops, hosted, h_ref, de_ref, rows_seg_ref, edge_ref, q_ref, f_ref, e_ref, root_ref,
    feed_ref, s_ref, skip_ref, back_ref, zeros_ref, *refs
):
    refs = list(refs)
    pack_ref = refs.pop(0) if hosted else None
    outs = [refs.pop(0) for _ in range(6)]
    back = [refs.pop(0) for _ in hops]
    sum_ref = refs.pop(0) if hosted else None
    seg_ref, kend_ref, k0_ref, cont_ref, mkr_ref = (refs.pop(0) for _ in range(5))
    pulls, heads, got, entry, state_sems, back_sems, local_sems, *rest = refs
    held, rest = rest[:9], rest[9:]
    hs, ds, la, table, qs = held[:5]
    groups = rows // (8 * STEP)
    step = pl.program_id(0)
    z = lax.axis_index("tensor")
    blocks = pulls.shape[0]
    k = step % blocks
    stages = reduce_stages(parts, pack_ref, sum_ref, *rest) if hosted else []
    states = lambda hop, at: Along(
        parts, -hop, heads.at[at], got.at[hop - 1, at], state_sems.at[0, hop - 1, at], state_sems.at[1, hop - 1, at]
    )
    moves, fills, end = [], [], halo
    for h, n in enumerate(hops):
        moves.append(Along(parts, -h - 1, back_ref.at[pl.ds(end - n, n)], back[h], back_sems.at[0, h], back_sems.at[1, h]))
        fills.append((z + h + 1 >= parts, (zeros_ref.at[pl.ds(0, n)], back[h], local_sems.at[h])))
        end -= n

    def filling(action):
        for condition, copy in fills:
            @pl.when(condition)
            def _():
                action(pltpu.make_async_copy(*copy))

    @pl.when(step == 0)
    def _():
        greet(parts, 3 if hosted else 0)
        filling(lambda c: c.start())
        fill_masks(groups, rows_seg_ref, edge_ref[0:1, :], seg_ref, kend_ref, k0_ref, cont_ref, mkr_ref, True)

    @pl.when(step == blocks)
    def _():
        for move in moves:
            move.start()

    if hosted:
        run_stages(stages, step, REDUCE_PLAN, False)
    pw = power_list(dims, q_ref)
    turn = fill_scales(groups, dims, pw, qs)

    @pl.when(step < blocks)
    def _():
        fill_read(dims, pw, e_ref, table)
        for at in range(groups * STEP):
            ds[at] = de_ref[pl.ds(at, 8, stride=groups * STEP), :] * k0_ref[at]
        chunk_sums(groups, dims, table, ds, pulls.at[k], -1)

        def one(j, carry):
            zero = jnp.zeros((8, LANES), F32)
            _, head = reverse_states(groups, dims, j, pulls.at[k], qs, cont_ref, mkr_ref, zero, zero)
            heads[k, pl.ds(j, 1), :] = head[0][0:1]
            heads[k, pl.ds(dims + j, 1), :] = head[1][0:1]
            return carry

        lax.fori_loop(0, dims, one, 0)
        for hop in (1, 2):
            states(hop, k).start()

    @pl.when(step >= blocks)
    def _():
        entry[...] = jnp.zeros_like(entry)

        def near_one():
            entry[...] = got[0, k]

        def far_one():
            cross = edge_ref[3:4, :]
            r, i = times(turn[0], -turn[1], got[1, k, :dims], got[1, k, dims:])
            entry[:dims] += cross * r
            entry[dims:] += cross * i

        states(1, k).wait_recv(near_one)
        states(2, k).wait_recv(far_one)
        ema_grads(
            groups, dims, h_ref, de_ref, seg_ref, kend_ref, k0_ref, pw, f_ref, e_ref, root_ref, feed_ref,
            cont_ref, mkr_ref, pulls.at[k], entry, s_ref, skip_ref, *outs, *held,
        )

    @pl.when(step == 2 * blocks - 1)
    def _():
        for at in range(blocks):
            for hop in (1, 2):
                states(hop, at).wait_send()
        for move in moves:
            move.wait_recv()
            move.wait_send()
        filling(lambda c: c.wait())

    if hosted:
        run_stages(stages, step, REDUCE_PLAN, True)


def ema_grads(
    groups, dims, h_ref, de_ref, seg_ref, kend_ref, k0_ref, pw, f_ref, e_ref, root_ref, feed_ref, cont_ref,
    mkr_ref, g_ref, in_ref, s_ref, skip_ref, dh_ref, ge_ref, gf_ref, gr_ref, ga_ref, gs_ref, hs, ds, la, tb, qs, pf,
    red, hn, dn
):
    last = lax.broadcasted_iota(jnp.int32, (8, LANES), 0) == 7
    fill_feed(dims, pw, f_ref, tb)
    taps = tap_list(dims, pw, e_ref, f_ref)
    for i in range(STEP):
        at = slice(i * dims, (i + 1) * dims)
        pf[0, at], pf[1, at] = pw[i + 1]
        pf[2, at], pf[3, at] = pw[STEP - 1 - i]

    def one(j, carry):
        inr = jnp.where(last, broadcast_row(in_ref, j), 0.0)
        ini = jnp.where(last, broadcast_row(in_ref, dims + j), 0.0)
        ends, _ = reverse_states(groups, dims, j, g_ref, qs, cont_ref, mkr_ref, inr, ini)
        qr = jnp.zeros((8, LANES), F32)
        qi = jnp.zeros((8, LANES), F32)
        for g in range(groups):
            yr, yi = ends[g]
            la[(g * dims + j) * 2] = yr
            la[(g * dims + j) * 2 + 1] = yi
            keep = cont_ref[g]
            sr, si = s_ref[(g * dims + j) * 2], s_ref[(g * dims + j) * 2 + 1]
            qr = qr + keep * (yr * sr + yi * si)
            qi = qi + keep * (yi * sr - yr * si)
        red[0, pl.ds(j, 1), :] = jnp.sum(qr, axis=0, keepdims=True)
        red[1, pl.ds(j, 1), :] = jnp.sum(qi, axis=0, keepdims=True)
        return carry

    lax.fori_loop(0, dims, one, 0)
    total = jnp.zeros((8, LANES), F32)
    for at in range(groups * STEP):
        h = h_ref[pl.ds(at, 8, stride=groups * STEP), :]
        d = de_ref[pl.ds(at, 8, stride=groups * STEP), :]
        hs[at] = h
        ds[at] = d
        hn[pl.ds(at, 8, stride=groups * STEP), :] = h * kend_ref[at]
        dn[pl.ds(at, 8, stride=groups * STEP), :] = d * k0_ref[at]
        total = total + h * d
    gs_ref[...] = jnp.sum(total, axis=0, keepdims=True)
    position_sums(groups, dims, tb, la, kend_ref, hs, groups * STEP, 1)
    tap0 = taps[0] + jnp.broadcast_to(skip_ref[...], (8, LANES))

    def within(g, kacc):
        kacc = list(kacc)
        for s in range(STEP):
            at = g * STEP + s
            seg = seg_ref[at]
            h = hs[at]
            out = hs[groups * STEP + at] + tap0 * ds[at]
            for t in range(s + 1, STEP):
                d = jnp.where(seg_ref[g * STEP + t] == seg, ds[g * STEP + t], 0.0)
                out = out + taps[t - s] * d
                kacc[t - s] = kacc[t - s] + h * d
            dh_ref[pl.ds(at, 8, stride=groups * STEP), :] = out
        return tuple(kacc)

    kacc = lax.fori_loop(0, groups, within, (total,) + (jnp.zeros((8, LANES), F32),) * (STEP - 1))

    width = 4
    place = (lax.broadcasted_iota(jnp.int32, (STEP, LANES), 0) + 1).astype(F32)

    def tables(jq, carry):
        def chunk(n, acc):
            sub, g = n // groups, n % groups
            d0, d1 = (dn[pl.ds(pl.multiple_of(n * STEP + 8 * p, 8), 8), :] for p in range(2))
            h0, h1 = (hn[pl.ds(pl.multiple_of(n * STEP + 8 * p, 8), 8), :] for p in range(2))
            out = []
            for k in range(width):
                at = (g * dims + jq * width + k) * 2
                sr, si = (s_ref[at + p, pl.ds(sub, 8, stride=0), :] for p in range(2))
                yr, yi = (la[at + p, pl.ds(sub, 8, stride=0), :] for p in range(2))
                a = acc[8 * k : 8 * k + 8]
                out += [a[0] + d0 * sr, a[1] + d1 * sr, a[2] - d0 * si, a[3] - d1 * si]
                out += [a[4] + h0 * yr, a[5] + h1 * yr, a[6] + h0 * yi, a[7] + h1 * yi]
            return tuple(out)

        acc = lax.fori_loop(0, 8 * groups, chunk, (jnp.zeros((8, LANES), F32),) * (8 * width))
        for k in range(width):
            j = jq * width + k
            ar, ai, br, bi = (
                jnp.concatenate([acc[8 * k + 2 * p], acc[8 * k + 2 * p + 1]], axis=0) for p in range(4)
            )
            pr, pi, wr, wi = (pf[p, pl.ds(j, STEP, stride=dims), :] for p in range(4))
            ur, ui = ar * pr + ai * pi, ai * pr - ar * pi
            vr, vi = br * wr + bi * wi, bi * wr - br * wi
            rest = STEP - place
            sums = (ur, ui, place * ur, place * ui, vr, rest * vr, rest * vi)
            for p, v in enumerate(sums):
                red[2 + p, pl.ds(j, 1), :] = jnp.sum(v, axis=0, keepdims=True)
        return carry

    lax.fori_loop(0, dims // width, tables, 0)
    e0, e1, f = e_ref[:dims], e_ref[dims:], f_ref[...]
    zero = jnp.zeros((dims, LANES), F32)
    tr, ti, ur, ui = zero, zero, zero, zero
    for d in range(STEP):
        tap = jnp.broadcast_to(jnp.sum(kacc[d], axis=0, keepdims=True), (dims, LANES))
        r, m = tap * pw[d][0], tap * pw[d][1]
        tr, ti = tr + r, ti - m
        if d > 0:
            ur, ui = ur + d * r, ui - d * m
    ge_ref[:dims] = red[2] + f * tr
    ge_ref[dims:] = red[3] + f * ti
    gf = red[6] + e0 * tr + e1 * ti
    xr, xi = red[4] + f * ur, red[5] + f * ui
    lr = e0 * xr + e1 * xi + f * red[7]
    li = e0 * xi - e1 * xr + f * red[8]
    zr, zi = pw[STEP]
    lr = lr + STEP * (red[0] * zr + red[1] * zi)
    li = li + STEP * (red[1] * zr - red[0] * zi)
    root = root_ref[...]
    gf_ref[...] = gf * root
    gr_ref[...] = gf * feed_ref[...] * (1.0 - root * root) / root - lr
    ga_ref[...] = li


def whole(*shape):
    return pl.BlockSpec(shape, lambda i: (0,) * len(shape))


def ema_call(body, width, ins, outs, scratch, name, flops, collective_id):
    return pl.pallas_call(
        body,
        grid=(2 * (width // LANES),),
        in_specs=[s for _, s in ins],
        out_specs=[s for _, s in outs],
        out_shape=[o for o, _ in outs],
        scratch_shapes=scratch,
        compiler_params=pltpu.CompilerParams(
            vmem_limit_bytes=60 << 20, collective_id=collective_id, has_side_effects=True
        ),
        cost_estimate=pl.CostEstimate(flops=flops // 1000, bytes_accessed=1024, transcendentals=0),
        name=name,
    )(*[a for a, _ in ins])


def merged(ref):
    v = ref[...]
    return v.reshape(-1, v.shape[-1])


GATHER_PLAN = ((0, 2, False), (1, 1, False), (2, 1, False), (3, 1, False), (3, 0, True))


def attend_kernel(halo, parts, hops, hosted, q_ref, own_k_ref, seg_ref, segk_ref, h_ref, m_ref, x_ref, gain_ref, wv_ref, wg_ref,
                  wo_ref, *refs):
    refs = list(refs)
    pack_ref = refs.pop(0) if hosted else None
    p_ref, vp_ref, v_ref, gp_ref, o_ref, g_ref, y_ref, n_ref, k_ref = (refs.pop(0) for _ in range(9))
    all_ref = refs.pop(0) if hosted else None
    pb_ref, keys, key_sems, *rest = refs
    t = pl.program_id(0)
    z = lax.axis_index("tensor")
    rows = q_ref.shape[0]
    stages = gather_stages(parts, pack_ref, all_ref, *rest) if hosted else []
    moves, places, end = [], [], halo
    for h, n in enumerate(hops):
        place = pl.ds(end - n, n)
        moves.append(Along(parts, h + 1, own_k_ref.at[pl.ds(rows - n, n)], keys.at[place], key_sems.at[0, h], key_sems.at[1, h]))
        places.append((h + 1, slice(end - n, end)))
        end -= n

    @pl.when(t == 0)
    def _():
        greet(parts, 3 if hosted else 0)
        for move in moves:
            move.start()
        keys[halo:, :] = own_k_ref[...]
        if end > 0:
            keys[:end, :] = jnp.zeros((end, keys.shape[1]), BF16)
        for first, place in places:
            @pl.when(z < first)
            def _():
                keys[place, :] = jnp.zeros((place.stop - place.start, keys.shape[1]), BF16)

    if hosted:
        run_stages(stages, t, GATHER_PLAN, False)

    vp = dot32(h_ref[...], merged(wv_ref))
    v = silu_of(vp).astype(BF16)
    vp_ref[...] = vp.astype(BF16)
    v_ref[...] = v
    gp = dot32(m_ref[...], merged(wg_ref))
    gp_ref[...] = gp.astype(BF16)

    @pl.when(t == 0)
    def _():
        for move in moves:
            move.wait_recv()
            move.wait_send()
        k_ref[...] = keys[...]
        count = keys.shape[0]
        scores = dot32(q_ref[...], keys[...], NT) * (1.0 / math.sqrt(q_ref.shape[1]))
        at_row = lax.broadcasted_iota(jnp.int32, (rows, count), 0)
        at_key = lax.broadcasted_iota(jnp.int32, (rows, count), 1)
        allowed = (at_key <= at_row + halo) & (segk_ref[...] == seg_ref[...])
        scores = jnp.where(allowed, scores, -1e30)
        raw = jnp.exp(scores - jnp.max(scores, axis=1, keepdims=True))
        p = raw / jnp.sum(raw, axis=1, keepdims=True)
        p_ref[...] = p
        pb_ref[...] = p.astype(BF16)
        y_ref[...] = x_ref[...].astype(F32)

    o = dot32(pb_ref[...], v)
    o_ref[...] = o.astype(BF16)
    g = (silu_of(gp) * o).astype(BF16)
    g_ref[...] = g
    y_ref[...] += dot32(g, merged(wo_ref), NT)

    @pl.when(t == pl.num_programs(0) - 1)
    def _():
        y = y_ref[...]
        rr = lax.rsqrt(jnp.mean(y * y, axis=1, keepdims=True) + EPSILON)
        n_ref[...] = (y * rr * gain_ref[...]).astype(BF16)

    if hosted:
        run_stages(stages, t, GATHER_PLAN, True)


def ffn_kernel(
    y_ref, n_ref, og_ref, gain_ref, w1_ref, w3_ref, w2_ref, out_ref, dy_ref, branch_ref, gain_grad_ref, grads_ref,
    acc, dn,
):
    t = pl.program_id(0)

    @pl.when(t == 0)
    def _():
        acc[...] = y_ref[...]
        dn[...] = jnp.zeros_like(dn)

    w1, w3, w2 = merged(w1_ref), merged(w3_ref), merged(w2_ref)
    nn, og = n_ref[...], og_ref[...]
    u1, u3 = dot32(nn, w1), dot32(nn, w3)
    sg = jax.nn.sigmoid(u1)
    act = u1 * sg
    hd = (act * u3).astype(BF16)
    acc[...] += dot32(hd, w2, NT)
    dh = dot32(og, w2)
    d1 = (dh * u3 * (sg * (1.0 + u1 * (1.0 - sg)))).astype(BF16)
    d3 = (dh * act).astype(BF16)
    dn[...] += dot32(d1, w1, NT) + dot32(d3, w3, NT)
    depth = grads_ref.shape[3]
    for k, (a, b) in enumerate(((nn, d1), (nn, d3), (og, hd))):
        grads_ref[:, 0, k] = dot32(a, b, TN).astype(BF16).reshape(-1, depth, b.shape[1])

    @pl.when(t == pl.num_programs(0) - 1)
    def _():
        out_ref[...] = acc[...].astype(BF16)
        y = y_ref[...]
        rr = lax.rsqrt(jnp.mean(y * y, axis=1, keepdims=True) + EPSILON)
        nh = y * rr
        g = dn[...]
        gain_grad_ref[...] = jnp.sum(nh * g, axis=0, keepdims=True)
        scaled = g * gain_ref[...]
        dy = og.astype(F32) + rr * (scaled - nh * jnp.mean(nh * scaled, axis=1, keepdims=True))
        dy_ref[...] = dy
        branch_ref[...] = dy.astype(BF16)


def attend_back_kernel(
    halo, parts, hops, br_ref, p_ref, h_ref, m_ref, q_ref, k_ref, vp_ref, v_ref, gp_ref, o_ref, g_ref, wv_ref, wg_ref, wo_ref,
    dq_ref, dk_ref, dhn_ref, dh_ref, dm_ref, grads_ref, dp, dhv, pb_ref, give, got, key_sems,
):
    t = pl.program_id(0)
    rows = br_ref.shape[0]
    moves, end = [], halo
    for h, n in enumerate(hops):
        moves.append((n, Along(parts, -h - 1, give.at[pl.ds(end - n, n)], got.at[h, pl.ds(0, n)], key_sems.at[0, h], key_sems.at[1, h])))
        end -= n

    @pl.when(t == 0)
    def _():
        greet(parts, 0)
        pb_ref[...] = p_ref[...].astype(BF16)
        dp[...] = jnp.zeros_like(dp)
        dhv[...] = jnp.zeros_like(dhv)
        dm_ref[...] = jnp.zeros_like(dm_ref)

    branch, pb = br_ref[...], pb_ref[...]
    dg = dot32(branch, merged(wo_ref))
    gp = gp_ref[...].astype(F32)
    sg = jax.nn.sigmoid(gp)
    da = (dg * (gp * sg)).astype(BF16)
    dr = (dg * o_ref[...].astype(F32) * (sg * (1.0 + gp * (1.0 - sg)))).astype(BF16)
    dp[...] += dot32(da, v_ref[...], NT)

    @pl.when(t == pl.num_programs(0) - 1)
    def _():
        scale = 1.0 / math.sqrt(q_ref.shape[1])
        p = p_ref[...]
        d = dp[...]
        ds = (p * (d - jnp.sum(p * d, axis=1, keepdims=True))).astype(BF16)
        dk = dot32(ds, q_ref[...], TN) * scale
        give[...] = dk[:halo].astype(BF16)
        for _, move in moves:
            move.start()
        dk_ref[...] = dk[halo:]
        dq_ref[...] = dot32(ds, k_ref[...]) * scale

    dv = dot32(pb, da, TN)
    dvp = (dv * silu_slope(vp_ref[...].astype(F32))).astype(BF16)
    dhv[...] += dot32(dvp, merged(wv_ref), NT)
    dm_ref[...] += dot32(dr, merged(wg_ref), NT)
    depth = grads_ref.shape[3]
    for k, (a, b) in enumerate(((h_ref[...], dvp), (m_ref[...], dr), (branch, g_ref[...]))):
        grads_ref[:, 0, k] = dot32(a, b, TN).astype(BF16).reshape(-1, depth, b.shape[1])

    @pl.when(t == pl.num_programs(0) - 1)
    def _():
        dhn_ref[...] = dhv[:halo, :].astype(BF16)
        dh_ref[...] = dhv[halo:, :]
        for h, (n, move) in enumerate(moves):
            def arrived(h=h, n=n):
                dk_ref[rows - n :, :] += got[h, :n, :].astype(F32)
            move.wait_recv(arrived)
            move.wait_send()


def stage_call(body, steps, ins, outs, scratch, name, flops, collective_id=None):
    def spec(v, how):
        if how == "all":
            return pl.BlockSpec(v.shape, lambda t: (0,) * v.ndim)
        if how == "col":
            return pl.BlockSpec((v.shape[0], v.shape[1] // steps), lambda t: (0, t))
        return how

    outs = [(jax.ShapeDtypeStruct(s, d), how) for s, d, how in outs]
    return pl.pallas_call(
        body,
        grid=(steps,),
        in_specs=[spec(v, how) for v, how in ins],
        out_specs=[spec(v, how) for v, how in outs],
        out_shape=[v for v, _ in outs],
        scratch_shapes=scratch,
        compiler_params=pltpu.CompilerParams(
            vmem_limit_bytes=60 << 20, collective_id=collective_id, has_side_effects=collective_id is not None
        ),
        cost_estimate=pl.CostEstimate(flops=flops // 1000, bytes_accessed=1024, transcendentals=0),
        name=name,
    )(*[v for v, _ in ins])


def flipped(d, k):
    return d + (1 - 2 * ((d // (1 << k)) % 2)) * (1 << k)


def greet(parts, dp_bits):
    d, z = lax.axis_index("dp"), lax.axis_index("tensor")
    barrier = pltpu.get_barrier_semaphore()
    for k in range(dp_bits):
        pl.semaphore_signal(barrier, inc=1, device_id=(flipped(d, k), z), device_id_type=pl.DeviceIdType.MESH)
    for step in (-2, -1, 1, 2):
        @pl.when((z + step >= 0) & (z + step < parts))
        def _():
            pl.semaphore_signal(barrier, inc=1, device_id=(d, z + step), device_id_type=pl.DeviceIdType.MESH)
    pl.semaphore_wait(barrier, dp_bits + jnp.minimum(z, 2) + jnp.minimum(parts - 1 - z, 2))


class Along:
    def __init__(self, parts, hop, src, dst, send_sem, recv_sem, first=0):
        d, z = lax.axis_index("dp"), lax.axis_index("tensor")
        to = z + hop
        self.sends = (to >= 0) & (to < parts) & (z >= first)
        self.gets = (z - hop >= first) & (z - hop < parts)
        self.make = lambda: pltpu.make_async_remote_copy(
            src_ref=src, dst_ref=dst, send_sem=send_sem, recv_sem=recv_sem,
            device_id=(d, jnp.clip(to, 0, parts - 1)), device_id_type=pl.DeviceIdType.MESH,
        )

    def start(self):
        @pl.when(self.sends)
        def _():
            self.make().start()

    def wait_send(self):
        @pl.when(self.sends)
        def _():
            self.make().wait_send()

    def wait_recv(self, then=lambda: None):
        @pl.when(self.gets)
        def _():
            self.make().wait_recv()
            then()


def gather_stages(parts, pack_ref, out_ref, sems, own_sem):
    d, z = lax.axis_index("dp"), lax.axis_index("tensor")
    total = pack_ref.shape[0]
    cut = total // 32 * 16
    upper, lower, full = pl.ds(0, cut), pl.ds(cut, total - cut), pl.ds(0, total)
    core, first, second = (flipped(d, k) for k in range(3))
    across = first + second - d
    MESH = pl.DeviceIdType.MESH

    LINE, TO_FIRST, TO_SECOND, UP, DOWN, C_OWN, C_FIRST, C_SECOND, C_UP, C_DOWN = range(10)

    def copy(kind, b, source, part, dp_to, z_to):
        here = out_ref.at[source, b, part]
        return pltpu.make_async_remote_copy(
            src_ref=here, dst_ref=here, send_sem=sems.at[0, kind, b], recv_sem=sems.at[1, kind, b],
            device_id=(dp_to, z_to), device_id_type=MESH,
        )

    def begin():
        mine = pltpu.make_async_copy(pack_ref, out_ref.at[d, z], own_sem)
        mine.start()
        mine.wait()

    def spread_block(b):
        copy(TO_FIRST, b, d, full, first, z).start()
        copy(TO_SECOND, b, d, full, second, z).start()
        copy(C_OWN, b, d, full, core, z).start()

    def along(b, step):
        @pl.when((z + step >= 0) & (z + step < parts))
        def _():
            here = out_ref.at[d, b]
            pltpu.make_async_remote_copy(
                src_ref=here, dst_ref=here, send_sem=sems.at[0, LINE + (10 if step > 0 else 11), b],
                recv_sem=sems.at[1, LINE, b], device_id=(d, z + step), device_id_type=MESH,
            ).start()

    def relay(b):
        copy(TO_FIRST, b, first, full, first, z).wait_recv()
        copy(UP, b, first, upper, second, z).start()
        copy(C_FIRST, b, first, full, core, z).start()
        copy(TO_SECOND, b, second, full, second, z).wait_recv()
        copy(DOWN, b, second, lower, first, z).start()
        copy(C_SECOND, b, second, full, core, z).start()

    def corner(b):
        copy(UP, b, across, upper, second, z).wait_recv()
        copy(C_UP, b, across, upper, core, z).start()
        copy(DOWN, b, across, lower, first, z).wait_recv()
        copy(C_DOWN, b, across, lower, core, z).start()

    def at_distance(dist, action):
        for side in ((0,) if dist == 0 else (-1, 1)):
            b = z + side * dist
            @pl.when((b >= 0) & (b < parts))
            def _():
                action(b, side)

    def arrive(b, side):
        if side != 0:
            copy(LINE, b, d, full, d, z).wait_recv()
        if side <= 0:
            along(b, 1)
        if side >= 0:
            along(b, -1)
        spread_block(b)

    def finish():
        other_first, other_second = core + first - d, core + second - d
        for b in range(parts):
            for kind, source, part in ((C_OWN, core, full), (C_FIRST, other_first, full), (C_SECOND, other_second, full),
                                       (C_UP, core + across - d, upper), (C_DOWN, core + across - d, lower)):
                copy(kind, b, source, part, core, z).wait_recv()
            for kind, source, part in ((TO_FIRST, d, full), (TO_SECOND, d, full), (C_OWN, d, full), (UP, first, upper),
                                       (DOWN, second, lower), (C_FIRST, first, full), (C_SECOND, second, full),
                                       (C_UP, across, upper), (C_DOWN, across, lower)):
                copy(kind, b, source, part, core, z).wait_send()
            for step, slot in ((1, 10), (-1, 11)):
                @pl.when((z + step >= 0) & (z + step < parts) & (step * (z - b) >= 0))
                def _():
                    copy(slot, b, d, full, core, z).wait_send()

    stages = [begin]
    for dist in range(parts + 2):
        if dist < parts:
            stages.append(functools.partial(at_distance, dist, arrive))
        if 1 <= dist < parts + 1:
            stages.append(functools.partial(at_distance, dist - 1, lambda b, side: relay(b)))
        if dist >= 2:
            stages.append(functools.partial(at_distance, dist - 2, lambda b, side: corner(b)))
    return stages + [finish]


def gather_scratch(parts):
    return [pltpu.SemaphoreType.DMA((2, 12, parts)), pltpu.SemaphoreType.DMA]


def run_stages(stages, step, plan, late):
    at = 0
    for when, count, end in plan:
        here = stages[at : at + count] if count else stages[at:]
        at += len(here)
        if end == late:
            @pl.when(step == when)
            def _():
                for stage in here:
                    stage()


R_CORE, R_FIRST, R_FIRST2, R_SECOND, R_SECOND2, R_UP, R_DOWN, R_RIGHT, R_LEFT = range(9)


def reduce_scratch(parts, rows, columns):
    upper = rows // 32 * 16
    vm = lambda *n: pltpu.VMEM((*n, columns), BF16)
    return [
        vm(parts, 4, rows), vm(parts, 4, rows), vm(parts, 2, upper), vm(parts, 2, rows - upper), vm(parts, upper),
        vm(parts, rows - upper), vm(2, parts, rows), pltpu.SemaphoreType.DMA((2, 9, parts)),
        pltpu.SemaphoreType.DMA((parts,)),
    ]


def reduce_stages(parts, pack, out, acc, got_core, got_first, got_second, got_up, got_down, got_line, sems, load_sems):
    d, z = lax.axis_index("dp"), lax.axis_index("tensor")
    MESH = pl.DeviceIdType.MESH
    rows = acc.shape[2]
    cut = rows // 32 * 16
    upper, lower = pl.ds(0, cut), pl.ds(cut, rows - cut)
    me, core = d // 2, d % 2
    bit = lambda k: (me // (1 << k)) % 2
    first = me + (1 - 2 * bit(0))
    second = me + 2 * (1 - 2 * bit(1))
    across = first + second - me
    on = lambda p: 2 * p + core
    far = z // (parts // 2)
    near_end = z + far * (parts - 1 - 2 * z)

    def unit(s):
        t = (parts - 1 - s) + near_end * ((3, 0, 2, 1)[s] - (parts - 1 - s))
        return t + far * (parts - 1 - 2 * t)

    def copy(kind, t, src, dst, where):
        return pltpu.make_async_remote_copy(
            src_ref=src, dst_ref=dst, send_sem=sems.at[0, kind, t], recv_sem=sems.at[1, kind, t], device_id=where,
            device_id_type=MESH,
        )

    def copies(s):
        t = unit(s)
        to_first, to_second = (on(first), z), (on(second), z)
        table = {
            R_CORE: (pack.at[:, 1 - core, t], got_core.at[t], (2 * me + 1 - core, z)),
            R_FIRST: (acc.at[t, first, upper], got_first.at[t, 0], to_first),
            R_FIRST2: (acc.at[t, across, upper], got_first.at[t, 1], to_first),
            R_SECOND: (acc.at[t, second, lower], got_second.at[t, 0], to_second),
            R_SECOND2: (acc.at[t, across, lower], got_second.at[t, 1], to_second),
            R_UP: (acc.at[t, second, upper], got_up.at[t], to_second),
            R_DOWN: (acc.at[t, first, lower], got_down.at[t], to_first),
            R_RIGHT: (acc.at[t, me], got_line.at[0, t], (d, jnp.minimum(z + 1, parts - 1))),
            R_LEFT: (acc.at[t, me], got_line.at[1, t], (d, jnp.maximum(z - 1, 0))),
        }
        return lambda kind: copy(kind, t, *table[kind])

    def load(s):
        t = unit(s)
        return pltpu.make_async_copy(pack.at[:, core, t], acc.at[t], load_sems.at[t])

    def add(target, at, count, source):
        tile = 32 if count % 32 == 0 else 16

        def some(i, carry):
            here = pl.ds(pl.multiple_of(at + i * tile, 16), tile)
            there = pl.ds(pl.multiple_of(i * tile, 16), tile)
            target[here, :] = (target[here, :].astype(F32) + source[there, :].astype(F32)).astype(BF16)
            return carry

        lax.fori_loop(0, count // tile, some, 0)

    def begin():
        for s in range(parts):
            load(s).start()
            copies(s)(R_CORE).start()

    def cores(s):
        t, c = unit(s), copies(s)
        load(s).wait()
        c(R_CORE).wait_recv()
        for p in (first, across, second, me):
            add(acc.at[t, p], 0, rows, got_core.at[t, p])
        for kind in (R_FIRST, R_FIRST2, R_SECOND, R_SECOND2):
            c(kind).start()

    def chips(s):
        t, c = unit(s), copies(s)
        for kind in (R_FIRST2, R_SECOND2, R_FIRST, R_SECOND):
            c(kind).wait_recv()
        add(acc.at[t, second], 0, cut, got_first.at[t, 1])
        c(R_UP).start()
        add(acc.at[t, first], cut, rows - cut, got_second.at[t, 1])
        c(R_DOWN).start()
        add(acc.at[t, me], 0, cut, got_first.at[t, 0])
        add(acc.at[t, me], cut, rows - cut, got_second.at[t, 0])

    def line(s):
        t, c = unit(s), copies(s)
        c(R_UP).wait_recv()
        add(acc.at[t, me], 0, cut, got_up.at[t])
        c(R_DOWN).wait_recv()
        add(acc.at[t, me], cut, rows - cut, got_down.at[t])

        @pl.when((z <= t) & (z > 0))
        def _():
            c(R_RIGHT).wait_recv()
            add(acc.at[t, me], 0, rows, got_line.at[0, t])

        @pl.when((z >= t) & (z < parts - 1))
        def _():
            c(R_LEFT).wait_recv()
            add(acc.at[t, me], 0, rows, got_line.at[1, t])

        @pl.when(z < t)
        def _():
            c(R_RIGHT).start()

        @pl.when(z > t)
        def _():
            c(R_LEFT).start()

    def finish():
        out[...] = acc[z, me].astype(F32)
        for s in range(parts):
            t, c = unit(s), copies(s)
            for kind in range(R_RIGHT):
                c(kind).wait_send()

            @pl.when(z < t)
            def _():
                c(R_RIGHT).wait_send()

            @pl.when(z > t)
            def _():
                c(R_LEFT).wait_send()

    order = [(cores, 0), (cores, 1), (cores, 2), (chips, 0), (cores, 3), (chips, 1), (line, 0), (chips, 2), (line, 1),
             (chips, 3), (line, 2), (line, 3)]
    return [begin] + [functools.partial(f, s) for f, s in order] + [finish]


def parts_of(v, count):
    out = []
    for _ in range(count):
        out.append(v.astype(BF16))
        v = v - out[-1].astype(F32)
    return out


def group_table(width, groups):
    low = lax.broadcasted_iota(jnp.int32, (width, groups), 1) * (width // groups)
    at = lax.broadcasted_iota(jnp.int32, (width, groups), 0)
    return ((at >= low) & (at < low + width // groups)).astype(BF16)


def add_rows(target, source, other, count, columns):
    def some(i, carry):
        here = pl.ds(pl.multiple_of(i * 32, 32), 32)
        target[here, :] = (source[here, :].astype(F32) + other[here, :].astype(F32)).astype(BF16)
        return carry

    lax.fori_loop(0, count // 32 if count % 32 == 0 else 0, some, 0)
    if count % 32:
        target[...] = (source[...].astype(F32) + other[...].astype(F32)).astype(BF16)


def end_kernel(
    bits, parts, replicas, per_tile, hops, x_ref, mean_ref, rho_ref, count_ref, gain_ref, own_ref, ema_ref, back0_ref,
    back1_ref, res_ref, segc_ref, segr_ref, next_ref, block_ref, *refs
):
    pieces, (ffn_ref, in_ref), outs, (own_sum_ref, ffn_sum_ref), scratch = (
        refs[:6], refs[6:8], refs[8:15], refs[15:17], refs[17:]
    )
    (gh, cen, rf, backed, head, head_got, total, acc, cube, buf, cbuf, summed, chain, chain_got,
     sems, head_sems, chain_sems) = scratch
    d, z = lax.axis_index("dp"), lax.axis_index("tensor")
    MESH = pl.DeviceIdType.MESH
    rows, width = x_ref.shape
    groups = mean_ref.shape[1]
    tiles = width // LANES
    greet(parts, sum(axis == "dp" for axis, _ in bits))

    far = z // (parts // 2)
    near_end = z + far * (parts - 1 - 2 * z)

    def unit(s):
        t = (parts - 1 - s) + near_end * ((3, 0, 2, 1)[s] - (parts - 1 - s))
        return t + far * (parts - 1 - 2 * t)

    def line_copy(s, side):
        t = unit(s)
        to = jnp.clip(z + (1 if side == 0 else -1), 0, parts - 1)
        return pltpu.make_async_remote_copy(
            src_ref=chain.at[t], dst_ref=chain_got.at[side, t], send_sem=chain_sems.at[0, side, t],
            recv_sem=chain_sems.at[1, side, t], device_id=(d, to), device_id_type=MESH,
        )

    def along(s):
        t = unit(s)
        span, columns = chain.shape[1:]
        from_left, from_right = (z <= t) & (z > 0), (z >= t) & (z < parts - 1)

        @pl.when(from_left)
        def _():
            line_copy(s, 0).wait_recv()
            add_rows(chain.at[t], ffn_ref.at[t], chain_got.at[0, t], span, columns)

        @pl.when(jnp.logical_not(from_left))
        def _():
            chain[t] = ffn_ref[t]

        @pl.when(from_right)
        def _():
            line_copy(s, 1).wait_recv()
            add_rows(chain.at[t], chain.at[t], chain_got.at[1, t], span, columns)

        @pl.when(z < t)
        def _():
            line_copy(s, 0).start()

        @pl.when(z > t)
        def _():
            line_copy(s, 1).start()

    def mine(axis, k):
        return ((d if axis == "dp" else z) // (1 << k)) % 2

    def partner(axis, k):
        step = (1 - 2 * mine(axis, k)) * (1 << k)
        return (d + step, z) if axis == "dp" else (d, z + step)

    def copy(n, which, src, dst):
        return pltpu.make_async_remote_copy(
            src_ref=src, dst_ref=dst, send_sem=sems.at[0, which, n], recv_sem=sems.at[1, which, n],
            device_id=partner(*bits[n]), device_id_type=MESH,
        )

    plan = []
    start, length, cstart, clength, at, cat = 0, acc.shape[0], 0, cube.shape[0], 0, 0
    for axis, k in bits:
        half = length // 2
        keep = pl.multiple_of(start + mine(axis, k) * half, 8)
        give = pl.multiple_of(start + (1 - mine(axis, k)) * half, 8)
        if axis == "dp":
            chalf = clength // 2
            ckeep = pl.multiple_of(cstart + mine(axis, k) * chalf, 16)
            cgive = pl.multiple_of(cstart + (1 - mine(axis, k)) * chalf, 16)
        else:
            chalf, ckeep, cgive = clength, cstart, cstart
        plan.append((start, length, half, keep, give, chalf, ckeep, cgive, at, cat))
        start, length, cstart, clength = keep, half, ckeep, chalf
        at, cat = at + half, cat + chalf

    def exchange(n):
        _, _, half, _, give, chalf, _, cgive, at, cat = plan[n]
        return (copy(n, 0, acc.at[pl.ds(give, half)], buf.at[pl.ds(at, half)]),
                copy(n, 1, cube.at[pl.ds(cgive, chalf)], cbuf.at[pl.ds(cat, chalf)]))

    def send(n):
        for c in exchange(n):
            c.start()

    def receive(n):
        for c in exchange(n):
            c.wait()
        _, _, half, keep, _, chalf, ckeep, _, at, cat = plan[n]
        acc[pl.ds(keep, half)] += buf[pl.ds(at, half)]
        both = cube[pl.ds(ckeep, chalf)].astype(F32) + cbuf[pl.ds(cat, chalf)].astype(F32)
        cube[pl.ds(ckeep, chalf)] = both.astype(BF16)

    along(0)

    table = group_table(width, groups)
    spread_of = lambda v: sum(dot32(p, table, NT) for p in parts_of(v, 3))
    sums_of = lambda v: sum(dot32(p, table) for p in parts_of(v, 2))
    gh[...] = own_ref[...] + ema_ref[...] + back0_ref[...].astype(F32)
    gh[rows - hops[1] :, :] += back1_ref[...].astype(F32)
    mean, rho, count = mean_ref[...], rho_ref[...], count_ref[...]
    rf[...] = spread_of(rho)
    cen[...] = x_ref[...].astype(F32) - spread_of(mean)
    gain_grad = jnp.sum(cen[...] * rf[...] * gh[...], axis=0, keepdims=True)
    last_rows = jnp.zeros((per_tile - sum(p.shape[0] for p in pieces) - 1, LANES), F32)
    for tile in range(tiles):
        lanes = slice(tile * LANES, (tile + 1) * LANES)
        row = tile * per_tile
        for p in pieces:
            acc[row : row + p.shape[0], :] = p[:, lanes]
            row += p.shape[0]
        acc[row : row + 1, :] = gain_grad[:, lanes]
        acc[row + 1 : (tile + 1) * per_tile, :] = last_rows
    depth = block_ref.shape[0] // replicas
    levels = replicas.bit_length() - 1
    for b in range(replicas):
        m = sum(((b >> k) & 1) << (levels - 1 - k) for k in range(levels))
        cube[m * depth : (m + 1) * depth, :] = block_ref[b * depth : (b + 1) * depth, :].astype(BF16)
    send(0)

    gh[...] = gh[...] * gain_ref[...]
    sum_a, sum_b = rho * sums_of(gh[...]), sums_of(gh[...] * cen[...])
    third = sum_b * rho * rho * rho
    lower = (segc_ref[...] == segr_ref[...]) & (
        lax.broadcasted_iota(jnp.int32, (rows, rows), 0) >= lax.broadcasted_iota(jnp.int32, (rows, rows), 1)
    )
    lower = lower.astype(F32).astype(BF16)
    back = lambda v: sum(dot32(lower, p, TN) for p in parts_of(v, 3))
    backed[0] = back((third * mean - sum_a) / count)
    backed[1] = back(-third / (2.0 * count))
    for half in range(2):
        head[half, :, :groups] = backed[half, 0:8, :]
    to_heads = [Along(parts, -hop, head, head_got.at[hop - 1], head_sems.at[0, hop - 1], head_sems.at[1, hop - 1])
                for hop in (1, 2)]
    for move in to_heads:
        move.start()
    receive(0)
    send(1)
    along(1)
    total[...] = jnp.zeros_like(total)
    for hop, move in enumerate(to_heads):
        def arrived(hop=hop):
            total[...] += next_ref[hop : hop + 1, :] * head_got[hop]
        move.wait_recv(arrived)
    tails = (segc_ref[...] == segc_ref[rows - 1 : rows, :]).astype(F32)
    first, second = (backed[half] + tails * total[half, 0:1, :groups] for half in range(2))
    in_ref[...] = res_ref[...] + gh[...] * rf[...] + spread_of(first) + 2.0 * x_ref[...].astype(F32) * spread_of(second)

    for n in range(1, len(bits)):
        receive(n)
        if n + 1 < len(bits):
            send(n + 1)
        if n + 1 < parts:
            along(n + 1)
    clast = pl.multiple_of(plan[-1][6], 16)
    own_sum_ref[...] = cube[pl.ds(clast, clength)].astype(F32)
    summed[pl.ds(start, length)] = acc[pl.ds(start, length)]
    for n in reversed(range(len(bits))):
        here = summed.at[pl.ds(start, length)]
        copy(n, 2, here, here).start()
        copy(n, 2, here, here).wait()
        start, length = plan[n][:2]
    for tile in range(tiles):
        lanes = slice(tile * LANES, (tile + 1) * LANES)
        row = tile * per_tile
        for out in outs:
            out[:, lanes] = summed[row : row + out.shape[0], :]
            row += out.shape[0]
    ffn_sum_ref[...] = chain[z].astype(F32)
    for s in range(parts):
        @pl.when(z < unit(s))
        def _():
            line_copy(s, 0).wait_send()

        @pl.when(z > unit(s))
        def _():
            line_copy(s, 1).wait_send()
    for move in to_heads:
        move.wait_send()


def end_call(replicas, parts, hops, per_row, pieces, ffn):
    bits = [("dp", k) for k in range(replicas.bit_length() - 1)]
    bits += [("tensor", k) for k in range(parts.bit_length() - 1)]
    x, block = per_row[0], per_row[-1]
    rows, width = x.shape
    tiles = width // LANES
    wanted = tiles * (sum(p.shape[0] for p in pieces) + 1)
    unit = max(replicas * parts * 8, tiles * 8)
    per_tile = -(-wanted // unit) * unit // tiles
    small = (tiles * per_tile, LANES)
    own = block.shape[0] // replicas
    got = sum(block.shape[0] >> (k + 1) for k in range(replicas.bit_length() - 1))
    got += own * (parts.bit_length() - 1)
    groups = per_row[1].shape[1]
    vm = pltpu.VMEM
    dma = lambda *n: pltpu.SemaphoreType.DMA(n)
    shape = jax.ShapeDtypeStruct
    ins = (*per_row, *pieces, ffn)
    outs = ([shape((rows, width), F32)] + [shape(p.shape, F32) for p in pieces]
            + [shape((1, width), F32), shape((own, block.shape[1]), F32), shape(ffn.shape[1:], F32)])
    return pl.pallas_call(
        functools.partial(end_kernel, bits, parts, replicas, per_tile, hops),
        in_specs=[pl.BlockSpec(memory_space=vm)] * len(ins),
        out_specs=[pl.BlockSpec(memory_space=vm)] * len(outs),
        out_shape=outs,
        scratch_shapes=[
            vm((rows, width), F32), vm((rows, width), F32), vm((rows, width), F32), vm((2, rows, groups), F32),
            vm((2, 8, LANES), F32), vm((2, 2, 8, LANES), F32), vm((2, 8, LANES), F32), vm(small, F32),
            vm(block.shape, BF16), vm(small, F32), vm((got, block.shape[1]), BF16), vm(small, F32),
            vm(ffn.shape, BF16), vm((2,) + ffn.shape, BF16), dma(2, 3, len(bits)), dma(2, 2), dma(2, 2, parts),
        ],
        compiler_params=pltpu.CompilerParams(collective_id=0, has_side_effects=True, vmem_limit_bytes=60 << 20),
        name="ending",
    )(*ins)


def on_device(
    block_in, segments, norm_gain, ema_rate, ema_angle, ema_input, ema_output, ema_skip, w_shared, query_gain,
    query_bias, key_gain, w_value, w_gate, w_out, ffn_gain, w_swish, w_up, w_down, out_grad,
):
    parts = lax.axis_size("tensor")
    replicas = lax.axis_size("dp")
    rank = lax.axis_index("tensor")
    rows, width = block_in.shape
    dims = ema_rate.shape[0]
    length = segments.shape[1]
    groups = TN_GROUPS
    span = width // groups
    latent_width = w_shared.shape[1]
    value_width = w_value.shape[1] * parts
    ffn_width = w_swish.shape[1] * parts
    depth = w_value.shape[0]
    halo = -(-REACH // LANES) * LANES
    hops = [min(rows, REACH - h * rows) for h in range(-(-REACH // rows))]

    chip_links = replicas == 8 and parts == 4

    piece = depth // parts
    shared_piece = lax.dynamic_slice_in_dim(w_shared, rank * piece, piece, 0)
    low = lambda w: w.astype(BF16)
    vw, fw = value_width // parts, ffn_width // parts
    pack_a = jnp.concatenate(
        [low(w_value), low(w_gate), low(w_out.T), low(shared_piece).reshape(-1, vw)], axis=0
    )
    pack_f1 = low(w_swish)
    pack_f2 = jnp.concatenate([low(w_up), low(w_down.T)], axis=0)
    gathered = lambda v: lax.all_gather(v, BOTH, axis=0).reshape(replicas, parts, *v.shape)
    pack_f2 = with_layout_constraint(pack_f2, Layout((0, 1)))

    def part(k, columns):
        return pl.BlockSpec((replicas, 1, depth, columns), lambda t: (0, t, k, 0))

    seg_all = segments[0]
    padded = jnp.concatenate([jnp.full((halo,), -1, jnp.int32), seg_all, jnp.full((halo,), -2, jnp.int32)])
    near = lax.dynamic_slice_in_dim(padded, rank * rows, halo + rows + halo, 0)
    seg_keys = near[: halo + rows]
    seg = near[halo : halo + rows]
    before = near[halo - 1]
    index = rank * rows + jnp.arange(rows, dtype=jnp.int32)
    start = jnp.sum((seg_all[None, :] < seg[:, None]).astype(jnp.int32), axis=1)
    count = (index - start + 1).astype(F32)[:, None] * span
    tri = jnp.arange(rows)
    link2 = (before == near[halo - rows - 1]).astype(F32)
    last = seg[-1]
    next1 = (near[halo + rows] == last).astype(F32)
    next2 = ((near[halo + 2 * rows - 1] == last) & (near[halo + 2 * rows] == last)).astype(F32) if halo > rows else 0.0
    cross = near[halo + 2 * rows - 1] == last
    edge = jnp.stack([before.astype(F32), jnp.float32(1.0), link2, cross.astype(F32)])[:, None] * jnp.ones((1, LANES), F32)
    seg_lanes = jnp.broadcast_to(seg.astype(F32)[:, None], (rows, LANES))

    size = jnp.exp(-ema_rate)
    unit = jnp.concatenate([size * jnp.cos(ema_angle), size * jnp.sin(ema_angle)])
    root = jnp.sqrt(1.0 - size * size)
    feed = ema_input * root
    reads = ema_output.reshape(2 * dims, width)
    skip = ema_skip[None]
    gcount = rows // (8 * STEP)
    nstate = gcount * dims * 2
    at_rows = gcount * STEP
    blocks = width // LANES
    col = lambda n: pl.BlockSpec((n, LANES), lambda i: (0, i % blocks))
    late = lambda n: pl.BlockSpec((n, LANES), lambda i: (0, jnp.maximum(i - blocks, 0)))
    late3 = lambda n, m: pl.BlockSpec((n, m, LANES), lambda i: (0, 0, jnp.maximum(i - blocks, 0)))
    anywhere = pl.BlockSpec(memory_space=pl.ANY)
    shape_of = jax.ShapeDtypeStruct
    vm = lambda *n: pltpu.VMEM((*n, 8, LANES), F32)
    flat_vm = lambda *n: pltpu.VMEM((*n, LANES), F32)
    dma = lambda *n: pltpu.SemaphoreType.DMA(n)
    table_vm, scale_vm = flat_vm(2, STEP * dims), flat_vm(8 * dims)
    state_vms = [vm(blocks, nstate), flat_vm(blocks, 2 * dims), flat_vm(2, blocks, 2 * dims), flat_vm(2 * dims),
                 dma(2, 2, blocks), dma(2, 3), dma(4)]
    mac = rows * width * dims * 4
    zeros = (jnp.zeros((rows, width), BF16), anywhere)
    near_rows = halo + rows
    full = lambda v: (v, whole(*v.shape))
    norm_shape = (shape_of((rows, groups), F32), whole(rows, groups))
    rows_late = (shape_of((rows, width), F32), late(rows))
    mask_vms = [vm(at_rows), vm(at_rows), vm(at_rows), vm(gcount), vm(3)]
    results = ema_call(
        functools.partial(ema_forward, rows, dims, parts, halo, hops, chip_links), width,
        [full(block_in), full(norm_gain[None]), full(seg_lanes), full(seg[:, None]), full(seg[None]), full(count),
         full(edge), (unit, col(2 * dims)), (feed, col(dims)), (reads, col(2 * dims)), (skip, col(1)), zeros]
        + [(pack_a, anywhere)] * chip_links,
        [rows_late, (shape_of((rows, width), BF16), late(rows)), (shape_of((nstate, 8, width), F32), late3(nstate, 8)),
         rows_late, norm_shape, norm_shape, (shape_of((near_rows, width), BF16), anywhere)]
        + [(shape_of((replicas, parts) + pack_a.shape, BF16), anywhere)] * chip_links,
        [flat_vm(blocks, rows), pltpu.VMEM((rows, width), BF16), vm(2), vm(2, 2), vm(2), dma(2, 2)] + mask_vms
        + [vm(2 * at_rows), table_vm, scale_vm] + state_vms + (gather_scratch(parts) if chip_links else []),
        "ema_forward", 2 * mac, 3,
    )
    ema_out, mixed, states, hidden, mean, rho, hidden_near = results[:7]
    all_f1 = gathered(lax.optimization_barrier((pack_f1, mixed))[0])
    all_a = results[-1] if chip_links else gathered(pack_a)
    shared_b = all_a[:, :, 3 * depth :].reshape(width, latent_width)

    latent = dot32(mixed, shared_b)
    queries = low(latent * query_gain + query_bias)
    keys_own = low(latent * key_gain)
    one = lambda v: v[None]
    matmul = rows * width * vw * 2 * parts
    col_v = lambda n: ((n, value_width), BF16, "col")
    ins = [(queries, "all"), (keys_own, "all"), (seg[:, None], "all"), (one(seg_keys), "all"), (hidden_near, "all"),
           (mixed, "all"), (block_in, "all"), (one(ffn_gain), "all"), (all_a, part(0, vw)), (all_a, part(1, vw)),
           (all_a, part(2, vw))]
    outs = [((rows, near_rows), F32, "all"), col_v(near_rows), col_v(near_rows), col_v(rows), col_v(rows), col_v(rows),
            ((rows, width), F32, "all"), ((rows, width), BF16, "all"), ((near_rows, latent_width), BF16, "all")]
    results = stage_call(
        functools.partial(attend_kernel, halo, parts, hops, chip_links), parts,
        ins + [(pack_f2, anywhere)] * chip_links,
        outs + [((replicas, parts) + pack_f2.shape, BF16, anywhere)] * chip_links,
        [pltpu.VMEM((rows, near_rows), BF16), pltpu.VMEM((near_rows, latent_width), BF16), dma(2, len(hops))]
        + (gather_scratch(parts) if chip_links else []),
        "attend", 6 * matmul, collective_id=1,
    )
    all_f2 = results[-1] if chip_links else gathered(pack_f2)
    probs, value_pre, values, gate_pre, attended, gated, residual, norm_in, keys_near = results[:9]

    row_vm = lambda n: pltpu.VMEM((n, width), F32)
    block_out, grad_residual, branch, grad_ffn_gain, ffn_grads = stage_call(
        ffn_kernel, parts,
        [(residual, "all"), (norm_in, "all"), (out_grad, "all"), (one(ffn_gain), "all"), (all_f1, part(0, fw)),
         (all_f2, part(0, fw)), (all_f2, part(1, fw))],
        [((rows, width), BF16, "all"), ((rows, width), F32, "all"), ((rows, width), BF16, "all"),
         ((1, width), F32, "all"),
         ((replicas, parts, 3, depth, fw), BF16,
          pl.BlockSpec((replicas, 1, 3, depth, fw), lambda t: (0, t, 0, 0, 0)))],
        [row_vm(rows), row_vm(rows)], "ffn", 11 * matmul,
    )

    def summed(g):
        g = g.reshape(replicas, parts, -1, g.shape[-1])
        return lax.psum_scatter(g, "dp", scatter_dimension=0, tiled=False)

    def summed_along(g, after):
        g = lax.optimization_barrier((g, after))[0]
        return lax.psum_scatter(g, "tensor", scatter_dimension=0, tiled=False).astype(F32)

    ffn_sum = summed(ffn_grads)

    grad_queries, grad_keys, hidden_back, hidden_own, grad_mixed, attn_grads = stage_call(
        functools.partial(attend_back_kernel, halo, parts, hops), parts,
        [(branch, "all"), (probs, "all"), (hidden_near, "all"), (mixed, "all"), (queries, "all"), (keys_near, "all"),
         (value_pre, "col"), (values, "col"), (gate_pre, "col"), (attended, "col"), (gated, "col"),
         (all_a, part(0, vw)), (all_a, part(1, vw)), (all_a, part(2, vw))],
        [((rows, latent_width), F32, "all"), ((rows, latent_width), F32, "all"),
         ((halo, width), BF16, "all"), ((rows, width), F32, "all"), ((rows, width), F32, "all"),
         ((replicas, parts, 3, depth, vw), BF16,
          pl.BlockSpec((replicas, 1, 3, depth, vw), lambda t: (0, t, 0, 0, 0)))],
        [pltpu.VMEM((rows, near_rows), F32), row_vm(near_rows), pltpu.VMEM((rows, near_rows), BF16),
         pltpu.VMEM((halo, latent_width), BF16), pltpu.VMEM((len(hops), rows, latent_width), BF16), dma(2, len(hops))],
        "attend_back", 12 * matmul, collective_id=4,
    )
    grad_query_gain = jnp.sum(latent * grad_queries, axis=0)
    grad_query_bias = jnp.sum(grad_queries, axis=0)
    grad_key_gain = jnp.sum(latent * grad_keys, axis=0)
    grad_latent = low(grad_queries * query_gain + grad_keys * key_gain)
    grad_shared = dot32(mixed, grad_latent, TN)
    grad_ema = (dot32(grad_latent, shared_b, NT) + grad_mixed) * silu_slope(ema_out)

    dim_late = late(dims)
    results = ema_call(
        functools.partial(ema_backward, rows, dims, parts, halo, hops, chip_links), width,
        [(hidden, late(rows)), (grad_ema, col(rows)), full(seg_lanes), full(edge), (unit, col(2 * dims)),
         (feed, dim_late), (reads, col(2 * dims)), (root, dim_late), (ema_input, dim_late),
         (states, late3(nstate, 8)), (skip, late(1)), (hidden_back, anywhere), zeros]
        + [(attn_grads.reshape(replicas // 2, 2, parts, 3 * depth, vw), anywhere)] * chip_links,
        [(shape_of((rows, width), F32), late(rows)), (shape_of((2 * dims, width), F32), late(2 * dims))]
        + [(shape_of((dims, width), F32), dim_late)] * 3 + [(shape_of((1, width), F32), late(1))]
        + [(shape_of((n, width), BF16), anywhere) for n in hops]
        + [(shape_of((3 * depth, vw), F32), whole(3 * depth, vw))] * chip_links,
        mask_vms + state_vms + [vm(2 * at_rows), vm(at_rows), vm(nstate), table_vm, scale_vm, flat_vm(4, STEP * dims),
                     flat_vm(9, dims), flat_vm(rows), flat_vm(rows)]
        + (reduce_scratch(parts, 3 * depth, vw) if chip_links else []),
        "ema_backward", 4 * mac, 2,
    )
    grad_hidden_ema, output_grad, input_grad, rate_grad, angle_grad, grad_skip = results[:6]
    attn_sum = results[-1] if chip_links else summed_along(summed(attn_grads), grad_skip)
    zero = jnp.zeros((1, width - 3 * latent_width), F32)
    latents = jnp.concatenate([grad_query_gain[None], grad_query_bias[None], grad_key_gain[None], zero], axis=1)
    nexts = jnp.stack([next1, jnp.asarray(next2, F32)])[:, None] * jnp.ones((1, LANES), F32)
    results = end_call(
        replicas, parts, hops,
        (block_in, mean, rho, count, norm_gain[None], hidden_own, grad_hidden_ema, results[6], results[7],
         grad_residual, seg[:, None], seg[None], nexts, grad_shared),
        (output_grad, input_grad, rate_grad, angle_grad, grad_skip,
         jnp.concatenate([grad_ffn_gain, latents], axis=0)),
        ffn_sum,
    )
    in_grad, output_grad, input_grad, rate_grad, angle_grad, skip_grad, two, gain_grad, shared_sum, ffn_sum = results
    latents = two[1].reshape(-1, latent_width)

    cut = lambda g, k: g[k * depth : (k + 1) * depth]
    return (
        block_out, in_grad, gain_grad[0], rate_grad, angle_grad, input_grad, output_grad.reshape(ema_output.shape),
        skip_grad[0], shared_sum, latents[0], latents[1], latents[2], cut(attn_sum, 0), cut(attn_sum, 1),
        cut(attn_sum, 2).T, two[0], cut(ffn_sum, 0), cut(ffn_sum, 1), cut(ffn_sum, 2).T,
    )


def solution(mesh):
    rows, dp, copy = P(BOTH, None), P("dp", None), P()
    wide, tall = P("dp", "tensor"), P("tensor", "dp")
    return jax.shard_map(
        on_device,
        mesh=mesh,
        in_specs=(
            rows, dp, copy, copy, copy, copy, copy, copy, dp, copy, copy, copy, wide, wide, tall, copy, wide, wide,
            tall, rows,
        ),
        out_specs=(
            rows, rows, copy, copy, copy, copy, copy, copy, dp, copy, copy, copy, wide, wide, tall, copy, wide, wide,
            tall,
        ),
        check_vma=False,
    )
```

```python
import functools
import math

import jax
import jax.numpy as jnp
from jax import lax
from jax.experimental import pallas as pl
from jax.experimental.pallas import tpu as pltpu
from jax.experimental.layout import Layout, with_layout_constraint
from jax.sharding import PartitionSpec as P

TN_GROUPS = 16
EPSILON = 1e-05
REACH = 800
STEP = 16
LANES = 128
F32 = jnp.float32
BF16 = jnp.bfloat16
HIGHEST = lax.Precision.HIGHEST
BOTH = ("dp", "tensor")


def dot32(a, b, dims=((1,), (0,)), precision=None):
    return lax.dot_general(a, b, (dims, ((), ())), precision=precision, preferred_element_type=F32)


NT = ((1,), (1,))
TN = ((0,), (0,))


def silu_of(v):
    return v * jax.nn.sigmoid(v)


def silu_slope(v):
    sg = jax.nn.sigmoid(v)
    return sg * (1.0 + v * (1.0 - sg))


def broadcast_row(ref, row):
    return ref[pl.ds(row, 8, stride=0), :]


def rotate(x, shift):
    return pltpu.roll(x, shift % 8, axis=0)


def times(ar, ai, br, bi):
    return ar * br - ai * bi, ar * bi + ai * br


def power_list(dims, q_ref):
    qr, qi = q_ref[:dims], q_ref[dims:]
    out = [(jnp.ones_like(qr), jnp.zeros_like(qr))]
    for n in range(STEP):
        out.append(times(*out[-1], qr, qi))
    return out


def fill_scales(groups, dims, pw, qs):
    step = pw[STEP]
    qs[:dims], qs[dims : 2 * dims] = step
    turn = step
    for _ in range(groups - 1):
        turn = times(*turn, *step)
    for k in range(3):
        base = 2 * dims * (k + 1)
        qs[base : base + dims], qs[base + dims : base + 2 * dims] = turn
        turn = times(*turn, *turn)
    return turn


def fill_read(dims, pw, e_ref, ta):
    e0, e1 = e_ref[:dims], e_ref[dims:]
    for i in range(STEP):
        ta[0, i * dims : (i + 1) * dims], ta[1, i * dims : (i + 1) * dims] = times(e0, e1, *pw[i + 1])


def fill_feed(dims, pw, f_ref, tb):
    f = f_ref[...]
    for i in range(STEP):
        r, m = pw[STEP - 1 - i]
        tb[0, i * dims : (i + 1) * dims], tb[1, i * dims : (i + 1) * dims] = f * r, f * m


def tap_list(dims, pw, e_ref, f_ref):
    e0, e1, f = e_ref[:dims], e_ref[dims:], f_ref[...]
    out = []
    for d in range(STEP):
        row = jnp.sum(f * (e0 * pw[d][0] - e1 * pw[d][1]), axis=0, keepdims=True)
        out.append(jnp.broadcast_to(row, (8, LANES)))
    return out


def chunk_sums(groups, dims, table, source, out, sign):
    def pair(jp, carry):
        acc = [None] * groups
        for i in range(STEP):
            c = [broadcast_row(table.at[p], i * dims + jp * 2 + k) for k in range(2) for p in range(2)]
            for g in range(groups):
                h = source[g * STEP + i]
                terms = [v * h for v in c]
                acc[g] = terms if i == 0 else [u + v for u, v in zip(acc[g], terms)]
        for g in range(groups):
            for k in range(2):
                at = (g * dims + jp * 2 + k) * 2
                out[at] = acc[g][2 * k]
                out[at + 1] = acc[g][2 * k + 1] if sign > 0 else -acc[g][2 * k + 1]
        return carry

    lax.fori_loop(0, dims // 2, pair, 0)


def position_sums(groups, dims, table, states, mask, out, base, sign):
    block = 4

    def some(iq, carry):
        acc = [[None] * block for _ in range(groups)]
        for j in range(dims):
            here = [(states[(g * dims + j) * 2], states[(g * dims + j) * 2 + 1]) for g in range(groups)]
            for i in range(block):
                cr = broadcast_row(table.at[0], (iq * block + i) * dims + j)
                ci = broadcast_row(table.at[1], (iq * block + i) * dims + j)
                for g in range(groups):
                    u, v = cr * here[g][0], ci * here[g][1]
                    term = u - v if sign < 0 else u + v
                    acc[g][i] = term if j == 0 else acc[g][i] + term
        for g in range(groups):
            for i in range(block):
                at = g * STEP + iq * block + i
                out[base + at] = acc[g][i] * mask[at]
        return carry

    lax.fori_loop(0, STEP // block, some, 0)


def scan_states(groups, dims, j, l_ref, qs, cont_ref, mk_ref, inr, ini):
    qr, qi = broadcast_row(qs, j), broadcast_row(qs, dims + j)
    part = [(l_ref[(g * dims + j) * 2], l_ref[(g * dims + j) * 2 + 1]) for g in range(groups)]

    def through(sr, si):
        starts = []
        for g in range(groups):
            starts.append((sr, si))
            keep = cont_ref[g]
            tr, ti = times(qr, qi, sr, si)
            sr, si = keep * tr + part[g][0], keep * ti + part[g][1]
        return starts, sr, si

    _, er, ei = through(inr, ini)
    for k in range(3):
        base = 2 * dims * (k + 1)
        wr, wi = broadcast_row(qs, base + j), broadcast_row(qs, base + dims + j)
        pr, pi = times(wr, wi, rotate(er, 1 << k), rotate(ei, 1 << k))
        keep = mk_ref[k]
        er, ei = er + keep * pr, ei + keep * pi
    first = lax.broadcasted_iota(jnp.int32, (8, LANES), 0) == 0
    starts, _, _ = through(jnp.where(first, inr, rotate(er, 1)), jnp.where(first, ini, rotate(ei, 1)))
    return starts, (er, ei)


def fill_masks(groups, seg_ref, before, seg, kend, keep0, cont, ahead, reverse):
    sub = lax.broadcasted_iota(jnp.int32, (8, LANES), 0)
    for at in range(groups * STEP):
        seg[at] = seg_ref[pl.ds(at, 8, stride=groups * STEP), :]
    ends = [seg[g * STEP + STEP - 1] for g in range(groups)]
    start = jnp.where(sub == 0, before, rotate(ends[-1], 1))
    prior = [start] + ends[:-1]
    same = lambda a, b: (a == b).astype(F32)
    for g in range(groups):
        cont[g] = same(ends[g], prior[g])
        for i in range(STEP):
            here = seg[g * STEP + i]
            keep0[g * STEP + i] = same(here, prior[g])
            kend[g * STEP + i] = same(here, ends[g])
    for k in range(3):
        w = 1 << k
        if reverse:
            ahead[k] = jnp.where(sub + w <= 7, same(start, rotate(start, -w)), 0.0)
        else:
            ahead[k] = jnp.where(sub >= w, same(ends[-1], rotate(ends[-1], w)), 0.0)


ENTER_PLAN = (
    (0, 2, False), (8, 1, False), (9, 1, False), (10, 1, False), (11, 2, False), (12, 1, False), (13, 1, False),
    (14, 2, False), (15, 0, True),
)


def shifted_rows(parts, halo, hops, rows, source, near, zeros, sems, local_sems):
    z = lax.axis_index("tensor")
    late = hops[1]
    early = rows - late
    cut = halo - late
    move = lambda n, src, at, count, first: Along(
        parts, 1, src, near.at[pl.ds(at, count)], sems.at[0, n], sems.at[1, n], first
    )
    last = move(0, source.at[pl.ds(early, late)], cut, late, 0)
    other = move(1, source.at[pl.ds(0, early)], halo - rows, early, 0)
    onward = move(2, near.at[pl.ds(cut, late)], halo - rows - late, late, 1)
    ahead = halo - rows - late
    fills = [(z < 1, rows, halo - rows), (z < 2, late, ahead)]
    if ahead > 0:
        fills.append((z < parts, ahead, 0))

    def each(action):
        action(pltpu.make_async_copy(source, near.at[pl.ds(halo, rows)], local_sems.at[3]))
        for n, (condition, count, at) in enumerate(fills):
            @pl.when(condition)
            def _():
                action(pltpu.make_async_copy(zeros.at[pl.ds(0, count)], near.at[pl.ds(at, count)], local_sems.at[n]))

    def begin():
        last.start()
        each(lambda c: c.start())

    def relay():
        last.wait_recv()
        onward.start()

    def wait():
        other.wait_recv()
        onward.wait_recv()
        for one in (last, other, onward):
            one.wait_send()
        each(lambda c: c.wait())

    return begin, other.start, relay, wait


def normalize(
    parts, x_ref, gain_ref, seg_ref, segc_ref, segr_ref, count_ref, edge_ref, mean_ref, rho_ref, hid, low, tail,
    tail_got, tail_total, tail_sems
):
    rows, width = x_ref.shape
    groups = mean_ref.shape[1]
    table = group_table(width, groups)
    spread_of = lambda v: sum(dot32(p, table, NT) for p in parts_of(v, 3))
    lower = (segc_ref[...] == segr_ref[...]) & (
        lax.broadcasted_iota(jnp.int32, (rows, rows), 0) >= lax.broadcasted_iota(jnp.int32, (rows, rows), 1)
    )
    lower = lower.astype(F32).astype(BF16)
    running_of = lambda v: sum(dot32(lower, p) for p in parts_of(v, 3))
    x = x_ref[...].astype(F32)
    running = [
        running_of(dot32(x_ref[...], table)),
        running_of(sum(dot32(p, table) for p in parts_of(x * x, 2))),
    ]
    for half in range(2):
        tail[half, :, :groups] = running[half][rows - 8 :]
    moves = [Along(parts, hop, tail, tail_got.at[hop - 1], tail_sems.at[0, hop - 1], tail_sems.at[1, hop - 1])
             for hop in (1, 2)]
    for move in moves:
        move.start()
    tail_total[...] = jnp.zeros_like(tail_total)
    for hop, move in enumerate(moves):
        def arrived(hop=hop):
            tail_total[...] += edge_ref[1 + hop : 2 + hop, :] * tail_got[hop]
        move.wait_recv(arrived)
    heads = (seg_ref[:, 0:1] == edge_ref[0:1, 0:1]).astype(F32)
    count = count_ref[...]
    first, second = (running[half] + heads * tail_total[half, 7:8, :groups] for half in range(2))
    mean = first / count
    rho = lax.rsqrt(second / count - mean * mean + EPSILON)
    mean_ref[...] = mean
    rho_ref[...] = rho
    hidden = (x - spread_of(mean)) * spread_of(rho) * gain_ref[...]
    low[...] = hidden.astype(BF16)
    for k in range(width // LANES):
        hid[k] = hidden[:, k * LANES : (k + 1) * LANES]
    for move in moves:
        move.wait_send()


def ema_forward(
    rows, dims, parts, halo, hops, hosted, x_ref, gain_ref, seg_ref, segc_ref, segr_ref, count_ref, edge_ref, q_ref,
    f_ref, e_ref, skip_ref, zeros_ref, *refs
):
    refs = list(refs)
    pack_ref = refs.pop(0) if hosted else None
    out_ref, m_ref, s_ref, hidden_ref, mean_ref, rho_ref, near_ref = (refs.pop(0) for _ in range(7))
    all_ref = refs.pop(0) if hosted else None
    hid, low, tail, tail_got, tail_total, tail_sems, seg, kend, keep0, cont, ahead = (refs.pop(0) for _ in range(11))
    hs, table, qs, parts_all, ends, got, entry, state_sems, near_sems, local_sems, *rest = refs
    groups = rows // (8 * STEP)
    step = pl.program_id(0)
    blocks = parts_all.shape[0]
    k = step % blocks
    stages = gather_stages(parts, pack_ref, all_ref, *rest) if hosted else []
    near_begin, near_more, near_relay, near_wait = shifted_rows(parts, halo, hops, rows, low, near_ref, zeros_ref, near_sems, local_sems)
    states = lambda hop, at: Along(
        parts, hop, ends.at[at], got.at[hop - 1, at], state_sems.at[0, hop - 1, at], state_sems.at[1, hop - 1, at]
    )

    @pl.when(step == 0)
    def _():
        greet(parts, 3 if hosted else 0)

    @pl.when(step == blocks)
    def _():
        near_more()

    @pl.when(step == blocks + 2)
    def _():
        near_relay()

    if hosted:
        run_stages(stages, step, ENTER_PLAN, False)

    @pl.when(step == 0)
    def _():
        normalize(
            parts, x_ref, gain_ref, seg_ref, segc_ref, segr_ref, count_ref, edge_ref, mean_ref, rho_ref, hid, low,
            tail, tail_got, tail_total, tail_sems,
        )
        near_begin()
        fill_masks(groups, seg_ref, edge_ref[0:1, :], seg, kend, keep0, cont, ahead, False)

    pw = power_list(dims, q_ref)
    turn = fill_scales(groups, dims, pw, qs)

    @pl.when(step < blocks)
    def _():
        fill_feed(dims, pw, f_ref, table)
        for at in range(groups * STEP):
            hs[at] = hid[k, pl.ds(at, 8, stride=groups * STEP), :] * kend[at]
        chunk_sums(groups, dims, table, hs, parts_all.at[k], 1)

        def one(j, carry):
            zero = jnp.zeros((8, LANES), F32)
            _, last = scan_states(groups, dims, j, parts_all.at[k], qs, cont, ahead, zero, zero)
            ends[k, pl.ds(j, 1), :] = last[0][7:8]
            ends[k, pl.ds(dims + j, 1), :] = last[1][7:8]
            return carry

        lax.fori_loop(0, dims, one, 0)
        for hop in (1, 2):
            states(hop, k).start()

    @pl.when(step >= blocks)
    def _():
        hidden_ref[...] = hid[k]
        entry[...] = jnp.zeros_like(entry)

        def near_one():
            entry[...] = got[0, k]

        def far_one():
            link = edge_ref[2:3, :]
            r, i = times(*turn, got[1, k, :dims], got[1, k, dims:])
            entry[:dims] += link * r
            entry[dims:] += link * i

        states(1, k).wait_recv(near_one)
        states(2, k).wait_recv(far_one)
        ema_read(
            groups, dims, hid.at[k], seg, keep0, pw, f_ref, e_ref, cont, ahead, parts_all.at[k], entry, skip_ref,
            out_ref, m_ref, s_ref, hs, table, qs,
        )

    @pl.when(step == 2 * blocks - 1)
    def _():
        for at in range(blocks):
            for hop in (1, 2):
                states(hop, at).wait_send()
        near_wait()

    if hosted:
        run_stages(stages, step, ENTER_PLAN, True)


def ema_read(
    groups, dims, h_ref, seg_ref, k0_ref, pw, f_ref, e_ref, cont_ref, mk_ref, l_ref, in_ref, skip_ref, out_ref, m_ref,
    s_ref, hs, ta, qs
):
    first = lax.broadcasted_iota(jnp.int32, (8, LANES), 0) == 0
    fill_read(dims, pw, e_ref, ta)
    taps = tap_list(dims, pw, e_ref, f_ref)

    def one(j, carry):
        inr = jnp.where(first, broadcast_row(in_ref, j), 0.0)
        ini = jnp.where(first, broadcast_row(in_ref, dims + j), 0.0)
        starts, _ = scan_states(groups, dims, j, l_ref, qs, cont_ref, mk_ref, inr, ini)
        for g in range(groups):
            s_ref[(g * dims + j) * 2] = starts[g][0]
            s_ref[(g * dims + j) * 2 + 1] = starts[g][1]
        return carry

    lax.fori_loop(0, dims, one, 0)
    for at in range(groups * STEP):
        hs[at] = h_ref[pl.ds(at, 8, stride=groups * STEP), :]
    position_sums(groups, dims, ta, s_ref, k0_ref, hs, groups * STEP, -1)
    tap0 = taps[0] + jnp.broadcast_to(skip_ref[...], (8, LANES))

    def within(g, carry):
        for i in range(STEP):
            at = g * STEP + i
            seg = seg_ref[at]
            out = hs[groups * STEP + at] + tap0 * hs[at]
            for s in range(i):
                src = g * STEP + s
                out = out + taps[i - s] * jnp.where(seg_ref[src] == seg, hs[src], 0.0)
            out_ref[pl.ds(at, 8, stride=groups * STEP), :] = out
        return carry

    lax.fori_loop(0, groups, within, 0)
    m_ref[...] = silu_of(out_ref[...]).astype(m_ref.dtype)


def reverse_states(groups, dims, j, g_ref, qs, cont_ref, mkr_ref, inr, ini):
    qr, qi = broadcast_row(qs, j), broadcast_row(qs, dims + j)
    part = [(g_ref[(g * dims + j) * 2], g_ref[(g * dims + j) * 2 + 1]) for g in range(groups)]

    def through(yr, yi):
        ends = [None] * groups
        for g in reversed(range(groups)):
            ends[g] = (yr, yi)
            keep = cont_ref[g]
            tr, ti = qr * yr + qi * yi, qr * yi - qi * yr
            yr, yi = keep * tr + part[g][0], keep * ti + part[g][1]
        return ends, yr, yi

    _, fr, fi = through(inr, ini)
    for k in range(3):
        base = 2 * dims * (k + 1)
        wr, wi = broadcast_row(qs, base + j), broadcast_row(qs, base + dims + j)
        pr, pi = rotate(fr, -(1 << k)), rotate(fi, -(1 << k))
        keep = mkr_ref[k]
        fr, fi = fr + keep * (wr * pr + wi * pi), fi + keep * (wr * pi - wi * pr)
    last = lax.broadcasted_iota(jnp.int32, (8, LANES), 0) == 7
    ends, _, _ = through(jnp.where(last, inr, rotate(fr, -1)), jnp.where(last, ini, rotate(fi, -1)))
    return ends, (fr, fi)


REDUCE_PLAN = (
    (0, 1, False), (5, 1, False), (7, 1, False), (8, 1, False), (9, 1, False), (12, 1, False), (14, 1, False),
    (15, 0, True),
)


def ema_backward(
    rows, dims, parts, halo, hops, hosted, h_ref, de_ref, rows_seg_ref, edge_ref, q_ref, f_ref, e_ref, root_ref,
    feed_ref, s_ref, skip_ref, back_ref, zeros_ref, *refs
):
    refs = list(refs)
    pack_ref = refs.pop(0) if hosted else None
    outs = [refs.pop(0) for _ in range(6)]
    back = [refs.pop(0) for _ in hops]
    sum_ref = refs.pop(0) if hosted else None
    seg_ref, kend_ref, k0_ref, cont_ref, mkr_ref = (refs.pop(0) for _ in range(5))
    pulls, heads, got, entry, state_sems, back_sems, local_sems, *rest = refs
    held, rest = rest[:9], rest[9:]
    hs, ds, la, table, qs = held[:5]
    groups = rows // (8 * STEP)
    step = pl.program_id(0)
    z = lax.axis_index("tensor")
    blocks = pulls.shape[0]
    k = step % blocks
    stages = reduce_stages(parts, pack_ref, sum_ref, *rest) if hosted else []
    states = lambda hop, at: Along(
        parts, -hop, heads.at[at], got.at[hop - 1, at], state_sems.at[0, hop - 1, at], state_sems.at[1, hop - 1, at]
    )
    moves, fills, end = [], [], halo
    for h, n in enumerate(hops):
        moves.append(Along(parts, -h - 1, back_ref.at[pl.ds(end - n, n)], back[h], back_sems.at[0, h], back_sems.at[1, h]))
        fills.append((z + h + 1 >= parts, (zeros_ref.at[pl.ds(0, n)], back[h], local_sems.at[h])))
        end -= n

    def filling(action):
        for condition, copy in fills:
            @pl.when(condition)
            def _():
                action(pltpu.make_async_copy(*copy))

    @pl.when(step == 0)
    def _():
        greet(parts, 3 if hosted else 0)
        filling(lambda c: c.start())
        fill_masks(groups, rows_seg_ref, edge_ref[0:1, :], seg_ref, kend_ref, k0_ref, cont_ref, mkr_ref, True)

    @pl.when(step == blocks)
    def _():
        for move in moves:
            move.start()

    if hosted:
        run_stages(stages, step, REDUCE_PLAN, False)
    pw = power_list(dims, q_ref)
    turn = fill_scales(groups, dims, pw, qs)

    @pl.when(step < blocks)
    def _():
        fill_read(dims, pw, e_ref, table)
        for at in range(groups * STEP):
            ds[at] = de_ref[pl.ds(at, 8, stride=groups * STEP), :] * k0_ref[at]
        chunk_sums(groups, dims, table, ds, pulls.at[k], -1)

        def one(j, carry):
            zero = jnp.zeros((8, LANES), F32)
            _, head = reverse_states(groups, dims, j, pulls.at[k], qs, cont_ref, mkr_ref, zero, zero)
            heads[k, pl.ds(j, 1), :] = head[0][0:1]
            heads[k, pl.ds(dims + j, 1), :] = head[1][0:1]
            return carry

        lax.fori_loop(0, dims, one, 0)
        for hop in (1, 2):
            states(hop, k).start()

    @pl.when(step >= blocks)
    def _():
        entry[...] = jnp.zeros_like(entry)

        def near_one():
            entry[...] = got[0, k]

        def far_one():
            cross = edge_ref[3:4, :]
            r, i = times(turn[0], -turn[1], got[1, k, :dims], got[1, k, dims:])
            entry[:dims] += cross * r
            entry[dims:] += cross * i

        states(1, k).wait_recv(near_one)
        states(2, k).wait_recv(far_one)
        ema_grads(
            groups, dims, h_ref, de_ref, seg_ref, kend_ref, k0_ref, pw, f_ref, e_ref, root_ref, feed_ref,
            cont_ref, mkr_ref, pulls.at[k], entry, s_ref, skip_ref, *outs, *held,
        )

    @pl.when(step == 2 * blocks - 1)
    def _():
        for at in range(blocks):
            for hop in (1, 2):
                states(hop, at).wait_send()
        for move in moves:
            move.wait_recv()
            move.wait_send()
        filling(lambda c: c.wait())

    if hosted:
        run_stages(stages, step, REDUCE_PLAN, True)


def ema_grads(
    groups, dims, h_ref, de_ref, seg_ref, kend_ref, k0_ref, pw, f_ref, e_ref, root_ref, feed_ref, cont_ref,
    mkr_ref, g_ref, in_ref, s_ref, skip_ref, dh_ref, ge_ref, gf_ref, gr_ref, ga_ref, gs_ref, hs, ds, la, tb, qs, pf,
    red, hn, dn
):
    last = lax.broadcasted_iota(jnp.int32, (8, LANES), 0) == 7
    fill_feed(dims, pw, f_ref, tb)
    taps = tap_list(dims, pw, e_ref, f_ref)
    for i in range(STEP):
        at = slice(i * dims, (i + 1) * dims)
        pf[0, at], pf[1, at] = pw[i + 1]
        pf[2, at], pf[3, at] = pw[STEP - 1 - i]

    def one(j, carry):
        inr = jnp.where(last, broadcast_row(in_ref, j), 0.0)
        ini = jnp.where(last, broadcast_row(in_ref, dims + j), 0.0)
        ends, _ = reverse_states(groups, dims, j, g_ref, qs, cont_ref, mkr_ref, inr, ini)
        qr = jnp.zeros((8, LANES), F32)
        qi = jnp.zeros((8, LANES), F32)
        for g in range(groups):
            yr, yi = ends[g]
            la[(g * dims + j) * 2] = yr
            la[(g * dims + j) * 2 + 1] = yi
            keep = cont_ref[g]
            sr, si = s_ref[(g * dims + j) * 2], s_ref[(g * dims + j) * 2 + 1]
            qr = qr + keep * (yr * sr + yi * si)
            qi = qi + keep * (yi * sr - yr * si)
        red[0, pl.ds(j, 1), :] = jnp.sum(qr, axis=0, keepdims=True)
        red[1, pl.ds(j, 1), :] = jnp.sum(qi, axis=0, keepdims=True)
        return carry

    lax.fori_loop(0, dims, one, 0)
    total = jnp.zeros((8, LANES), F32)
    for at in range(groups * STEP):
        h = h_ref[pl.ds(at, 8, stride=groups * STEP), :]
        d = de_ref[pl.ds(at, 8, stride=groups * STEP), :]
        hs[at] = h
        ds[at] = d
        hn[pl.ds(at, 8, stride=groups * STEP), :] = h * kend_ref[at]
        dn[pl.ds(at, 8, stride=groups * STEP), :] = d * k0_ref[at]
        total = total + h * d
    gs_ref[...] = jnp.sum(total, axis=0, keepdims=True)
    position_sums(groups, dims, tb, la, kend_ref, hs, groups * STEP, 1)
    tap0 = taps[0] + jnp.broadcast_to(skip_ref[...], (8, LANES))

    def within(g, kacc):
        kacc = list(kacc)
        for s in range(STEP):
            at = g * STEP + s
            seg = seg_ref[at]
            h = hs[at]
            out = hs[groups * STEP + at] + tap0 * ds[at]
            for t in range(s + 1, STEP):
                d = jnp.where(seg_ref[g * STEP + t] == seg, ds[g * STEP + t], 0.0)
                out = out + taps[t - s] * d
                kacc[t - s] = kacc[t - s] + h * d
            dh_ref[pl.ds(at, 8, stride=groups * STEP), :] = out
        return tuple(kacc)

    kacc = lax.fori_loop(0, groups, within, (total,) + (jnp.zeros((8, LANES), F32),) * (STEP - 1))

    width = 4
    place = (lax.broadcasted_iota(jnp.int32, (STEP, LANES), 0) + 1).astype(F32)

    def tables(jq, carry):
        def chunk(n, acc):
            sub, g = n // groups, n % groups
            d0, d1 = (dn[pl.ds(pl.multiple_of(n * STEP + 8 * p, 8), 8), :] for p in range(2))
            h0, h1 = (hn[pl.ds(pl.multiple_of(n * STEP + 8 * p, 8), 8), :] for p in range(2))
            out = []
            for k in range(width):
                at = (g * dims + jq * width + k) * 2
                sr, si = (s_ref[at + p, pl.ds(sub, 8, stride=0), :] for p in range(2))
                yr, yi = (la[at + p, pl.ds(sub, 8, stride=0), :] for p in range(2))
                a = acc[8 * k : 8 * k + 8]
                out += [a[0] + d0 * sr, a[1] + d1 * sr, a[2] - d0 * si, a[3] - d1 * si]
                out += [a[4] + h0 * yr, a[5] + h1 * yr, a[6] + h0 * yi, a[7] + h1 * yi]
            return tuple(out)

        acc = lax.fori_loop(0, 8 * groups, chunk, (jnp.zeros((8, LANES), F32),) * (8 * width))
        for k in range(width):
            j = jq * width + k
            ar, ai, br, bi = (
                jnp.concatenate([acc[8 * k + 2 * p], acc[8 * k + 2 * p + 1]], axis=0) for p in range(4)
            )
            pr, pi, wr, wi = (pf[p, pl.ds(j, STEP, stride=dims), :] for p in range(4))
            ur, ui = ar * pr + ai * pi, ai * pr - ar * pi
            vr, vi = br * wr + bi * wi, bi * wr - br * wi
            rest = STEP - place
            sums = (ur, ui, place * ur, place * ui, vr, rest * vr, rest * vi)
            for p, v in enumerate(sums):
                red[2 + p, pl.ds(j, 1), :] = jnp.sum(v, axis=0, keepdims=True)
        return carry

    lax.fori_loop(0, dims // width, tables, 0)
    e0, e1, f = e_ref[:dims], e_ref[dims:], f_ref[...]
    zero = jnp.zeros((dims, LANES), F32)
    tr, ti, ur, ui = zero, zero, zero, zero
    for d in range(STEP):
        tap = jnp.broadcast_to(jnp.sum(kacc[d], axis=0, keepdims=True), (dims, LANES))
        r, m = tap * pw[d][0], tap * pw[d][1]
        tr, ti = tr + r, ti - m
        if d > 0:
            ur, ui = ur + d * r, ui - d * m
    ge_ref[:dims] = red[2] + f * tr
    ge_ref[dims:] = red[3] + f * ti
    gf = red[6] + e0 * tr + e1 * ti
    xr, xi = red[4] + f * ur, red[5] + f * ui
    lr = e0 * xr + e1 * xi + f * red[7]
    li = e0 * xi - e1 * xr + f * red[8]
    zr, zi = pw[STEP]
    lr = lr + STEP * (red[0] * zr + red[1] * zi)
    li = li + STEP * (red[1] * zr - red[0] * zi)
    root = root_ref[...]
    gf_ref[...] = gf * root
    gr_ref[...] = gf * feed_ref[...] * (1.0 - root * root) / root - lr
    ga_ref[...] = li


def whole(*shape):
    return pl.BlockSpec(shape, lambda i: (0,) * len(shape))


def ema_call(body, width, ins, outs, scratch, name, flops, collective_id):
    return pl.pallas_call(
        body,
        grid=(2 * (width // LANES),),
        in_specs=[s for _, s in ins],
        out_specs=[s for _, s in outs],
        out_shape=[o for o, _ in outs],
        scratch_shapes=scratch,
        compiler_params=pltpu.CompilerParams(
            vmem_limit_bytes=60 << 20, collective_id=collective_id, has_side_effects=True
        ),
        cost_estimate=pl.CostEstimate(flops=flops // 1000, bytes_accessed=1024, transcendentals=0),
        name=name,
    )(*[a for a, _ in ins])


def merged(ref):
    v = ref[...]
    return v.reshape(-1, v.shape[-1])


GATHER_PLAN = ((0, 2, False), (1, 1, False), (2, 1, False), (3, 1, False), (3, 0, True))


def attend_kernel(halo, parts, hops, hosted, q_ref, own_k_ref, seg_ref, segk_ref, h_ref, m_ref, x_ref, gain_ref, wv_ref, wg_ref,
                  wo_ref, *refs):
    refs = list(refs)
    pack_ref = refs.pop(0) if hosted else None
    p_ref, vp_ref, v_ref, gp_ref, o_ref, g_ref, y_ref, n_ref, k_ref = (refs.pop(0) for _ in range(9))
    all_ref = refs.pop(0) if hosted else None
    pb_ref, keys, key_sems, *rest = refs
    t = pl.program_id(0)
    z = lax.axis_index("tensor")
    rows = q_ref.shape[0]
    stages = gather_stages(parts, pack_ref, all_ref, *rest) if hosted else []
    moves, places, end = [], [], halo
    for h, n in enumerate(hops):
        place = pl.ds(end - n, n)
        moves.append(Along(parts, h + 1, own_k_ref.at[pl.ds(rows - n, n)], keys.at[place], key_sems.at[0, h], key_sems.at[1, h]))
        places.append((h + 1, slice(end - n, end)))
        end -= n

    @pl.when(t == 0)
    def _():
        greet(parts, 3 if hosted else 0)
        for move in moves:
            move.start()
        keys[halo:, :] = own_k_ref[...]
        if end > 0:
            keys[:end, :] = jnp.zeros((end, keys.shape[1]), BF16)
        for first, place in places:
            @pl.when(z < first)
            def _():
                keys[place, :] = jnp.zeros((place.stop - place.start, keys.shape[1]), BF16)

    if hosted:
        run_stages(stages, t, GATHER_PLAN, False)

    vp = dot32(h_ref[...], merged(wv_ref))
    v = silu_of(vp).astype(BF16)
    vp_ref[...] = vp.astype(BF16)
    v_ref[...] = v
    gp = dot32(m_ref[...], merged(wg_ref))
    gp_ref[...] = gp.astype(BF16)

    @pl.when(t == 0)
    def _():
        for move in moves:
            move.wait_recv()
            move.wait_send()
        k_ref[...] = keys[...]
        count = keys.shape[0]
        scores = dot32(q_ref[...], keys[...], NT) * (1.0 / math.sqrt(q_ref.shape[1]))
        at_row = lax.broadcasted_iota(jnp.int32, (rows, count), 0)
        at_key = lax.broadcasted_iota(jnp.int32, (rows, count), 1)
        allowed = (at_key <= at_row + halo) & (segk_ref[...] == seg_ref[...])
        scores = jnp.where(allowed, scores, -1e30)
        raw = jnp.exp(scores - jnp.max(scores, axis=1, keepdims=True))
        p = raw / jnp.sum(raw, axis=1, keepdims=True)
        p_ref[...] = p
        pb_ref[...] = p.astype(BF16)
        y_ref[...] = x_ref[...].astype(F32)

    o = dot32(pb_ref[...], v)
    o_ref[...] = o.astype(BF16)
    g = (silu_of(gp) * o).astype(BF16)
    g_ref[...] = g
    y_ref[...] += dot32(g, merged(wo_ref), NT)

    @pl.when(t == pl.num_programs(0) - 1)
    def _():
        y = y_ref[...]
        rr = lax.rsqrt(jnp.mean(y * y, axis=1, keepdims=True) + EPSILON)
        n_ref[...] = (y * rr * gain_ref[...]).astype(BF16)

    if hosted:
        run_stages(stages, t, GATHER_PLAN, True)


def ffn_kernel(
    y_ref, n_ref, og_ref, gain_ref, w1_ref, w3_ref, w2_ref, out_ref, dy_ref, branch_ref, gain_grad_ref, grads_ref,
    acc, dn,
):
    t = pl.program_id(0)

    @pl.when(t == 0)
    def _():
        acc[...] = y_ref[...]
        dn[...] = jnp.zeros_like(dn)

    w1, w3, w2 = merged(w1_ref), merged(w3_ref), merged(w2_ref)
    nn, og = n_ref[...], og_ref[...]
    u1, u3 = dot32(nn, w1), dot32(nn, w3)
    sg = jax.nn.sigmoid(u1)
    act = u1 * sg
    hd = (act * u3).astype(BF16)
    acc[...] += dot32(hd, w2, NT)
    dh = dot32(og, w2)
    d1 = (dh * u3 * (sg * (1.0 + u1 * (1.0 - sg)))).astype(BF16)
    d3 = (dh * act).astype(BF16)
    dn[...] += dot32(d1, w1, NT) + dot32(d3, w3, NT)
    depth = grads_ref.shape[3]
    for k, (a, b) in enumerate(((nn, d1), (nn, d3), (og, hd))):
        grads_ref[:, 0, k] = dot32(a, b, TN).astype(BF16).reshape(-1, depth, b.shape[1])

    @pl.when(t == pl.num_programs(0) - 1)
    def _():
        out_ref[...] = acc[...].astype(BF16)
        y = y_ref[...]
        rr = lax.rsqrt(jnp.mean(y * y, axis=1, keepdims=True) + EPSILON)
        nh = y * rr
        g = dn[...]
        gain_grad_ref[...] = jnp.sum(nh * g, axis=0, keepdims=True)
        scaled = g * gain_ref[...]
        dy = og.astype(F32) + rr * (scaled - nh * jnp.mean(nh * scaled, axis=1, keepdims=True))
        dy_ref[...] = dy
        branch_ref[...] = dy.astype(BF16)


def attend_back_kernel(
    halo, parts, hops, br_ref, p_ref, h_ref, m_ref, q_ref, k_ref, vp_ref, v_ref, gp_ref, o_ref, g_ref, wv_ref, wg_ref, wo_ref,
    dq_ref, dk_ref, dhn_ref, dh_ref, dm_ref, grads_ref, dp, dhv, pb_ref, give, got, key_sems,
):
    t = pl.program_id(0)
    rows = br_ref.shape[0]
    moves, end = [], halo
    for h, n in enumerate(hops):
        moves.append((n, Along(parts, -h - 1, give.at[pl.ds(end - n, n)], got.at[h, pl.ds(0, n)], key_sems.at[0, h], key_sems.at[1, h])))
        end -= n

    @pl.when(t == 0)
    def _():
        greet(parts, 0)
        pb_ref[...] = p_ref[...].astype(BF16)
        dp[...] = jnp.zeros_like(dp)
        dhv[...] = jnp.zeros_like(dhv)
        dm_ref[...] = jnp.zeros_like(dm_ref)

    branch, pb = br_ref[...], pb_ref[...]
    dg = dot32(branch, merged(wo_ref))
    gp = gp_ref[...].astype(F32)
    sg = jax.nn.sigmoid(gp)
    da = (dg * (gp * sg)).astype(BF16)
    dr = (dg * o_ref[...].astype(F32) * (sg * (1.0 + gp * (1.0 - sg)))).astype(BF16)
    dp[...] += dot32(da, v_ref[...], NT)

    @pl.when(t == pl.num_programs(0) - 1)
    def _():
        scale = 1.0 / math.sqrt(q_ref.shape[1])
        p = p_ref[...]
        d = dp[...]
        ds = (p * (d - jnp.sum(p * d, axis=1, keepdims=True))).astype(BF16)
        dk = dot32(ds, q_ref[...], TN) * scale
        give[...] = dk[:halo].astype(BF16)
        for _, move in moves:
            move.start()
        dk_ref[...] = dk[halo:]
        dq_ref[...] = dot32(ds, k_ref[...]) * scale

    dv = dot32(pb, da, TN)
    dvp = (dv * silu_slope(vp_ref[...].astype(F32))).astype(BF16)
    dhv[...] += dot32(dvp, merged(wv_ref), NT)
    dm_ref[...] += dot32(dr, merged(wg_ref), NT)
    depth = grads_ref.shape[3]
    for k, (a, b) in enumerate(((h_ref[...], dvp), (m_ref[...], dr), (branch, g_ref[...]))):
        grads_ref[:, 0, k] = dot32(a, b, TN).astype(BF16).reshape(-1, depth, b.shape[1])

    @pl.when(t == pl.num_programs(0) - 1)
    def _():
        dhn_ref[...] = dhv[:halo, :].astype(BF16)
        dh_ref[...] = dhv[halo:, :]
        for h, (n, move) in enumerate(moves):
            def arrived(h=h, n=n):
                dk_ref[rows - n :, :] += got[h, :n, :].astype(F32)
            move.wait_recv(arrived)
            move.wait_send()


def stage_call(body, steps, ins, outs, scratch, name, flops, collective_id=None):
    def spec(v, how):
        if how == "all":
            return pl.BlockSpec(v.shape, lambda t: (0,) * v.ndim)
        if how == "col":
            return pl.BlockSpec((v.shape[0], v.shape[1] // steps), lambda t: (0, t))
        return how

    outs = [(jax.ShapeDtypeStruct(s, d), how) for s, d, how in outs]
    return pl.pallas_call(
        body,
        grid=(steps,),
        in_specs=[spec(v, how) for v, how in ins],
        out_specs=[spec(v, how) for v, how in outs],
        out_shape=[v for v, _ in outs],
        scratch_shapes=scratch,
        compiler_params=pltpu.CompilerParams(
            vmem_limit_bytes=60 << 20, collective_id=collective_id, has_side_effects=collective_id is not None
        ),
        cost_estimate=pl.CostEstimate(flops=flops // 1000, bytes_accessed=1024, transcendentals=0),
        name=name,
    )(*[v for v, _ in ins])


def flipped(d, k):
    return d + (1 - 2 * ((d // (1 << k)) % 2)) * (1 << k)


def greet(parts, dp_bits):
    d, z = lax.axis_index("dp"), lax.axis_index("tensor")
    barrier = pltpu.get_barrier_semaphore()
    for k in range(dp_bits):
        pl.semaphore_signal(barrier, inc=1, device_id=(flipped(d, k), z), device_id_type=pl.DeviceIdType.MESH)
    for step in (-2, -1, 1, 2):
        @pl.when((z + step >= 0) & (z + step < parts))
        def _():
            pl.semaphore_signal(barrier, inc=1, device_id=(d, z + step), device_id_type=pl.DeviceIdType.MESH)
    pl.semaphore_wait(barrier, dp_bits + jnp.minimum(z, 2) + jnp.minimum(parts - 1 - z, 2))


class Along:
    def __init__(self, parts, hop, src, dst, send_sem, recv_sem, first=0):
        d, z = lax.axis_index("dp"), lax.axis_index("tensor")
        to = z + hop
        self.sends = (to >= 0) & (to < parts) & (z >= first)
        self.gets = (z - hop >= first) & (z - hop < parts)
        self.make = lambda: pltpu.make_async_remote_copy(
            src_ref=src, dst_ref=dst, send_sem=send_sem, recv_sem=recv_sem,
            device_id=(d, jnp.clip(to, 0, parts - 1)), device_id_type=pl.DeviceIdType.MESH,
        )

    def start(self):
        @pl.when(self.sends)
        def _():
            self.make().start()

    def wait_send(self):
        @pl.when(self.sends)
        def _():
            self.make().wait_send()

    def wait_recv(self, then=lambda: None):
        @pl.when(self.gets)
        def _():
            self.make().wait_recv()
            then()


def gather_stages(parts, pack_ref, out_ref, sems, own_sem):
    d, z = lax.axis_index("dp"), lax.axis_index("tensor")
    total = pack_ref.shape[0]
    cut = total // 32 * 16
    upper, lower, full = pl.ds(0, cut), pl.ds(cut, total - cut), pl.ds(0, total)
    core, first, second = (flipped(d, k) for k in range(3))
    across = first + second - d
    MESH = pl.DeviceIdType.MESH

    LINE, TO_FIRST, TO_SECOND, UP, DOWN, C_OWN, C_FIRST, C_SECOND, C_UP, C_DOWN = range(10)

    def copy(kind, b, source, part, dp_to, z_to):
        here = out_ref.at[source, b, part]
        return pltpu.make_async_remote_copy(
            src_ref=here, dst_ref=here, send_sem=sems.at[0, kind, b], recv_sem=sems.at[1, kind, b],
            device_id=(dp_to, z_to), device_id_type=MESH,
        )

    def begin():
        mine = pltpu.make_async_copy(pack_ref, out_ref.at[d, z], own_sem)
        mine.start()
        mine.wait()

    def spread_block(b):
        copy(TO_FIRST, b, d, full, first, z).start()
        copy(TO_SECOND, b, d, full, second, z).start()
        copy(C_OWN, b, d, full, core, z).start()

    def along(b, step):
        @pl.when((z + step >= 0) & (z + step < parts))
        def _():
            here = out_ref.at[d, b]
            pltpu.make_async_remote_copy(
                src_ref=here, dst_ref=here, send_sem=sems.at[0, LINE + (10 if step > 0 else 11), b],
                recv_sem=sems.at[1, LINE, b], device_id=(d, z + step), device_id_type=MESH,
            ).start()

    def relay(b):
        copy(TO_FIRST, b, first, full, first, z).wait_recv()
        copy(UP, b, first, upper, second, z).start()
        copy(C_FIRST, b, first, full, core, z).start()
        copy(TO_SECOND, b, second, full, second, z).wait_recv()
        copy(DOWN, b, second, lower, first, z).start()
        copy(C_SECOND, b, second, full, core, z).start()

    def corner(b):
        copy(UP, b, across, upper, second, z).wait_recv()
        copy(C_UP, b, across, upper, core, z).start()
        copy(DOWN, b, across, lower, first, z).wait_recv()
        copy(C_DOWN, b, across, lower, core, z).start()

    def at_distance(dist, action):
        for side in ((0,) if dist == 0 else (-1, 1)):
            b = z + side * dist
            @pl.when((b >= 0) & (b < parts))
            def _():
                action(b, side)

    def arrive(b, side):
        if side != 0:
            copy(LINE, b, d, full, d, z).wait_recv()
        if side <= 0:
            along(b, 1)
        if side >= 0:
            along(b, -1)
        spread_block(b)

    def finish():
        other_first, other_second = core + first - d, core + second - d
        for b in range(parts):
            for kind, source, part in ((C_OWN, core, full), (C_FIRST, other_first, full), (C_SECOND, other_second, full),
                                       (C_UP, core + across - d, upper), (C_DOWN, core + across - d, lower)):
                copy(kind, b, source, part, core, z).wait_recv()
            for kind, source, part in ((TO_FIRST, d, full), (TO_SECOND, d, full), (C_OWN, d, full), (UP, first, upper),
                                       (DOWN, second, lower), (C_FIRST, first, full), (C_SECOND, second, full),
                                       (C_UP, across, upper), (C_DOWN, across, lower)):
                copy(kind, b, source, part, core, z).wait_send()
            for step, slot in ((1, 10), (-1, 11)):
                @pl.when((z + step >= 0) & (z + step < parts) & (step * (z - b) >= 0))
                def _():
                    copy(slot, b, d, full, core, z).wait_send()

    stages = [begin]
    for dist in range(parts + 2):
        if dist < parts:
            stages.append(functools.partial(at_distance, dist, arrive))
        if 1 <= dist < parts + 1:
            stages.append(functools.partial(at_distance, dist - 1, lambda b, side: relay(b)))
        if dist >= 2:
            stages.append(functools.partial(at_distance, dist - 2, lambda b, side: corner(b)))
    return stages + [finish]


def gather_scratch(parts):
    return [pltpu.SemaphoreType.DMA((2, 12, parts)), pltpu.SemaphoreType.DMA]


def run_stages(stages, step, plan, late):
    at = 0
    for when, count, end in plan:
        here = stages[at : at + count] if count else stages[at:]
        at += len(here)
        if end == late:
            @pl.when(step == when)
            def _():
                for stage in here:
                    stage()


R_CORE, R_FIRST, R_FIRST2, R_SECOND, R_SECOND2, R_UP, R_DOWN, R_RIGHT, R_LEFT = range(9)


def reduce_scratch(parts, rows, columns):
    upper = rows // 32 * 16
    vm = lambda *n: pltpu.VMEM((*n, columns), BF16)
    return [
        vm(parts, 4, rows), vm(parts, 4, rows), vm(parts, 2, upper), vm(parts, 2, rows - upper), vm(parts, upper),
        vm(parts, rows - upper), vm(2, parts, rows), pltpu.SemaphoreType.DMA((2, 9, parts)),
        pltpu.SemaphoreType.DMA((parts,)),
    ]


def reduce_stages(parts, pack, out, acc, got_core, got_first, got_second, got_up, got_down, got_line, sems, load_sems):
    d, z = lax.axis_index("dp"), lax.axis_index("tensor")
    MESH = pl.DeviceIdType.MESH
    rows = acc.shape[2]
    cut = rows // 32 * 16
    upper, lower = pl.ds(0, cut), pl.ds(cut, rows - cut)
    me, core = d // 2, d % 2
    bit = lambda k: (me // (1 << k)) % 2
    first = me + (1 - 2 * bit(0))
    second = me + 2 * (1 - 2 * bit(1))
    across = first + second - me
    on = lambda p: 2 * p + core
    far = z // (parts // 2)
    near_end = z + far * (parts - 1 - 2 * z)

    def unit(s):
        t = (parts - 1 - s) + near_end * ((3, 0, 2, 1)[s] - (parts - 1 - s))
        return t + far * (parts - 1 - 2 * t)

    def copy(kind, t, src, dst, where):
        return pltpu.make_async_remote_copy(
            src_ref=src, dst_ref=dst, send_sem=sems.at[0, kind, t], recv_sem=sems.at[1, kind, t], device_id=where,
            device_id_type=MESH,
        )

    def copies(s):
        t = unit(s)
        to_first, to_second = (on(first), z), (on(second), z)
        table = {
            R_CORE: (pack.at[:, 1 - core, t], got_core.at[t], (2 * me + 1 - core, z)),
            R_FIRST: (acc.at[t, first, upper], got_first.at[t, 0], to_first),
            R_FIRST2: (acc.at[t, across, upper], got_first.at[t, 1], to_first),
            R_SECOND: (acc.at[t, second, lower], got_second.at[t, 0], to_second),
            R_SECOND2: (acc.at[t, across, lower], got_second.at[t, 1], to_second),
            R_UP: (acc.at[t, second, upper], got_up.at[t], to_second),
            R_DOWN: (acc.at[t, first, lower], got_down.at[t], to_first),
            R_RIGHT: (acc.at[t, me], got_line.at[0, t], (d, jnp.minimum(z + 1, parts - 1))),
            R_LEFT: (acc.at[t, me], got_line.at[1, t], (d, jnp.maximum(z - 1, 0))),
        }
        return lambda kind: copy(kind, t, *table[kind])

    def load(s):
        t = unit(s)
        return pltpu.make_async_copy(pack.at[:, core, t], acc.at[t], load_sems.at[t])

    def add(target, at, count, source):
        tile = 32 if count % 32 == 0 else 16

        def some(i, carry):
            here = pl.ds(pl.multiple_of(at + i * tile, 16), tile)
            there = pl.ds(pl.multiple_of(i * tile, 16), tile)
            target[here, :] = (target[here, :].astype(F32) + source[there, :].astype(F32)).astype(BF16)
            return carry

        lax.fori_loop(0, count // tile, some, 0)

    def begin():
        for s in range(parts):
            load(s).start()
            copies(s)(R_CORE).start()

    def cores(s):
        t, c = unit(s), copies(s)
        load(s).wait()
        c(R_CORE).wait_recv()
        for p in (first, across, second, me):
            add(acc.at[t, p], 0, rows, got_core.at[t, p])
        for kind in (R_FIRST, R_FIRST2, R_SECOND, R_SECOND2):
            c(kind).start()

    def chips(s):
        t, c = unit(s), copies(s)
        for kind in (R_FIRST2, R_SECOND2, R_FIRST, R_SECOND):
            c(kind).wait_recv()
        add(acc.at[t, second], 0, cut, got_first.at[t, 1])
        c(R_UP).start()
        add(acc.at[t, first], cut, rows - cut, got_second.at[t, 1])
        c(R_DOWN).start()
        add(acc.at[t, me], 0, cut, got_first.at[t, 0])
        add(acc.at[t, me], cut, rows - cut, got_second.at[t, 0])

    def line(s):
        t, c = unit(s), copies(s)
        c(R_UP).wait_recv()
        add(acc.at[t, me], 0, cut, got_up.at[t])
        c(R_DOWN).wait_recv()
        add(acc.at[t, me], cut, rows - cut, got_down.at[t])

        @pl.when((z <= t) & (z > 0))
        def _():
            c(R_RIGHT).wait_recv()
            add(acc.at[t, me], 0, rows, got_line.at[0, t])

        @pl.when((z >= t) & (z < parts - 1))
        def _():
            c(R_LEFT).wait_recv()
            add(acc.at[t, me], 0, rows, got_line.at[1, t])

        @pl.when(z < t)
        def _():
            c(R_RIGHT).start()

        @pl.when(z > t)
        def _():
            c(R_LEFT).start()

    def finish():
        out[...] = acc[z, me].astype(F32)
        for s in range(parts):
            t, c = unit(s), copies(s)
            for kind in range(R_RIGHT):
                c(kind).wait_send()

            @pl.when(z < t)
            def _():
                c(R_RIGHT).wait_send()

            @pl.when(z > t)
            def _():
                c(R_LEFT).wait_send()

    order = [(cores, 0), (cores, 1), (cores, 2), (cores, 3), (chips, 0), (chips, 1), (line, 0), (chips, 2), (line, 1),
             (chips, 3), (line, 2), (line, 3)]
    return [begin] + [functools.partial(f, s) for f, s in order] + [finish]


def parts_of(v, count):
    out = []
    for _ in range(count):
        out.append(v.astype(BF16))
        v = v - out[-1].astype(F32)
    return out


def group_table(width, groups):
    low = lax.broadcasted_iota(jnp.int32, (width, groups), 1) * (width // groups)
    at = lax.broadcasted_iota(jnp.int32, (width, groups), 0)
    return ((at >= low) & (at < low + width // groups)).astype(BF16)


def add_rows(target, source, other, count, columns):
    def some(i, carry):
        here = pl.ds(pl.multiple_of(i * 32, 32), 32)
        target[here, :] = (source[here, :].astype(F32) + other[here, :].astype(F32)).astype(BF16)
        return carry

    lax.fori_loop(0, count // 32 if count % 32 == 0 else 0, some, 0)
    if count % 32:
        target[...] = (source[...].astype(F32) + other[...].astype(F32)).astype(BF16)


def end_kernel(
    bits, parts, replicas, per_tile, hops, x_ref, mean_ref, rho_ref, count_ref, gain_ref, own_ref, ema_ref, back0_ref,
    back1_ref, res_ref, segc_ref, segr_ref, next_ref, block_ref, *refs
):
    pieces, (ffn_ref, in_ref), outs, (own_sum_ref, ffn_sum_ref), scratch = (
        refs[:6], refs[6:8], refs[8:15], refs[15:17], refs[17:]
    )
    (gh, cen, rf, backed, head, head_got, total, acc, cube, buf, cbuf, summed, chain, chain_got,
     sems, head_sems, chain_sems) = scratch
    d, z = lax.axis_index("dp"), lax.axis_index("tensor")
    MESH = pl.DeviceIdType.MESH
    rows, width = x_ref.shape
    groups = mean_ref.shape[1]
    tiles = width // LANES
    greet(parts, sum(axis == "dp" for axis, _ in bits))

    far = z // (parts // 2)
    near_end = z + far * (parts - 1 - 2 * z)

    def unit(s):
        t = (parts - 1 - s) + near_end * ((3, 0, 2, 1)[s] - (parts - 1 - s))
        return t + far * (parts - 1 - 2 * t)

    def line_copy(s, side):
        t = unit(s)
        to = jnp.clip(z + (1 if side == 0 else -1), 0, parts - 1)
        return pltpu.make_async_remote_copy(
            src_ref=chain.at[t], dst_ref=chain_got.at[side, t], send_sem=chain_sems.at[0, side, t],
            recv_sem=chain_sems.at[1, side, t], device_id=(d, to), device_id_type=MESH,
        )

    def along(s):
        t = unit(s)
        span, columns = chain.shape[1:]
        from_left, from_right = (z <= t) & (z > 0), (z >= t) & (z < parts - 1)

        @pl.when(from_left)
        def _():
            line_copy(s, 0).wait_recv()
            add_rows(chain.at[t], ffn_ref.at[t], chain_got.at[0, t], span, columns)

        @pl.when(jnp.logical_not(from_left))
        def _():
            chain[t] = ffn_ref[t]

        @pl.when(from_right)
        def _():
            line_copy(s, 1).wait_recv()
            add_rows(chain.at[t], chain.at[t], chain_got.at[1, t], span, columns)

        @pl.when(z < t)
        def _():
            line_copy(s, 0).start()

        @pl.when(z > t)
        def _():
            line_copy(s, 1).start()

    def mine(axis, k):
        return ((d if axis == "dp" else z) // (1 << k)) % 2

    def partner(axis, k):
        step = (1 - 2 * mine(axis, k)) * (1 << k)
        return (d + step, z) if axis == "dp" else (d, z + step)

    def copy(n, which, src, dst):
        return pltpu.make_async_remote_copy(
            src_ref=src, dst_ref=dst, send_sem=sems.at[0, which, n], recv_sem=sems.at[1, which, n],
            device_id=partner(*bits[n]), device_id_type=MESH,
        )

    plan = []
    start, length, cstart, clength, at, cat = 0, acc.shape[0], 0, cube.shape[0], 0, 0
    for axis, k in bits:
        half = length // 2
        keep = pl.multiple_of(start + mine(axis, k) * half, 8)
        give = pl.multiple_of(start + (1 - mine(axis, k)) * half, 8)
        if axis == "dp":
            chalf = clength // 2
            ckeep = pl.multiple_of(cstart + mine(axis, k) * chalf, 16)
            cgive = pl.multiple_of(cstart + (1 - mine(axis, k)) * chalf, 16)
        else:
            chalf, ckeep, cgive = clength, cstart, cstart
        plan.append((start, length, half, keep, give, chalf, ckeep, cgive, at, cat))
        start, length, cstart, clength = keep, half, ckeep, chalf
        at, cat = at + half, cat + chalf

    def exchange(n):
        _, _, half, _, give, chalf, _, cgive, at, cat = plan[n]
        return (copy(n, 0, acc.at[pl.ds(give, half)], buf.at[pl.ds(at, half)]),
                copy(n, 1, cube.at[pl.ds(cgive, chalf)], cbuf.at[pl.ds(cat, chalf)]))

    def send(n):
        for c in exchange(n):
            c.start()

    def receive(n):
        for c in exchange(n):
            c.wait()
        _, _, half, keep, _, chalf, ckeep, _, at, cat = plan[n]
        acc[pl.ds(keep, half)] += buf[pl.ds(at, half)]
        both = cube[pl.ds(ckeep, chalf)].astype(F32) + cbuf[pl.ds(cat, chalf)].astype(F32)
        cube[pl.ds(ckeep, chalf)] = both.astype(BF16)

    along(0)

    table = group_table(width, groups)
    spread_of = lambda v: sum(dot32(p, table, NT) for p in parts_of(v, 3))
    sums_of = lambda v: sum(dot32(p, table) for p in parts_of(v, 2))
    gh[...] = own_ref[...] + ema_ref[...] + back0_ref[...].astype(F32)
    gh[rows - hops[1] :, :] += back1_ref[...].astype(F32)
    mean, rho, count = mean_ref[...], rho_ref[...], count_ref[...]
    rf[...] = spread_of(rho)
    cen[...] = x_ref[...].astype(F32) - spread_of(mean)
    gain_grad = jnp.sum(cen[...] * rf[...] * gh[...], axis=0, keepdims=True)
    last_rows = jnp.zeros((per_tile - sum(p.shape[0] for p in pieces) - 1, LANES), F32)
    for tile in range(tiles):
        lanes = slice(tile * LANES, (tile + 1) * LANES)
        row = tile * per_tile
        for p in pieces:
            acc[row : row + p.shape[0], :] = p[:, lanes]
            row += p.shape[0]
        acc[row : row + 1, :] = gain_grad[:, lanes]
        acc[row + 1 : (tile + 1) * per_tile, :] = last_rows
    depth = block_ref.shape[0] // replicas
    levels = replicas.bit_length() - 1
    for b in range(replicas):
        m = sum(((b >> k) & 1) << (levels - 1 - k) for k in range(levels))
        cube[m * depth : (m + 1) * depth, :] = block_ref[b * depth : (b + 1) * depth, :].astype(BF16)
    send(0)

    gh[...] = gh[...] * gain_ref[...]
    sum_a, sum_b = rho * sums_of(gh[...]), sums_of(gh[...] * cen[...])
    third = sum_b * rho * rho * rho
    lower = (segc_ref[...] == segr_ref[...]) & (
        lax.broadcasted_iota(jnp.int32, (rows, rows), 0) >= lax.broadcasted_iota(jnp.int32, (rows, rows), 1)
    )
    lower = lower.astype(F32).astype(BF16)
    back = lambda v: sum(dot32(lower, p, TN) for p in parts_of(v, 3))
    backed[0] = back((third * mean - sum_a) / count)
    backed[1] = back(-third / (2.0 * count))
    for half in range(2):
        head[half, :, :groups] = backed[half, 0:8, :]
    to_heads = [Along(parts, -hop, head, head_got.at[hop - 1], head_sems.at[0, hop - 1], head_sems.at[1, hop - 1])
                for hop in (1, 2)]
    for move in to_heads:
        move.start()
    receive(0)
    send(1)
    along(1)
    total[...] = jnp.zeros_like(total)
    for hop, move in enumerate(to_heads):
        def arrived(hop=hop):
            total[...] += next_ref[hop : hop + 1, :] * head_got[hop]
        move.wait_recv(arrived)
    tails = (segc_ref[...] == segc_ref[rows - 1 : rows, :]).astype(F32)
    first, second = (backed[half] + tails * total[half, 0:1, :groups] for half in range(2))
    in_ref[...] = res_ref[...] + gh[...] * rf[...] + spread_of(first) + 2.0 * x_ref[...].astype(F32) * spread_of(second)

    for n in range(1, len(bits)):
        receive(n)
        if n + 1 < len(bits):
            send(n + 1)
        if n + 1 < parts:
            along(n + 1)
    clast = pl.multiple_of(plan[-1][6], 16)
    own_sum_ref[...] = cube[pl.ds(clast, clength)].astype(F32)
    summed[pl.ds(start, length)] = acc[pl.ds(start, length)]
    for n in reversed(range(len(bits))):
        here = summed.at[pl.ds(start, length)]
        copy(n, 2, here, here).start()
        copy(n, 2, here, here).wait()
        start, length = plan[n][:2]
    for tile in range(tiles):
        lanes = slice(tile * LANES, (tile + 1) * LANES)
        row = tile * per_tile
        for out in outs:
            out[:, lanes] = summed[row : row + out.shape[0], :]
            row += out.shape[0]
    ffn_sum_ref[...] = chain[z].astype(F32)
    for s in range(parts):
        @pl.when(z < unit(s))
        def _():
            line_copy(s, 0).wait_send()

        @pl.when(z > unit(s))
        def _():
            line_copy(s, 1).wait_send()
    for move in to_heads:
        move.wait_send()


def end_call(replicas, parts, hops, per_row, pieces, ffn):
    bits = [("dp", k) for k in range(replicas.bit_length() - 1)]
    bits += [("tensor", k) for k in range(parts.bit_length() - 1)]
    x, block = per_row[0], per_row[-1]
    rows, width = x.shape
    tiles = width // LANES
    wanted = tiles * (sum(p.shape[0] for p in pieces) + 1)
    unit = max(replicas * parts * 8, tiles * 8)
    per_tile = -(-wanted // unit) * unit // tiles
    small = (tiles * per_tile, LANES)
    own = block.shape[0] // replicas
    got = sum(block.shape[0] >> (k + 1) for k in range(replicas.bit_length() - 1))
    got += own * (parts.bit_length() - 1)
    groups = per_row[1].shape[1]
    vm = pltpu.VMEM
    dma = lambda *n: pltpu.SemaphoreType.DMA(n)
    shape = jax.ShapeDtypeStruct
    ins = (*per_row, *pieces, ffn)
    outs = ([shape((rows, width), F32)] + [shape(p.shape, F32) for p in pieces]
            + [shape((1, width), F32), shape((own, block.shape[1]), F32), shape(ffn.shape[1:], F32)])
    return pl.pallas_call(
        functools.partial(end_kernel, bits, parts, replicas, per_tile, hops),
        in_specs=[pl.BlockSpec(memory_space=vm)] * len(ins),
        out_specs=[pl.BlockSpec(memory_space=vm)] * len(outs),
        out_shape=outs,
        scratch_shapes=[
            vm((rows, width), F32), vm((rows, width), F32), vm((rows, width), F32), vm((2, rows, groups), F32),
            vm((2, 8, LANES), F32), vm((2, 2, 8, LANES), F32), vm((2, 8, LANES), F32), vm(small, F32),
            vm(block.shape, BF16), vm(small, F32), vm((got, block.shape[1]), BF16), vm(small, F32),
            vm(ffn.shape, BF16), vm((2,) + ffn.shape, BF16), dma(2, 3, len(bits)), dma(2, 2), dma(2, 2, parts),
        ],
        compiler_params=pltpu.CompilerParams(collective_id=0, has_side_effects=True, vmem_limit_bytes=60 << 20),
        name="ending",
    )(*ins)


def on_device(
    block_in, segments, norm_gain, ema_rate, ema_angle, ema_input, ema_output, ema_skip, w_shared, query_gain,
    query_bias, key_gain, w_value, w_gate, w_out, ffn_gain, w_swish, w_up, w_down, out_grad,
):
    parts = lax.axis_size("tensor")
    replicas = lax.axis_size("dp")
    rank = lax.axis_index("tensor")
    rows, width = block_in.shape
    dims = ema_rate.shape[0]
    length = segments.shape[1]
    groups = TN_GROUPS
    span = width // groups
    latent_width = w_shared.shape[1]
    value_width = w_value.shape[1] * parts
    ffn_width = w_swish.shape[1] * parts
    depth = w_value.shape[0]
    halo = -(-REACH // LANES) * LANES
    hops = [min(rows, REACH - h * rows) for h in range(-(-REACH // rows))]

    chip_links = replicas == 8 and parts == 4

    piece = depth // parts
    shared_piece = lax.dynamic_slice_in_dim(w_shared, rank * piece, piece, 0)
    low = lambda w: w.astype(BF16)
    vw, fw = value_width // parts, ffn_width // parts
    pack_a = jnp.concatenate(
        [low(w_value), low(w_gate), low(w_out.T), low(shared_piece).reshape(-1, vw)], axis=0
    )
    pack_f1 = low(w_swish)
    pack_f2 = jnp.concatenate([low(w_up), low(w_down.T)], axis=0)
    gathered = lambda v: lax.all_gather(v, BOTH, axis=0).reshape(replicas, parts, *v.shape)
    pack_f2 = with_layout_constraint(pack_f2, Layout((0, 1)))

    def part(k, columns):
        return pl.BlockSpec((replicas, 1, depth, columns), lambda t: (0, t, k, 0))

    seg_all = segments[0]
    padded = jnp.concatenate([jnp.full((halo,), -1, jnp.int32), seg_all, jnp.full((halo,), -2, jnp.int32)])
    near = lax.dynamic_slice_in_dim(padded, rank * rows, halo + rows + halo, 0)
    seg_keys = near[: halo + rows]
    seg = near[halo : halo + rows]
    before = near[halo - 1]
    index = rank * rows + jnp.arange(rows, dtype=jnp.int32)
    start = jnp.sum((seg_all[None, :] < seg[:, None]).astype(jnp.int32), axis=1)
    count = (index - start + 1).astype(F32)[:, None] * span
    tri = jnp.arange(rows)
    link2 = (before == near[halo - rows - 1]).astype(F32)
    last = seg[-1]
    next1 = (near[halo + rows] == last).astype(F32)
    next2 = ((near[halo + 2 * rows - 1] == last) & (near[halo + 2 * rows] == last)).astype(F32) if halo > rows else 0.0
    cross = near[halo + 2 * rows - 1] == last
    edge = jnp.stack([before.astype(F32), jnp.float32(1.0), link2, cross.astype(F32)])[:, None] * jnp.ones((1, LANES), F32)
    seg_lanes = jnp.broadcast_to(seg.astype(F32)[:, None], (rows, LANES))

    size = jnp.exp(-ema_rate)
    unit = jnp.concatenate([size * jnp.cos(ema_angle), size * jnp.sin(ema_angle)])
    root = jnp.sqrt(1.0 - size * size)
    feed = ema_input * root
    reads = ema_output.reshape(2 * dims, width)
    skip = ema_skip[None]
    gcount = rows // (8 * STEP)
    nstate = gcount * dims * 2
    at_rows = gcount * STEP
    blocks = width // LANES
    col = lambda n: pl.BlockSpec((n, LANES), lambda i: (0, i % blocks))
    late = lambda n: pl.BlockSpec((n, LANES), lambda i: (0, jnp.maximum(i - blocks, 0)))
    late3 = lambda n, m: pl.BlockSpec((n, m, LANES), lambda i: (0, 0, jnp.maximum(i - blocks, 0)))
    anywhere = pl.BlockSpec(memory_space=pl.ANY)
    shape_of = jax.ShapeDtypeStruct
    vm = lambda *n: pltpu.VMEM((*n, 8, LANES), F32)
    flat_vm = lambda *n: pltpu.VMEM((*n, LANES), F32)
    dma = lambda *n: pltpu.SemaphoreType.DMA(n)
    table_vm, scale_vm = flat_vm(2, STEP * dims), flat_vm(8 * dims)
    state_vms = [vm(blocks, nstate), flat_vm(blocks, 2 * dims), flat_vm(2, blocks, 2 * dims), flat_vm(2 * dims),
                 dma(2, 2, blocks), dma(2, 3), dma(4)]
    mac = rows * width * dims * 4
    zeros = (jnp.zeros((rows, width), BF16), anywhere)
    near_rows = halo + rows
    full = lambda v: (v, whole(*v.shape))
    norm_shape = (shape_of((rows, groups), F32), whole(rows, groups))
    rows_late = (shape_of((rows, width), F32), late(rows))
    mask_vms = [vm(at_rows), vm(at_rows), vm(at_rows), vm(gcount), vm(3)]
    results = ema_call(
        functools.partial(ema_forward, rows, dims, parts, halo, hops, chip_links), width,
        [full(block_in), full(norm_gain[None]), full(seg_lanes), full(seg[:, None]), full(seg[None]), full(count),
         full(edge), (unit, col(2 * dims)), (feed, col(dims)), (reads, col(2 * dims)), (skip, col(1)), zeros]
        + [(pack_a, anywhere)] * chip_links,
        [rows_late, (shape_of((rows, width), BF16), late(rows)), (shape_of((nstate, 8, width), F32), late3(nstate, 8)),
         rows_late, norm_shape, norm_shape, (shape_of((near_rows, width), BF16), anywhere)]
        + [(shape_of((replicas, parts) + pack_a.shape, BF16), anywhere)] * chip_links,
        [flat_vm(blocks, rows), pltpu.VMEM((rows, width), BF16), vm(2), vm(2, 2), vm(2), dma(2, 2)] + mask_vms
        + [vm(2 * at_rows), table_vm, scale_vm] + state_vms + (gather_scratch(parts) if chip_links else []),
        "ema_forward", 2 * mac, 3,
    )
    ema_out, mixed, states, hidden, mean, rho, hidden_near = results[:7]
    all_f1 = gathered(lax.optimization_barrier((pack_f1, mixed))[0])
    all_a = results[-1] if chip_links else gathered(pack_a)
    shared_b = all_a[:, :, 3 * depth :].reshape(width, latent_width)

    latent = dot32(mixed, shared_b)
    queries = low(latent * query_gain + query_bias)
    keys_own = low(latent * key_gain)
    one = lambda v: v[None]
    matmul = rows * width * vw * 2 * parts
    col_v = lambda n: ((n, value_width), BF16, "col")
    ins = [(queries, "all"), (keys_own, "all"), (seg[:, None], "all"), (one(seg_keys), "all"), (hidden_near, "all"),
           (mixed, "all"), (block_in, "all"), (one(ffn_gain), "all"), (all_a, part(0, vw)), (all_a, part(1, vw)),
           (all_a, part(2, vw))]
    outs = [((rows, near_rows), F32, "all"), col_v(near_rows), col_v(near_rows), col_v(rows), col_v(rows), col_v(rows),
            ((rows, width), F32, "all"), ((rows, width), BF16, "all"), ((near_rows, latent_width), BF16, "all")]
    results = stage_call(
        functools.partial(attend_kernel, halo, parts, hops, chip_links), parts,
        ins + [(pack_f2, anywhere)] * chip_links,
        outs + [((replicas, parts) + pack_f2.shape, BF16, anywhere)] * chip_links,
        [pltpu.VMEM((rows, near_rows), BF16), pltpu.VMEM((near_rows, latent_width), BF16), dma(2, len(hops))]
        + (gather_scratch(parts) if chip_links else []),
        "attend", 6 * matmul, collective_id=1,
    )
    all_f2 = results[-1] if chip_links else gathered(pack_f2)
    probs, value_pre, values, gate_pre, attended, gated, residual, norm_in, keys_near = results[:9]

    row_vm = lambda n: pltpu.VMEM((n, width), F32)
    block_out, grad_residual, branch, grad_ffn_gain, ffn_grads = stage_call(
        ffn_kernel, parts,
        [(residual, "all"), (norm_in, "all"), (out_grad, "all"), (one(ffn_gain), "all"), (all_f1, part(0, fw)),
         (all_f2, part(0, fw)), (all_f2, part(1, fw))],
        [((rows, width), BF16, "all"), ((rows, width), F32, "all"), ((rows, width), BF16, "all"),
         ((1, width), F32, "all"),
         ((replicas, parts, 3, depth, fw), BF16,
          pl.BlockSpec((replicas, 1, 3, depth, fw), lambda t: (0, t, 0, 0, 0)))],
        [row_vm(rows), row_vm(rows)], "ffn", 11 * matmul,
    )

    def summed(g):
        g = g.reshape(replicas, parts, -1, g.shape[-1])
        return lax.psum_scatter(g, "dp", scatter_dimension=0, tiled=False)

    def summed_along(g, after):
        g = lax.optimization_barrier((g, after))[0]
        return lax.psum_scatter(g, "tensor", scatter_dimension=0, tiled=False).astype(F32)

    ffn_sum = summed(ffn_grads)

    grad_queries, grad_keys, hidden_back, hidden_own, grad_mixed, attn_grads = stage_call(
        functools.partial(attend_back_kernel, halo, parts, hops), parts,
        [(branch, "all"), (probs, "all"), (hidden_near, "all"), (mixed, "all"), (queries, "all"), (keys_near, "all"),
         (value_pre, "col"), (values, "col"), (gate_pre, "col"), (attended, "col"), (gated, "col"),
         (all_a, part(0, vw)), (all_a, part(1, vw)), (all_a, part(2, vw))],
        [((rows, latent_width), F32, "all"), ((rows, latent_width), F32, "all"),
         ((halo, width), BF16, "all"), ((rows, width), F32, "all"), ((rows, width), F32, "all"),
         ((replicas, parts, 3, depth, vw), BF16,
          pl.BlockSpec((replicas, 1, 3, depth, vw), lambda t: (0, t, 0, 0, 0)))],
        [pltpu.VMEM((rows, near_rows), F32), row_vm(near_rows), pltpu.VMEM((rows, near_rows), BF16),
         pltpu.VMEM((halo, latent_width), BF16), pltpu.VMEM((len(hops), rows, latent_width), BF16), dma(2, len(hops))],
        "attend_back", 12 * matmul, collective_id=4,
    )
    grad_query_gain = jnp.sum(latent * grad_queries, axis=0)
    grad_query_bias = jnp.sum(grad_queries, axis=0)
    grad_key_gain = jnp.sum(latent * grad_keys, axis=0)
    grad_latent = low(grad_queries * query_gain + grad_keys * key_gain)
    grad_shared = dot32(mixed, grad_latent, TN)
    grad_ema = (dot32(grad_latent, shared_b, NT) + grad_mixed) * silu_slope(ema_out)

    dim_late = late(dims)
    results = ema_call(
        functools.partial(ema_backward, rows, dims, parts, halo, hops, chip_links), width,
        [(hidden, late(rows)), (grad_ema, col(rows)), full(seg_lanes), full(edge), (unit, col(2 * dims)),
         (feed, dim_late), (reads, col(2 * dims)), (root, dim_late), (ema_input, dim_late),
         (states, late3(nstate, 8)), (skip, late(1)), (hidden_back, anywhere), zeros]
        + [(attn_grads.reshape(replicas // 2, 2, parts, 3 * depth, vw), anywhere)] * chip_links,
        [(shape_of((rows, width), F32), late(rows)), (shape_of((2 * dims, width), F32), late(2 * dims))]
        + [(shape_of((dims, width), F32), dim_late)] * 3 + [(shape_of((1, width), F32), late(1))]
        + [(shape_of((n, width), BF16), anywhere) for n in hops]
        + [(shape_of((3 * depth, vw), F32), whole(3 * depth, vw))] * chip_links,
        mask_vms + state_vms + [vm(2 * at_rows), vm(at_rows), vm(nstate), table_vm, scale_vm, flat_vm(4, STEP * dims),
                     flat_vm(9, dims), flat_vm(rows), flat_vm(rows)]
        + (reduce_scratch(parts, 3 * depth, vw) if chip_links else []),
        "ema_backward", 4 * mac, 2,
    )
    grad_hidden_ema, output_grad, input_grad, rate_grad, angle_grad, grad_skip = results[:6]
    attn_sum = results[-1] if chip_links else summed_along(summed(attn_grads), grad_skip)
    zero = jnp.zeros((1, width - 3 * latent_width), F32)
    latents = jnp.concatenate([grad_query_gain[None], grad_query_bias[None], grad_key_gain[None], zero], axis=1)
    nexts = jnp.stack([next1, jnp.asarray(next2, F32)])[:, None] * jnp.ones((1, LANES), F32)
    results = end_call(
        replicas, parts, hops,
        (block_in, mean, rho, count, norm_gain[None], hidden_own, grad_hidden_ema, results[6], results[7],
         grad_residual, seg[:, None], seg[None], nexts, grad_shared),
        (output_grad, input_grad, rate_grad, angle_grad, grad_skip,
         jnp.concatenate([grad_ffn_gain, latents], axis=0)),
        ffn_sum,
    )
    in_grad, output_grad, input_grad, rate_grad, angle_grad, skip_grad, two, gain_grad, shared_sum, ffn_sum = results
    latents = two[1].reshape(-1, latent_width)

    cut = lambda g, k: g[k * depth : (k + 1) * depth]
    return (
        block_out, in_grad, gain_grad[0], rate_grad, angle_grad, input_grad, output_grad.reshape(ema_output.shape),
        skip_grad[0], shared_sum, latents[0], latents[1], latents[2], cut(attn_sum, 0), cut(attn_sum, 1),
        cut(attn_sum, 2).T, two[0], cut(ffn_sum, 0), cut(ffn_sum, 1), cut(ffn_sum, 2).T,
    )


def solution(mesh):
    rows, dp, copy = P(BOTH, None), P("dp", None), P()
    wide, tall = P("dp", "tensor"), P("tensor", "dp")
    return jax.shard_map(
        on_device,
        mesh=mesh,
        in_specs=(
            rows, dp, copy, copy, copy, copy, copy, copy, dp, copy, copy, copy, wide, wide, tall, copy, wide, wide,
            tall, rows,
        ),
        out_specs=(
            rows, rows, copy, copy, copy, copy, copy, copy, dp, copy, copy, copy, wide, wide, tall, copy, wide, wide,
            tall,
        ),
        check_vma=False,
    )
```
